32 devices in a mesh: ha: 4 (over y, core), wa: 2 (over x), ta: 4 (over z).
Axes of the slice: x: 2, y: 2, z: 4, core: 2. Of those that a mesh axis runs over, the one named last changes fastest.
Arguments:
- video: bfloat16 [16, 96, 64, 256], P('ta', 'ha', 'wa'), may hold values from -210 to 210
- norm_gain: float32 [256], replicated, may hold values from 0.1 to 1.9
- norm_bias: float32 [256], replicated, may hold values from -3 to 3
- spatial_weight: bfloat16 [3, 3, 256, 256], replicated, may hold values from -0.125 to 0.125
- spatial_bias: float32 [256], replicated, may hold values from -3 to 3
- temporal_weight: bfloat16 [3, 256, 256], replicated, may hold values from -0.21875 to 0.21875
- temporal_bias: float32 [256], replicated, may hold values from -3 to 3
Outputs:
- encoded: bfloat16 [16, 96, 64, 256], P('ta', 'ha', 'wa')
The draws below stay inside these ranges and needn't reach their ends.
All inputs are finite; a program needn't handle non-finite values.
Results may differ from the reference program's by a relative error of at most 0.0054.
Values may be sent and summed in bfloat16 or wider, within the bound.
No kernel may reach another device: no remote copies, remote signals or barrier semaphores. Data moves between devices by JAX's collectives and lax.ppermute only.
A program may use at most 64 MiB of HBM per device.

```python
import math
import jax
import jax.numpy as jnp
from jax import lax

C = 256
G = 32
HB = 24
WB = 32
FRAMES = 16
H = 96
W = 64


def upsample(blocks, block_rows, block_cols):
    return jnp.repeat(jnp.repeat(blocks, block_rows, axis=1), block_cols, axis=2)


def draw_video(key, part):
    base_key, scale_key, offset_key, chan_key, frame_key = jax.random.split(key, 5)
    block_rows = max(HB // 2, 1)
    block_cols = max(WB // 2, 1)
    grid_rows = H // block_rows
    grid_cols = W // block_cols
    rows = jnp.arange(H, dtype=jnp.float32) / max(H - 1, 1)
    cols = jnp.arange(W, dtype=jnp.float32) / max(W - 1, 1)
    chan_scale = jnp.exp(jax.random.uniform(chan_key, (C,), jnp.float32, -0.7, 0.7))
    block_scale = jnp.exp(jax.random.uniform(scale_key, (FRAMES, grid_rows, grid_cols, 1), jnp.float32, 0.0, math.log(3.0)))
    block_scale = upsample(block_scale, block_rows, block_cols)
    trend = 10.0 ** (0.35 * (rows[:, None] + cols[None, :]))
    base = jnp.clip(jax.random.normal(base_key, (FRAMES, H, W, C), jnp.float32), -3.5, 3.5)
    block_offset = jax.random.uniform(offset_key, (FRAMES, grid_rows, grid_cols, 1), jnp.float32, -1.0, 1.0)
    frame_offset = jax.random.uniform(frame_key, (FRAMES, 1, 1, C), jnp.float32, -0.5, 0.5)
    base = base + upsample(block_offset, block_rows, block_cols) + frame_offset
    values = base * block_scale * trend[None, :, :, None] * chan_scale
    return values.astype(jnp.bfloat16)


def noise(own_key, extent, width, bound, held_as=jnp.bfloat16):
    return jnp.clip(width * jax.random.normal(own_key, extent, jnp.float32), -bound, bound).astype(held_as)


def setup_inputs(seed: int = 0) -> dict:
    keys = jax.random.split(jax.random.key(seed), 8)
    video = draw_video(jax.random.fold_in(keys[7], 71), 0)
    norm_gain = jnp.clip(1.0 + 0.18 * jax.random.normal(keys[1], (C,), jnp.float32), 0.1, 1.9)
    norm_bias = noise(keys[2], (C,), 0.5, 3.0, jnp.float32)
    spatial_weight = noise(keys[3], (3, 3, C, C), (9 * C) ** -0.5, 0.125)
    spatial_bias = noise(keys[4], (C,), 0.5, 3.0, jnp.float32)
    temporal_weight = noise(keys[5], (3, C, C), (3 * C) ** -0.5, 0.21875)
    temporal_bias = noise(keys[6], (C,), 0.5, 3.0, jnp.float32)
    return dict(video=video, norm_gain=norm_gain, norm_bias=norm_bias, spatial_weight=spatial_weight, spatial_bias=spatial_bias, temporal_weight=temporal_weight, temporal_bias=temporal_bias)


def normalize(frame, norm_gain, norm_bias):
    rows, cols, chans = frame.shape
    x = frame.astype(jnp.float32).reshape(rows, cols, G, chans // G)
    mean = lax.optimization_barrier(jnp.mean(x, axis=(0, 1, 3)))
    centered = x - mean[:, None]
    var = lax.optimization_barrier(jnp.mean(centered * centered, axis=(0, 1, 3)))
    scaled = centered * lax.rsqrt(var + 1e-06)[:, None]
    scaled = scaled.reshape(rows, cols, chans) * norm_gain + norm_bias
    return jax.nn.silu(scaled).astype(jnp.bfloat16)

def spatial_frame(frame, norm_gain, norm_bias, spatial_weight, spatial_bias):
    act = normalize(frame, norm_gain, norm_bias)
    rows, cols, chans = act.shape
    padded = jnp.pad(act, ((1, 1), (1, 1), (0, 0)))
    total = jnp.zeros((rows, cols, spatial_weight.shape[3]), jnp.float32)
    for dy in range(3):
        for dx in range(3):
            total = total + jnp.einsum('hwc,cd->hwd', padded[dy:dy + rows, dx:dx + cols].astype(jnp.float32), spatial_weight[dy, dx].astype(jnp.float32))
    return (total + spatial_bias).astype(jnp.bfloat16)

def reference(video, norm_gain, norm_bias, spatial_weight, spatial_bias, temporal_weight, temporal_bias):
    spatial = lax.map(lambda frame: spatial_frame(frame, norm_gain, norm_bias, spatial_weight, spatial_bias), video)
    extended = jnp.concatenate([spatial[:1], spatial[:1], spatial], axis=0)

    def one_frame(index):
        total = jnp.zeros(spatial.shape[1:], jnp.float32)
        for tap in range(3):
            frame = lax.dynamic_index_in_dim(extended, index + 2 - tap, 0, keepdims=False)
            total = total + jnp.einsum('hwc,cd->hwd', frame.astype(jnp.float32), temporal_weight[tap].astype(jnp.float32))
        return (total + temporal_bias).astype(jnp.bfloat16)
    return lax.map(one_frame, jnp.arange(spatial.shape[0], dtype=jnp.int32))
```

```python
import functools

import jax
import jax.numpy as jnp
from jax import lax
from jax.experimental import pallas as pl
from jax.experimental.pallas import tpu as pltpu
from jax.sharding import PartitionSpec as P

G = 32
EPS = 1e-06
PREV = 2
F32 = jnp.float32
BF16 = jnp.bfloat16
VMEM = pl.BlockSpec(memory_space=pltpu.VMEM)
ANY = pl.BlockSpec(memory_space=pl.ANY)


def call(kernel, outs, out_specs=None, scratch=(), flops=0, name=None, **kw):
    nbytes = sum(o.size * o.dtype.itemsize for o in outs)
    return pl.pallas_call(
        kernel,
        out_shape=outs,
        out_specs=out_specs or [VMEM] * len(outs),
        scratch_shapes=list(scratch),
        compiler_params=pltpu.CompilerParams(vmem_limit_bytes=40 << 20),
        cost_estimate=pl.CostEstimate(flops=flops, bytes_accessed=nbytes, transcendentals=0),
        name=name,
        **kw,
    )


def pad_to(n, k):
    return (n + k - 1) // k * k


def split3(x):
    hi = x.astype(BF16)
    rest = x - hi.astype(F32)
    mid = rest.astype(BF16)
    low = (rest - mid.astype(F32)).astype(BF16)
    return hi, mid, low


def as_terms(x, rows):
    parts = jnp.concatenate([t.astype(F32) for t in split3(x)], axis=0)
    fill = rows - parts.shape[0]
    if fill:
        parts = jnp.concatenate([parts, jnp.zeros((fill, x.shape[1]), F32)], axis=0)
    return parts.astype(BF16)


def from_terms(t, rows):
    t = t.astype(F32)
    return t[:rows] + t[rows : 2 * rows] + t[2 * rows : 3 * rows]


class Sizes:
    def __init__(self, video, ha, wa):
        self.frames, self.rows, self.cols, self.chans = video.shape
        self.ha, self.wa = ha, wa
        self.ncol = 1 if wa == 2 else 2
        self.colrow = pad_to(self.rows + 2, 16)
        self.all = self.frames + PREV
        self.strip = 2 * self.cols + self.ncol * self.colrow
        self.local_stats = pad_to(3 * 2 * PREV, 16)
        self.stats = pad_to(3 * 2 * self.all, 16)


def local_kernel(s, video, stats, strips, zstrip, bulk):
    wa = lax.axis_index("wa")
    first = s.frames - PREV
    tail_m, tail_q = [], []
    for f in range(s.frames):
        total = jnp.zeros((s.cols, s.chans), F32)
        for r in range(s.rows):
            total = total + video[f, r].astype(F32)
        mean = jnp.sum(total, axis=0, keepdims=True) * (1.0 / (s.rows * s.cols))
        spread = jnp.zeros((s.cols, s.chans), F32)
        left, right = [], []
        for r in range(s.rows):
            x = video[f, r].astype(F32)
            left.append(x[:1])
            right.append(x[s.cols - 1 :])
            x = x - mean
            spread = spread + x * x
        square = jnp.sum(spread, axis=0, keepdims=True)
        stats[f : f + 1] = mean
        stats[s.frames + f : s.frames + f + 1] = square
        fill = [jnp.zeros((s.colrow - s.rows, s.chans), F32)]
        left = jnp.concatenate(left + fill, axis=0)
        right = jnp.concatenate(right + fill, axis=0)
        if s.ncol == 1:
            edges = [jnp.where(wa == 0, right, left).astype(BF16)]
        else:
            edges = [left.astype(BF16), right.astype(BF16)]
        for ref, at, use in ((strips, f, True), (zstrip, f - first, f >= first)):
            if not use:
                continue
            o = at * s.strip
            ref[o : o + s.cols] = video[f, 0]
            ref[o + s.cols : o + 2 * s.cols] = video[f, s.rows - 1]
            for k, e in enumerate(edges):
                o2 = o + 2 * s.cols + k * s.colrow
                ref[o2 : o2 + s.colrow] = e
        if f >= first:
            bulk[f - first] = video[f, 1 : s.rows - 1]
            tail_m.append(mean)
            tail_q.append(square)
    o = PREV * s.strip
    zstrip[o : o + s.local_stats] = as_terms(jnp.concatenate(tail_m + tail_q, axis=0), s.local_stats)


def strip_of(s, strips, zrecv, f):
    if f < s.frames:
        return strips, f * s.strip
    return zrecv, (f - s.frames) * s.strip


def rows_kernel(s, stats, strips, zrecv, pay1, pay2, payt):
    ha = lax.axis_index("ha")
    even = lax.rem(ha, 2) == 0
    for f in range(s.all):
        ref, o = strip_of(s, strips, zrecv, f)
        top = ref[o : o + s.cols].astype(F32)
        bottom = ref[o + s.cols : o + 2 * s.cols].astype(F32)
        pay1[f * s.cols : (f + 1) * s.cols] = jnp.where(even, bottom, top).astype(BF16)
        pay2[f * s.cols : (f + 1) * s.cols] = jnp.where(even, top, bottom).astype(BF16)
    o = PREV * s.strip
    prev = from_terms(zrecv[o : o + s.local_stats], 2 * PREV)
    own = stats[...]
    both = jnp.concatenate([own[: s.frames], prev[:PREV], own[s.frames :], prev[PREV:]], axis=0)
    terms = as_terms(both, s.stats)
    o = s.all * s.cols
    pay1[o : o + s.stats] = terms
    pay2[o : o + s.stats] = terms
    payt[...] = terms


def merge(n, parts):
    half = parts[0].shape[0] // 2
    mean = sum(p[:half] for p in parts) * (1.0 / len(parts))
    square = sum(p[half:] + n * (p[:half] - mean) * (p[:half] - mean) for p in parts)
    return jnp.concatenate([mean, square], axis=0)


def cols_kernel(s, strips, zrecv, terms, got1, got2, gott, halo, payc, part):
    ha, wa = lax.axis_index("ha"), lax.axis_index("wa")
    even = lax.rem(ha, 2) == 0
    at = lax.broadcasted_iota(jnp.int32, (s.colrow, s.chans), 0)
    for f in range(s.all):
        one = got1[f * s.cols : (f + 1) * s.cols].astype(F32)
        two = got2[f * s.cols : (f + 1) * s.cols].astype(F32)
        top = jnp.where(even, two, one)
        bottom = jnp.where(even, one, two)
        halo[f, 0] = top.astype(BF16)
        halo[f, 1] = bottom.astype(BF16)
        ref, o = strip_of(s, strips, zrecv, f)
        for k in range(s.ncol):
            o2 = o + 2 * s.cols + k * s.colrow
            edge = ref[o2 : o2 + s.colrow].astype(F32)
            right = wa == 0 if s.ncol == 1 else k == 1
            tcell = jnp.where(right, top[s.cols - 1 :], top[:1])
            bcell = jnp.where(right, bottom[s.cols - 1 :], bottom[:1])
            edge = jnp.where(at == s.rows, tcell, edge)
            edge = jnp.where(at == s.rows + 1, bcell, edge)
            o3 = (f * s.ncol + k) * s.colrow
            payc[o3 : o3 + s.colrow] = edge.astype(BF16)
    if gott is not None:
        o = s.all * s.cols
        rows = 2 * s.all
        parts = [from_terms(terms[...], rows)]
        parts += [from_terms(g[o : o + s.stats], rows) for g in (got1, got2)]
        parts += [from_terms(gott[...], rows)]
        merged = merge(float(s.rows * s.cols), parts)
        part[...] = merged
        o = s.all * s.ncol * s.colrow
        payc[o : o + s.stats] = as_terms(merged, s.stats)


def activation(x, mean, scale, shift):
    h = (x - mean) * scale + shift
    return h + h * jnp.tanh(h)


def fill_taps(s, taps, raw_row, edges, mean, scale, shift):
    ha, wa = lax.axis_index("ha"), lax.axis_index("wa")
    top_in = jnp.where(ha > 0, 1.0, 0.0).astype(F32)
    bottom_in = jnp.where(ha < s.ha - 1, 1.0, 0.0).astype(F32)
    left_in = jnp.where(wa > 0, 1.0, 0.0).astype(F32)
    right_in = jnp.where(wa < s.wa - 1, 1.0, 0.0).astype(F32)
    acts = [activation(e.astype(F32), mean, scale, shift) for e in edges]
    left, right = acts[0] * left_in, acts[-1] * right_in
    at = lax.broadcasted_iota(jnp.int32, (s.cols, s.chans), 0)
    for i in range(s.rows + 2):
        act = activation(raw_row(i).astype(F32), mean, scale, shift)
        j = s.rows if i == 0 else s.rows + 1 if i == s.rows + 1 else i - 1
        lcell, rcell = left[j : j + 1], right[j : j + 1]
        west = jnp.where(at == 0, lcell, pltpu.roll(act, 1, 0))
        east = jnp.where(at == s.cols - 1, rcell, pltpu.roll(act, s.cols - 1, 0))
        if i in (0, s.rows + 1):
            inside = top_in if i == 0 else bottom_in
            west, act, east = west * inside, act * inside, east * inside
        taps[0, i] = west.astype(BF16)
        taps[1, i] = act.astype(BF16)
        taps[2, i] = east.astype(BF16)


def spatial_dot(s, taps, weight, bias):
    lhs = jnp.concatenate(
        [
            taps[dx, dy : dy + s.rows].reshape(s.rows * s.cols, s.chans)
            for dy in range(3)
            for dx in range(3)
        ],
        axis=1,
    )
    return (jnp.dot(lhs, weight[...], preferred_element_type=F32) + bias[...]).astype(BF16)


def temporal_dot(s, frames, weight, bias):
    lhs = jnp.concatenate(frames, axis=1)
    out = jnp.dot(lhs, weight[...], preferred_element_type=F32) + bias[...]
    return out.astype(BF16).reshape(s.rows, s.cols, s.chans)


def edges_of(s, got, f):
    edges = []
    for k in range(s.ncol):
        o = (f * s.ncol + k) * s.colrow
        edges.append(got[k][pl.ds(f * s.colrow, s.colrow)] if s.ncol > 1 else got[0][pl.ds(o, s.colrow)])
    return edges


def own_kernel(s, nstat, video, halo, *refs):
    gotc = refs[: s.ncol]
    (part, gain, nbias, sw, sb, tw, tb, enc, lead, aff, taps, spatial, out, sem) = refs[s.ncol :]
    rows = 2 * s.all
    count = float(s.rows * s.cols * s.ha * s.wa)
    stat = part[...]
    if nstat == 2:
        o = s.all * s.colrow
        stat = merge(count / 2, [stat, from_terms(gotc[0][o : o + s.stats], rows)])
    width = s.chans // G
    a = lax.broadcasted_iota(jnp.int32, (s.chans, s.chans), 0) // width
    b = lax.broadcasted_iota(jnp.int32, (s.chans, s.chans), 1) // width
    group = jnp.where(a == b, 1.0, 0.0).astype(F32)
    tot = functools.partial(jnp.dot, precision=lax.Precision.HIGHEST, preferred_element_type=F32)
    m, q = stat[: s.all], stat[s.all :]
    mean = tot(m, group) * (1.0 / width)
    var = tot(q + count * (m - mean) * (m - mean), group) * (1.0 / (count * width))
    scale = lax.rsqrt(var + EPS) * gain[...] * 0.5
    shift = nbias[...] * 0.5
    aff[: s.all] = mean
    aff[s.all :] = scale
    ta = lax.axis_index("ta")

    def put(f):
        return pltpu.make_async_copy(out.at[f], enc.at[f], sem.at[f])

    def frame(f, _):
        def raw_row(i):
            if i == 0:
                return halo[f, 0]
            if i == s.rows + 1:
                return halo[f, 1]
            return video[f, i - 1]

        fill_taps(s, taps, raw_row, edges_of(s, gotc, f), aff[pl.ds(f, 1)], aff[pl.ds(s.all + f, 1)], shift)
        spatial[f] = spatial_dot(s, taps, sw, sb)
        return _

    lax.fori_loop(0, s.frames, frame, 0)
    for f in range(PREV, s.frames):
        out[f] = temporal_dot(s, [spatial[f - k] for k in range(3)], tw, tb)
        put(f).start()

    @pl.when(ta == 0)
    def _():
        for f in range(PREV):
            out[f] = temporal_dot(s, [spatial[max(f - k, 0)] for k in range(3)], tw, tb)
            put(f).start()
            put(f).wait()

    for f in range(PREV):
        lead[f] = spatial[f]
    for f in range(PREV, s.frames):
        put(f).wait()


def prev_kernel(s, bulk, zrecv, halo, *refs):
    gotc = refs[: s.ncol]
    (aff, nbias, sw, sb, tw, tb, lead, enc_in, enc, taps, spatial, out, sem) = refs[s.ncol :]
    ta = lax.axis_index("ta")
    shift = nbias[...] * 0.5

    @pl.when(ta > 0)
    def _():
        def frame(p, _):
            f = s.frames + p
            o = p * s.strip

            def raw_row(i):
                if i == 0:
                    return halo[f, 0]
                if i == s.rows + 1:
                    return halo[f, 1]
                if i == 1:
                    return zrecv[pl.ds(o, s.cols)]
                if i == s.rows:
                    return zrecv[pl.ds(o + s.cols, s.cols)]
                return bulk[p, i - 2]

            fill_taps(s, taps, raw_row, edges_of(s, gotc, f), aff[pl.ds(f, 1)], aff[pl.ds(s.all + f, 1)], shift)
            spatial[p] = spatial_dot(s, taps, sw, sb)
            return _

        lax.fori_loop(0, PREV, frame, 0)
        seq = [spatial[0], spatial[1], lead[0], lead[1]]
        copies = []
        for f in range(PREV):
            out[f] = temporal_dot(s, [seq[PREV + f - k] for k in range(3)], tw, tb)
            copies.append(pltpu.make_async_copy(out.at[f], enc.at[f], sem.at[f]))
            copies[-1].start()
        for c in copies:
            c.wait()


def mates(n, phase):
    pairs = [(i, i ^ 1) for i in range(n)]
    if phase == 0:
        return pairs
    return [(i, (((i + 1) % n) ^ 1) - 1 if ((i + 1) % n) ^ 1 else n - 1) for i in range(n)]


def local(video, norm_gain, norm_bias, spatial_weight, spatial_bias, temporal_weight, temporal_bias):
    nta, nha, nwa = (lax.axis_size(a) for a in ("ta", "ha", "wa"))
    s = Sizes(video, nha, nwa)
    c = s.chans
    sd = jax.ShapeDtypeStruct
    ring = [(i, (i + 1) % nta) for i in range(nta)]
    sw = spatial_weight.reshape(9 * c, c)
    tw = temporal_weight.reshape(3 * c, c)
    gain, nbias, sb, tb = (v.reshape(1, c) for v in (norm_gain, norm_bias, spatial_bias, temporal_bias))

    stats, strips, zstrip, bulk = call(
        functools.partial(local_kernel, s),
        [
            sd((2 * s.frames, c), F32),
            sd((s.frames * s.strip, c), BF16),
            sd((PREV * s.strip + s.local_stats, c), BF16),
            sd((PREV, s.rows - 2, s.cols, c), BF16),
        ],
        name="local",
        in_specs=[VMEM],
    )(video)
    zrecv = lax.ppermute(zstrip, "ta", ring)
    bulk = lax.ppermute(bulk, "ta", ring)

    fused = nha == 4 and nwa == 2
    rowpay = sd((s.all * s.cols + s.stats, c), BF16)
    pay1, pay2, terms = call(
        functools.partial(rows_kernel, s),
        [rowpay, rowpay, sd((s.stats, c), BF16)],
        name="rows",
        in_specs=[VMEM] * 3,
    )(stats, strips, zrecv)
    got1 = lax.ppermute(pay1, "ha", mates(nha, 0))
    got2 = lax.ppermute(pay2, "ha", mates(nha, 1))
    colrows = s.all * s.ncol * s.colrow + (s.stats if fused else 0)
    outs = [sd((s.all, 2, s.cols, c), BF16), sd((colrows, c), BF16)]
    if fused:
        gott = lax.ppermute(terms, "ha", [(i, i ^ 2) for i in range(nha)])
        halo, payc, part = call(
            functools.partial(cols_kernel, s),
            outs + [sd((2 * s.all, c), F32)],
            name="cols",
            in_specs=[VMEM] * 6,
        )(strips, zrecv, terms, got1, got2, gott)
        gotc = [lax.ppermute(payc, "wa", [(0, 1), (1, 0)])]
    else:
        def kernel(strips, zrecv, got1, got2, halo, payc):
            cols_kernel(s, strips, zrecv, None, got1, got2, None, halo, payc, None)

        halo, payc = call(kernel, outs, name="cols", in_specs=[VMEM] * 4)(strips, zrecv, got1, got2)
        rows = 2 * s.all
        both = from_terms(terms, rows)
        every = lax.all_gather(both, ("ha", "wa"))
        part = merge(float(s.rows * s.cols), [every[i] for i in range(nha * nwa)])
        if s.ncol == 1:
            gotc = [lax.ppermute(payc, "wa", [(0, 1), (1, 0)])]
        else:
            sides = payc.reshape(s.all, 2, s.colrow, c)
            up = [(i, (i + 1) % nwa) for i in range(nwa)]
            down = [((i + 1) % nwa, i) for i in range(nwa)]
            gotc = [
                lax.ppermute(sides[:, 1].reshape(-1, c), "wa", up),
                lax.ppermute(sides[:, 0].reshape(-1, c), "wa", down),
            ]
    flops = 2 * s.rows * s.cols * c * c
    frame = (s.rows * s.cols, c)
    taps = pltpu.VMEM((3, s.rows + 2, s.cols, c), BF16)
    enc, lead, aff = call(
        functools.partial(own_kernel, s, 2 if fused else 1),
        [sd(video.shape, BF16), sd((PREV,) + frame, BF16), sd((2 * s.all, c), F32)],
        out_specs=[ANY, VMEM, VMEM],
        scratch=[
            taps,
            pltpu.VMEM((s.frames,) + frame, BF16),
            pltpu.VMEM((s.frames, s.rows, s.cols, c), BF16),
            pltpu.SemaphoreType.DMA((s.frames,)),
        ],
        flops=flops * (9 * s.frames + 3 * (s.frames - PREV)),
        name="own",
        in_specs=[VMEM] * (9 + s.ncol),
    )(video, halo, *gotc, part, gain, nbias, sw, sb, tw, tb)
    (enc,) = call(
        functools.partial(prev_kernel, s),
        [sd(video.shape, BF16)],
        out_specs=[ANY],
        scratch=[
            taps,
            pltpu.VMEM((PREV,) + frame, BF16),
            pltpu.VMEM((PREV, s.rows, s.cols, c), BF16),
            pltpu.SemaphoreType.DMA((PREV,)),
        ],
        flops=flops * 12 * PREV,
        name="prev",
        in_specs=[VMEM] * (10 + s.ncol) + [ANY],
        input_output_aliases={10 + s.ncol: 0},
    )(bulk, zrecv, halo, *gotc, aff, nbias, sw, sb, tw, tb, lead, enc)
    return enc


def solution(mesh):
    placed = (P("ta", "ha", "wa", None), P(), P(), P(), P(), P(), P())
    return jax.shard_map(
        local, mesh=mesh, in_specs=placed, out_specs=P("ta", "ha", "wa", None), check_vma=False
    )
```

```python
import functools

import jax
import jax.numpy as jnp
from jax import lax
from jax.experimental import pallas as pl
from jax.experimental.pallas import tpu as pltpu
from jax.sharding import PartitionSpec as P

G = 32
EPS = 1e-06
QUARTERS = 4
DOTS = 6
PREV = 2
F32 = jnp.float32
BF16 = jnp.bfloat16
VMEM = pl.BlockSpec(memory_space=pltpu.VMEM)
ANY = pl.BlockSpec(memory_space=pl.ANY)


def call(kernel, outs, out_specs=None, scratch=(), name=None, **kw):
    return pl.pallas_call(
        kernel,
        out_shape=outs,
        out_specs=out_specs or [VMEM] * len(outs),
        scratch_shapes=list(scratch),
        compiler_params=pltpu.CompilerParams(vmem_limit_bytes=24 << 20),
        cost_estimate=pl.CostEstimate(flops=1024, bytes_accessed=1024, transcendentals=0),
        name=name,
        **kw,
    )


def pad_to(n, k):
    return (n + k - 1) // k * k


def split3(x):
    hi = x.astype(BF16)
    rest = x - hi.astype(F32)
    mid = rest.astype(BF16)
    low = (rest - mid.astype(F32)).astype(BF16)
    return hi, mid, low


def as_terms(x, rows):
    parts = jnp.concatenate([t.astype(F32) for t in split3(x)], axis=0)
    fill = rows - parts.shape[0]
    if fill:
        parts = jnp.concatenate([parts, jnp.zeros((fill, x.shape[1]), F32)], axis=0)
    return parts.astype(BF16)


def from_terms(t, rows):
    t = t.astype(F32)
    return t[:rows] + t[rows : 2 * rows] + t[2 * rows : 3 * rows]


class Sizes:
    def __init__(self, video, ha, wa):
        self.frames, self.rows, self.cols, self.chans = video.shape
        self.ha, self.wa = ha, wa
        self.ncol = 1 if wa == 2 else 2
        self.fused = ha == 4 and wa == 2
        self.colrow = pad_to(self.rows + 2, 16)
        self.strip = 2 * self.cols + self.ncol * self.colrow
        self.stats = pad_to(3 * 2 * self.frames, 16)
        self.last = pad_to(3 * 2 * PREV, 16)
        self.corner = pad_to(self.frames, 16)


def head_kernel(s, video, bulk):
    for p in range(PREV):
        bulk[p] = video[s.frames - PREV + p]


def local_kernel(s, video, bulk, pay, stats, *cols):
    ha, wa = lax.axis_index("ha"), lax.axis_index("wa")
    even = lax.rem(ha, 2) == 0
    means, squares = [], []
    for f in range(s.frames):
        total = jnp.zeros((s.cols, s.chans), F32)
        for r in range(s.rows):
            total = total + video[f, r].astype(F32)
        mean = jnp.sum(total, axis=0, keepdims=True) * (1.0 / (s.rows * s.cols))
        spread = jnp.zeros((s.cols, s.chans), F32)
        left, right = [], []
        for r in range(s.rows):
            x = video[f, r].astype(F32)
            left.append(x[:1])
            right.append(x[s.cols - 1 :])
            x = x - mean
            spread = spread + x * x
        means.append(mean)
        squares.append(jnp.sum(spread, axis=0, keepdims=True))
        fill = [jnp.zeros((s.colrow - s.rows, s.chans), F32)]
        left = jnp.concatenate(left + fill, axis=0)
        right = jnp.concatenate(right + fill, axis=0)
        if s.ncol == 1:
            edges = [jnp.where(wa == 0, right, left)]
        else:
            edges = [right, left]
        for ref, e in zip(cols, edges):
            ref[f * s.colrow : (f + 1) * s.colrow] = e.astype(BF16)
        top = video[f, 0].astype(F32)
        bottom = video[f, s.rows - 1].astype(F32)
        pay[f * s.cols : (f + 1) * s.cols] = jnp.where(even, bottom, top).astype(BF16)
    stat = jnp.concatenate(means + squares, axis=0)
    stats[...] = stat
    o = s.frames * s.cols
    pay[o : o + s.stats] = as_terms(stat, s.stats)


def merge(n, parts):
    half = parts[0].shape[0] // 2
    mean = sum(p[:half] for p in parts) * (1.0 / len(parts))
    square = sum(p[half:] + n * (p[:half] - mean) * (p[:half] - mean) for p in parts)
    return jnp.concatenate([mean, square], axis=0)


def pair_kernel(s, video, stats, got, *refs):
    cols, refs = refs[: s.ncol], refs[s.ncol :]
    payy, part = refs[:2]
    payx, payd = refs[2 : 2 + s.ncol], refs[2 + s.ncol :]
    ha, wa = lax.axis_index("ha"), lax.axis_index("wa")
    even = lax.rem(ha, 2) == 0
    o = s.frames * s.cols
    stat = merge(float(s.rows * s.cols), [stats[...], from_terms(got[o : o + s.stats], 2 * s.frames)])
    part[...] = stat
    terms = as_terms(stat, s.stats)
    at = lax.broadcasted_iota(jnp.int32, (s.colrow, s.chans), 0)
    cells = [[] for _ in range(s.ncol)]
    for f in range(s.frames):
        top = video[f, 0].astype(F32)
        bottom = video[f, s.rows - 1].astype(F32)
        outer = jnp.where(even, top, bottom)
        payy[f * s.cols : (f + 1) * s.cols] = outer.astype(BF16)
        inner = got[f * s.cols : (f + 1) * s.cols].astype(F32)
        for k in range(s.ncol):
            right = wa == 0 if s.ncol == 1 else k == 0
            cell = jnp.where(right, inner[s.cols - 1 :], inner[:1])
            cells[k].append(jnp.where(right, outer[s.cols - 1 :], outer[:1]))
            edge = cols[k][f * s.colrow : (f + 1) * s.colrow].astype(F32)
            edge = jnp.where(at >= s.rows, cell, edge)
            payx[k][f * s.colrow : (f + 1) * s.colrow] = edge.astype(BF16)
    for k in range(s.ncol):
        fill = s.corner - s.frames
        rows = cells[k] + ([jnp.zeros((fill, s.chans), F32)] if fill else [])
        payd[k][: s.corner] = jnp.concatenate(rows, axis=0).astype(BF16)
    payy[o : o + s.stats] = terms
    if s.fused:
        o = s.frames * s.colrow
        payx[0][o : o + s.stats] = terms
        payd[0][s.corner : s.corner + s.stats] = terms


def edge_kernel(s, part, gain, got, goty, *refs):
    gotx, gotd = refs[: s.ncol], refs[s.ncol : 2 * s.ncol]
    aff, hand, halo, *cols = refs[2 * s.ncol :]
    even = lax.rem(lax.axis_index("ha"), 2) == 0
    rows = 2 * s.frames
    count = float(s.rows * s.cols * s.ha * s.wa)
    stat = part[...]
    if s.fused:
        offsets = ((goty, s.frames * s.cols), (gotx[0], s.frames * s.colrow), (gotd[0], s.corner))
        stat = merge(count / 4, [stat] + [from_terms(ref[o : o + s.stats], rows) for ref, o in offsets])
    width = s.chans // G
    a = lax.broadcasted_iota(jnp.int32, (s.chans, s.chans), 0) // width
    b = lax.broadcasted_iota(jnp.int32, (s.chans, s.chans), 1) // width
    group = jnp.where(a == b, 1.0, 0.0).astype(BF16)

    def tot(x):
        terms = jnp.concatenate(split3(x), axis=0)
        y = jnp.dot(terms, group, preferred_element_type=F32)
        n = s.frames
        return y[:n] + y[n : 2 * n] + y[2 * n :]

    m, q = stat[: s.frames], stat[s.frames :]
    mean = tot(m) * (1.0 / width)
    var = tot(q + count * (m - mean) * (m - mean)) * (1.0 / (count * width))
    scale = lax.rsqrt(var + EPS) * gain[...] * 0.5
    aff[: s.frames] = mean
    aff[s.frames :] = scale
    first = s.frames - PREV
    at = lax.broadcasted_iota(jnp.int32, (s.colrow, s.chans), 0)
    for f in range(s.frames):
        p = (f - first) * s.strip
        one = got[f * s.cols : (f + 1) * s.cols].astype(F32)
        two = goty[f * s.cols : (f + 1) * s.cols].astype(F32)
        top = jnp.where(even, two, one).astype(BF16)
        bottom = jnp.where(even, one, two).astype(BF16)
        halo[f, 0] = top
        halo[f, 1] = bottom
        if f >= first:
            hand[p : p + s.cols] = top
            hand[p + s.cols : p + 2 * s.cols] = bottom
        for k in range(s.ncol):
            cell = gotd[k][: s.corner].astype(F32)[f : f + 1]
            edge = gotx[k][f * s.colrow : (f + 1) * s.colrow].astype(F32)
            outer = jnp.where(even, s.rows, s.rows + 1)
            edge = jnp.where(at == outer, cell, edge).astype(BF16)
            cols[k][f * s.colrow : (f + 1) * s.colrow] = edge
            if f >= first:
                o = p + 2 * s.cols + k * s.colrow
                hand[o : o + s.colrow] = edge
    o = PREV * s.strip
    hand[o : o + s.last] = as_terms(jnp.concatenate([mean[first:], scale[first:]], axis=0), s.last)


def activation(x, mean, scale, shift):
    h = (x - mean) * scale + shift
    return h + h * jnp.tanh(h)


def fill_taps(s, taps, raw_row, edges, mean, scale, shift):
    ha, wa = lax.axis_index("ha"), lax.axis_index("wa")
    top_in = jnp.where(ha > 0, 1.0, 0.0).astype(F32)
    bottom_in = jnp.where(ha < s.ha - 1, 1.0, 0.0).astype(F32)
    left_in = jnp.where(wa > 0, 1.0, 0.0).astype(F32)
    right_in = jnp.where(wa < s.wa - 1, 1.0, 0.0).astype(F32)
    acts = [activation(e.astype(F32), mean, scale, shift) for e in edges]
    left, right = acts[0] * left_in, acts[-1] * right_in
    at = lax.broadcasted_iota(jnp.int32, (s.cols, s.chans), 0)
    for i in range(s.rows + 2):
        act = activation(raw_row(i).astype(F32), mean, scale, shift)
        j = s.rows if i == 0 else s.rows + 1 if i == s.rows + 1 else i - 1
        lcell, rcell = left[j : j + 1], right[j : j + 1]
        west = jnp.where(at == 0, lcell, pltpu.roll(act, 1, 0))
        east = jnp.where(at == s.cols - 1, rcell, pltpu.roll(act, s.cols - 1, 0))
        if i in (0, s.rows + 1):
            inside = top_in if i == 0 else bottom_in
            west, act, east = west * inside, act * inside, east * inside
        taps[0, i] = west.astype(BF16)
        taps[1, i] = act.astype(BF16)
        taps[2, i] = east.astype(BF16)


def spatial_dot(s, taps, weight, bias):
    step = s.rows // DOTS
    done = []
    for r in range(0, s.rows, step):
        lhs = jnp.concatenate(
            [
                taps[dx, r + dy : r + dy + step].reshape(step * s.cols, s.chans)
                for dy in range(3)
                for dx in range(3)
            ],
            axis=1,
        )
        done.append((jnp.dot(lhs, weight[...], preferred_element_type=F32) + bias[...]).astype(BF16))
    return jnp.concatenate(done, axis=0)


def temporal_dot(s, frames, weight, bias):
    lhs = jnp.concatenate(frames, axis=1)
    out = jnp.dot(lhs, weight[...], preferred_element_type=F32) + bias[...]
    return out.astype(BF16).reshape(s.rows, s.cols, s.chans)


def put(s, ref, enc, sem, f, skip=0):
    step = s.rows // QUARTERS
    parts = [pl.ds(k * step, step) for k in range(QUARTERS)]
    return [
        pltpu.make_async_copy(ref.at[f - skip, part], enc.at[f, part], sem.at[f, k])
        for k, part in enumerate(parts)
    ]


def start(copies):
    for c in copies:
        c.start()


def wait(copies):
    for c in copies:
        c.wait()


def own_kernel(s, video, halo, aff, nbias, sw, sb, tw, tb, *refs):
    cols = refs[: s.ncol]
    enc, last, lead, taps, spatial, out, sem = refs[s.ncol :]
    shift = nbias[...] * 0.5
    first = lax.axis_index("ta") == 0

    def conv(f):
        def raw_row(i):
            if i == 0:
                return halo[f, 0]
            if i == s.rows + 1:
                return halo[f, 1]
            return video[f, i - 1]

        edges = [c[pl.ds(f * s.colrow, s.colrow)] for c in cols]
        fill_taps(s, taps, raw_row, edges, aff[pl.ds(f, 1)], aff[pl.ds(s.frames + f, 1)], shift)
        spatial[f] = spatial_dot(s, taps, sw, sb)

    def encode(f):
        out[f] = temporal_dot(s, [spatial[max(f - k, 0)] for k in range(3)], tw, tb)
        start(put(s, out, enc, sem, f))

    def frame(f, _):
        conv(f)
        return _

    lax.fori_loop(0, s.frames, frame, 0)

    @pl.when(first)
    def _():
        for f in range(PREV):
            encode(f)

    for f in range(PREV, s.frames):
        last[f - PREV] = temporal_dot(s, [spatial[f - k] for k in range(3)], tw, tb)
    for f in range(PREV):
        lead[f] = spatial[f]

    @pl.when(first)
    def _():
        for f in range(PREV):
            wait(put(s, out, enc, sem, f))


def prev_kernel(s, bulk, got, nbias, sw, sb, tw, tb, lead, last, _, enc, taps, spatial, out, sem):
    shift = nbias[...] * 0.5
    for f in range(PREV, s.frames):
        start(put(s, last, enc, sem, f, PREV))

    @pl.when(lax.axis_index("ta") > 0)
    def _():
        o = PREV * s.strip
        stat = from_terms(got[o : o + s.last], 2 * PREV)
        for p in range(PREV):
            o = p * s.strip

            def raw_row(i):
                if i == 0:
                    return got[o : o + s.cols]
                if i == s.rows + 1:
                    return got[o + s.cols : o + 2 * s.cols]
                return bulk[p, i - 1]

            o2 = o + 2 * s.cols
            edges = [got[o2 + k * s.colrow : o2 + (k + 1) * s.colrow] for k in range(s.ncol)]
            fill_taps(s, taps.at[p], raw_row, edges, stat[p : p + 1], stat[PREV + p : PREV + p + 1], shift)
            spatial[p] = spatial_dot(s, taps.at[p], sw, sb)
        seq = [spatial[0], spatial[1], lead[0], lead[1]]
        for f in range(PREV):
            out[f] = temporal_dot(s, [seq[PREV + f - k] for k in range(3)], tw, tb)
            start(put(s, out, enc, sem, f))
        for f in range(PREV):
            wait(put(s, out, enc, sem, f))

    for f in range(PREV, s.frames):
        wait(put(s, last, enc, sem, f, PREV))


def mates(n, phase):
    if phase == 0:
        return [(i, i ^ 1) for i in range(n)]
    return [(i, (i - 1) % n if i % 2 == 0 else (i + 1) % n) for i in range(n)]


def local(video, norm_gain, norm_bias, spatial_weight, spatial_bias, temporal_weight, temporal_bias):
    nta, nha, nwa = (lax.axis_size(a) for a in ("ta", "ha", "wa"))
    s = Sizes(video, nha, nwa)
    c = s.chans
    sd = jax.ShapeDtypeStruct
    ring = [(i, (i + 1) % nta) for i in range(nta)]
    if nwa == 2:
        sides = [[(0, 1), (1, 0)]]
    else:
        sides = [[(i, (i + d) % nwa) for i in range(nwa)] for d in (1, -1)]
    sw = spatial_weight.reshape(9 * c, c)
    tw = temporal_weight.reshape(3 * c, c)
    gain, nbias, sb, tb = (v.reshape(1, c) for v in (norm_gain, norm_bias, spatial_bias, temporal_bias))

    (bulk,) = call(
        functools.partial(head_kernel, s),
        [sd((PREV,) + video.shape[1:], BF16)],
        name="head",
        in_specs=[VMEM],
    )(video)
    rowpay = sd((s.frames * s.cols + s.stats, c), BF16)
    stat = sd((2 * s.frames, c), F32)
    colout = [sd((s.frames * s.colrow, c), BF16)] * s.ncol
    riding = s.stats if s.fused else 0
    pay, stats, *cols = call(
        functools.partial(local_kernel, s),
        [rowpay, stat] + colout,
        name="local",
        in_specs=[VMEM, ANY],
    )(video, bulk)
    bulk = lax.ppermute(bulk, "ta", ring)
    got1 = lax.ppermute(pay, "ha", mates(nha, 0))
    payy, part, *pays = call(
        functools.partial(pair_kernel, s),
        [rowpay, stat]
        + [sd((s.frames * s.colrow + riding, c), BF16)] * s.ncol
        + [sd((s.corner + riding, c), BF16)] * s.ncol,
        name="pair",
        in_specs=[VMEM] * (3 + s.ncol),
    )(video, stats, got1, *cols)
    outer = mates(nha, 1)
    diagonal = [[(h * nwa + w, g * nwa + v) for h, g in outer for w, v in p] for p in sides]
    goty = lax.ppermute(payy, "ha", outer)
    gotx = [lax.ppermute(x, "wa", p) for x, p in zip(pays[: s.ncol], sides)]
    gotd = [lax.ppermute(x, ("ha", "wa"), p) for x, p in zip(pays[s.ncol :], diagonal)]
    if not s.fused:
        every = lax.all_gather(stats, ("ha", "wa"))
        part = merge(float(s.rows * s.cols), [every[i] for i in range(nha * nwa)])
    aff, hand, halo, *cols = call(
        functools.partial(edge_kernel, s),
        [stat, sd((PREV * s.strip + s.last, c), BF16), sd((s.frames, 2, s.cols, c), BF16)] + colout,
        name="edge",
        in_specs=[VMEM] * (4 + 2 * s.ncol),
    )(part, gain, got1, goty, *gotx, *gotd)
    got = lax.ppermute(hand, "ta", ring)
    frame = (s.rows * s.cols, c)
    taps = (3, s.rows + 2, s.cols, c)
    one = video.shape[1:]
    enc, last, lead = call(
        functools.partial(own_kernel, s),
        [sd(video.shape, BF16), sd((s.frames - PREV,) + one, BF16), sd((PREV,) + frame, BF16)],
        out_specs=[ANY, VMEM, VMEM],
        scratch=[
            pltpu.VMEM(taps, BF16),
            pltpu.VMEM((s.frames,) + frame, BF16),
            pltpu.VMEM((PREV,) + one, BF16),
            pltpu.SemaphoreType.DMA((PREV, QUARTERS)),
        ],
        name="own",
        in_specs=[VMEM] * (8 + s.ncol),
    )(video, halo, aff, nbias, sw, sb, tw, tb, *cols)
    (enc,) = call(
        functools.partial(prev_kernel, s),
        [sd(video.shape, BF16)],
        out_specs=[ANY],
        scratch=[
            pltpu.VMEM((PREV,) + taps, BF16),
            pltpu.VMEM((PREV,) + frame, BF16),
            pltpu.VMEM((PREV,) + one, BF16),
            pltpu.SemaphoreType.DMA((s.frames, QUARTERS)),
        ],
        name="prev",
        in_specs=[VMEM] * 9 + [ANY],
        input_output_aliases={9: 0},
    )(bulk, got, nbias, sw, sb, tw, tb, lead, last, enc)
    return enc


def solution(mesh):
    placed = (P("ta", "ha", "wa", None), P(), P(), P(), P(), P(), P())
    return jax.shard_map(
        local, mesh=mesh, in_specs=placed, out_specs=P("ta", "ha", "wa", None), check_vma=False
    )
```

```python
import functools

import jax
import jax.numpy as jnp
from jax import lax
from jax.experimental import pallas as pl
from jax.experimental.pallas import tpu as pltpu
from jax.sharding import PartitionSpec as P

G = 32
EPS = 1e-06
QUARTERS = 4
DOTS = 6
PREV = 2
F32 = jnp.float32
BF16 = jnp.bfloat16
VMEM = pl.BlockSpec(memory_space=pltpu.VMEM)
ANY = pl.BlockSpec(memory_space=pl.ANY)


def call(kernel, outs, out_specs=None, scratch=(), flops=1024, name=None, **kw):
    return pl.pallas_call(
        kernel,
        out_shape=outs,
        out_specs=out_specs or [VMEM] * len(outs),
        scratch_shapes=list(scratch),
        compiler_params=pltpu.CompilerParams(vmem_limit_bytes=24 << 20),
        cost_estimate=pl.CostEstimate(flops=flops, bytes_accessed=1024, transcendentals=0),
        name=name,
        **kw,
    )


def pad_to(n, k):
    return (n + k - 1) // k * k


def split3(x):
    hi = x.astype(BF16)
    rest = x - hi.astype(F32)
    mid = rest.astype(BF16)
    low = (rest - mid.astype(F32)).astype(BF16)
    return hi, mid, low


def as_terms(x, rows):
    parts = jnp.concatenate([t.astype(F32) for t in split3(x)], axis=0)
    fill = rows - parts.shape[0]
    if fill:
        parts = jnp.concatenate([parts, jnp.zeros((fill, x.shape[1]), F32)], axis=0)
    return parts.astype(BF16)


def from_terms(t, rows):
    t = t.astype(F32)
    return t[:rows] + t[rows : 2 * rows] + t[2 * rows : 3 * rows]


class Sizes:
    def __init__(self, video, ha, wa):
        self.frames, self.rows, self.cols, self.chans = video.shape
        self.ha, self.wa = ha, wa
        self.ncol = 1 if wa == 2 else 2
        self.fused = ha == 4 and wa == 2
        self.colrow = pad_to(self.rows + 2, 16)
        self.strip = 2 * self.cols + self.ncol * self.colrow
        self.stats = pad_to(3 * 2 * self.frames, 16)
        self.early = (PREV - 1) * self.rows + self.rows // 12
        self.corner = pad_to(self.frames, 16)


def head_kernel(s, video, early, late):
    flat = (PREV * s.rows, s.cols, s.chans)
    sent = video[s.frames - PREV :].reshape(flat)
    early[...] = sent[: s.early]
    late[...] = sent[s.early :]


def local_kernel(s, video, early, pay, stats, *cols):
    ha, wa = lax.axis_index("ha"), lax.axis_index("wa")
    even = lax.rem(ha, 2) == 0
    means, squares = [], []
    for f in range(s.frames):
        total = jnp.zeros((s.cols, s.chans), F32)
        for r in range(s.rows):
            total = total + video[f, r].astype(F32)
        mean = jnp.sum(total, axis=0, keepdims=True) * (1.0 / (s.rows * s.cols))
        spread = jnp.zeros((s.cols, s.chans), F32)
        left, right = [], []
        for r in range(s.rows):
            x = video[f, r].astype(F32)
            left.append(x[:1])
            right.append(x[s.cols - 1 :])
            x = x - mean
            spread = spread + x * x
        means.append(mean)
        squares.append(jnp.sum(spread, axis=0, keepdims=True))
        fill = [jnp.zeros((s.colrow - s.rows, s.chans), F32)]
        left = jnp.concatenate(left + fill, axis=0)
        right = jnp.concatenate(right + fill, axis=0)
        if s.ncol == 1:
            edges = [jnp.where(wa == 0, right, left)]
        else:
            edges = [right, left]
        for ref, e in zip(cols, edges):
            ref[f * s.colrow : (f + 1) * s.colrow] = e.astype(BF16)
        top = video[f, 0].astype(F32)
        bottom = video[f, s.rows - 1].astype(F32)
        pay[f * s.cols : (f + 1) * s.cols] = jnp.where(even, bottom, top).astype(BF16)
    stat = jnp.concatenate(means + squares, axis=0)
    stats[...] = stat
    o = s.frames * s.cols
    pay[o : o + s.stats] = as_terms(stat, s.stats)


def merge(n, parts):
    half = parts[0].shape[0] // 2
    mean = sum(p[:half] for p in parts) * (1.0 / len(parts))
    square = sum(p[half:] + n * (p[:half] - mean) * (p[:half] - mean) for p in parts)
    return jnp.concatenate([mean, square], axis=0)


def pair_kernel(s, video, stats, got, *refs):
    cols, refs = refs[: s.ncol], refs[s.ncol + 1 :]
    _, payy, part = refs[:3]
    payx, payd = refs[3 : 3 + s.ncol], refs[3 + s.ncol :]
    ha, wa = lax.axis_index("ha"), lax.axis_index("wa")
    even = lax.rem(ha, 2) == 0
    o = s.frames * s.cols
    stat = merge(float(s.rows * s.cols), [stats[...], from_terms(got[o : o + s.stats], 2 * s.frames)])
    part[...] = stat
    terms = as_terms(stat, s.stats)
    at = lax.broadcasted_iota(jnp.int32, (s.colrow, s.chans), 0)
    cells = [[] for _ in range(s.ncol)]
    for f in range(s.frames):
        top = video[f, 0].astype(F32)
        bottom = video[f, s.rows - 1].astype(F32)
        outer = jnp.where(even, top, bottom)
        payy[f * s.cols : (f + 1) * s.cols] = outer.astype(BF16)
        inner = got[f * s.cols : (f + 1) * s.cols].astype(F32)
        for k in range(s.ncol):
            right = wa == 0 if s.ncol == 1 else k == 0
            cell = jnp.where(right, inner[s.cols - 1 :], inner[:1])
            cells[k].append(jnp.where(right, outer[s.cols - 1 :], outer[:1]))
            edge = cols[k][f * s.colrow : (f + 1) * s.colrow].astype(F32)
            edge = jnp.where(at >= s.rows, cell, edge)
            payx[k][f * s.colrow : (f + 1) * s.colrow] = edge.astype(BF16)
    for k in range(s.ncol):
        fill = s.corner - s.frames
        rows = cells[k] + ([jnp.zeros((fill, s.chans), F32)] if fill else [])
        payd[k][: s.corner] = jnp.concatenate(rows, axis=0).astype(BF16)
    payy[o : o + s.stats] = terms
    if s.fused:
        o = s.frames * s.colrow
        payx[0][o : o + s.stats] = terms
        payd[0][s.corner : s.corner + s.stats] = terms


def group_kernel(s, part, gain, goty, *refs):
    gotx, gotd = refs[: s.ncol], refs[s.ncol : 2 * s.ncol]
    aff, moved = refs[2 * s.ncol :]
    rows = 2 * s.frames
    count = float(s.rows * s.cols * s.ha * s.wa)
    stat = part[...]
    if s.fused:
        offsets = ((goty, s.frames * s.cols), (gotx[0], s.frames * s.colrow), (gotd[0], s.corner))
        stat = merge(count / 4, [stat] + [from_terms(ref[o : o + s.stats], rows) for ref, o in offsets])
    width = s.chans // G
    a = lax.broadcasted_iota(jnp.int32, (s.chans, s.chans), 0) // width
    b = lax.broadcasted_iota(jnp.int32, (s.chans, s.chans), 1) // width
    group = jnp.where(a == b, 1.0, 0.0).astype(BF16)

    def tot(x):
        terms = jnp.concatenate(split3(x), axis=0)
        y = jnp.dot(terms, group, preferred_element_type=F32)
        n = s.frames
        return y[:n] + y[n : 2 * n] + y[2 * n :]

    m, q = stat[: s.frames], stat[s.frames :]
    mean = tot(m) * (1.0 / width)
    var = tot(q + count * (m - mean) * (m - mean)) * (1.0 / (count * width))
    scale = lax.rsqrt(var + EPS) * gain[...] * 0.5
    aff[: s.frames] = mean
    aff[s.frames :] = scale
    first = s.frames - PREV
    moved[:PREV] = mean[first:]
    moved[PREV:] = scale[first:]


def edge_kernel(s, aff, got, goty, *refs):
    gotx, gotd = refs[: s.ncol], refs[s.ncol : 2 * s.ncol]
    hand, halo, *cols = refs[2 * s.ncol :]
    even = lax.rem(lax.axis_index("ha"), 2) == 0
    first = s.frames - PREV
    at = lax.broadcasted_iota(jnp.int32, (s.colrow, s.chans), 0)
    for f in range(s.frames):
        p = (f - first) * s.strip
        one = got[f * s.cols : (f + 1) * s.cols].astype(F32)
        two = goty[f * s.cols : (f + 1) * s.cols].astype(F32)
        top = jnp.where(even, two, one).astype(BF16)
        bottom = jnp.where(even, one, two).astype(BF16)
        halo[f, 0] = top
        halo[f, 1] = bottom
        if f >= first:
            hand[p : p + s.cols] = top
            hand[p + s.cols : p + 2 * s.cols] = bottom
        for k in range(s.ncol):
            cell = gotd[k][: s.corner].astype(F32)[f : f + 1]
            edge = gotx[k][f * s.colrow : (f + 1) * s.colrow].astype(F32)
            outer = jnp.where(even, s.rows, s.rows + 1)
            edge = jnp.where(at == outer, cell, edge).astype(BF16)
            cols[k][f * s.colrow : (f + 1) * s.colrow] = edge
            if f >= first:
                o = p + 2 * s.cols + k * s.colrow
                hand[o : o + s.colrow] = edge


def activation(x, mean, scale, shift):
    h = (x - mean) * scale + shift
    return h + h * jnp.tanh(h)


def fill_taps(s, taps, raw_row, edges, mean, scale, shift):
    ha, wa = lax.axis_index("ha"), lax.axis_index("wa")
    top_in = jnp.where(ha > 0, 1.0, 0.0).astype(F32)
    bottom_in = jnp.where(ha < s.ha - 1, 1.0, 0.0).astype(F32)
    left_in = jnp.where(wa > 0, 1.0, 0.0).astype(F32)
    right_in = jnp.where(wa < s.wa - 1, 1.0, 0.0).astype(F32)
    if edges is not None:
        acts = [activation(e.astype(F32), mean, scale, shift) for e in edges]
        left, right = acts[0] * left_in, acts[-1] * right_in
    at = lax.broadcasted_iota(jnp.int32, (s.cols, s.chans), 0)
    for i in range(s.rows + 2):
        raw = raw_row(i)
        if raw is None:
            for dx in range(3):
                taps[dx, i] = jnp.zeros((s.cols, s.chans), BF16)
            continue
        act = activation(raw.astype(F32), mean, scale, shift)
        j = s.rows if i == 0 else s.rows + 1 if i == s.rows + 1 else i - 1
        lcell, rcell = (0.0, 0.0) if edges is None else (left[j : j + 1], right[j : j + 1])
        west = jnp.where(at == 0, lcell, pltpu.roll(act, 1, 0))
        east = jnp.where(at == s.cols - 1, rcell, pltpu.roll(act, s.cols - 1, 0))
        if i in (0, s.rows + 1):
            inside = top_in if i == 0 else bottom_in
            west, act, east = west * inside, act * inside, east * inside
        taps[0, i] = west.astype(BF16)
        taps[1, i] = act.astype(BF16)
        taps[2, i] = east.astype(BF16)


def spatial_dot(s, taps, weight, bias):
    step = s.rows // DOTS
    done = []
    for r in range(0, s.rows, step):
        lhs = jnp.concatenate(
            [
                taps[dx, r + dy : r + dy + step].reshape(step * s.cols, s.chans)
                for dy in range(3)
                for dx in range(3)
            ],
            axis=1,
        )
        done.append((jnp.dot(lhs, weight[...], preferred_element_type=F32) + bias[...]).astype(BF16))
    return jnp.concatenate(done, axis=0)


def temporal_dot(s, frames, weight, bias):
    lhs = jnp.concatenate(frames, axis=1)
    out = jnp.dot(lhs, weight[...], preferred_element_type=F32) + bias[...]
    return out.astype(BF16).reshape(s.rows, s.cols, s.chans)


def put(s, ref, enc, sem, f, quarters=range(QUARTERS)):
    step = s.rows // QUARTERS
    return [
        pltpu.make_async_copy(
            ref.at[f, pl.ds(k * step, step)], enc.at[f, pl.ds(k * step, step)], sem.at[f, k]
        )
        for k in quarters
    ]


def start(copies):
    for c in copies:
        c.start()


def wait(copies):
    for c in copies:
        c.wait()


def own_kernel(s, video, halo, aff, nbias, sw, sb, tw, tb, *refs):
    cols = refs[: s.ncol]
    enc, base, taps, spatial, out, sem = refs[s.ncol + 1 :]
    shift = nbias[...] * 0.5
    first = lax.axis_index("ta") == 0

    def frame(f, _):
        def raw_row(i):
            if i == 0:
                return halo[f, 0]
            if i == s.rows + 1:
                return halo[f, 1]
            return video[f, i - 1]

        edges = [c[pl.ds(f * s.colrow, s.colrow)] for c in cols]
        fill_taps(s, taps, raw_row, edges, aff[pl.ds(f, 1)], aff[pl.ds(s.frames + f, 1)], shift)
        spatial[f] = spatial_dot(s, taps, sw, sb)
        return _

    lax.fori_loop(0, s.frames, frame, 0)

    def encode(f):
        out[f] = temporal_dot(s, [spatial[max(f - k, 0)] for k in range(3)], tw, tb)
        start(put(s, out, enc, sem, f))

    for f in range(PREV, s.frames):
        encode(f)

    @pl.when(first)
    def _():
        for f in range(PREV):
            encode(f)
        for f in range(PREV):
            wait(put(s, out, enc, sem, f))

    @pl.when(jnp.logical_not(first))
    def _():
        for f in range(PREV):
            lhs = jnp.concatenate([spatial[f - k] for k in range(f + 1)], axis=1)
            weight = tw[: (f + 1) * s.chans]
            base[f] = jnp.dot(lhs, weight, preferred_element_type=F32) + tb[...]

    for f in range(PREV, s.frames):
        wait(put(s, out, enc, sem, f))


def inner_kernel(s, early, late, moved, nbias, sw, sb, taps, spatial):
    shift = nbias[...] * 0.5

    @pl.when(lax.axis_index("ta") > 0)
    def _():
        for p in range(PREV):

            def raw_row(i):
                if i == 0 or i == s.rows + 1:
                    return None
                r = p * s.rows + i - 1
                return early[r] if r < s.early else late[r - s.early]

            fill_taps(s, taps.at[p], raw_row, None, moved[p : p + 1], moved[PREV + p : PREV + p + 1], shift)
            spatial[p] = spatial_dot(s, taps.at[p], sw, sb)


def outer_kernel(s, got, moved, taps, spatial, nbias, sw, sb, tw, base, _, enc, grid, out, sem):
    ha, wa = lax.axis_index("ha"), lax.axis_index("wa")
    shift = nbias[...] * 0.5
    inside = [jnp.where(ha > 0, 1.0, 0.0).astype(F32), jnp.where(ha < s.ha - 1, 1.0, 0.0).astype(F32)]
    at = lax.broadcasted_iota(jnp.int32, (s.cols, s.chans), 0)
    down = lax.broadcasted_iota(jnp.int32, (s.colrow, s.chans), 0)
    if s.ncol == 1:
        sides = [wa == 0]
        present = [jnp.ones((), F32)]
    else:
        sides = [False, True]
        present = [jnp.where(wa > 0, 1.0, 0.0).astype(F32), jnp.where(wa < s.wa - 1, 1.0, 0.0).astype(F32)]

    @pl.when(lax.axis_index("ta") > 0)
    def _():
        lhs = []
        for p in range(PREV):
            mean, scale = moved[p : p + 1], moved[PREV + p : PREV + p + 1]
            o = p * s.strip
            acts = []
            for k in range(2):
                raw = got[o + k * s.cols : o + (k + 1) * s.cols].astype(F32)
                act = activation(raw, mean, scale, shift) * inside[k]
                west = jnp.where(at == 0, 0.0, pltpu.roll(act, 1, 0))
                east = jnp.where(at == s.cols - 1, 0.0, pltpu.roll(act, s.cols - 1, 0))
                acts.append((west, act, east))
            top = [a.astype(BF16) for a in acts[0]]
            bottom = [a.astype(BF16) for a in acts[1]]
            lhs.append(
                jnp.concatenate(top + [taps[p, dx, i] for i in (1, 2) for dx in range(3)], axis=1)
            )
            n = s.rows
            lhs.append(
                jnp.concatenate([taps[p, dx, i] for i in (n - 1, n) for dx in range(3)] + bottom, axis=1)
            )
            for k in range(s.ncol):
                o2 = o + 2 * s.cols + k * s.colrow
                cell = activation(got[o2 : o2 + s.colrow].astype(F32), mean, scale, shift) * present[k]
                upper = cell[n : n + 1] * inside[0]
                lower = cell[n + 1 : n + 2] * inside[1]
                right = sides[k]

                def end(x):
                    return jnp.where(right, x[-1:], x[:1])

                def column(d):
                    rows = []
                    for i in range(1, n + 1):
                        tile = taps[p, 1, i].astype(F32)
                        if d == 0:
                            rows.append(jnp.where(right, tile[s.cols - 1 :], tile[:1]))
                        else:
                            rows.append(jnp.where(right, tile[s.cols - 2 : s.cols - 1], tile[1:2]))
                    fill = jnp.zeros((s.colrow - n, s.chans), F32)
                    return jnp.concatenate(rows + [fill], axis=0)

                here, inner = column(0), column(1)
                far = jnp.where(down < n, cell, 0.0)
                ends = [
                    (end(acts[0][1]), end(acts[1][1])),
                    (
                        jnp.where(right, acts[0][1][s.cols - 2 : s.cols - 1], acts[0][1][1:2]),
                        jnp.where(right, acts[1][1][s.cols - 2 : s.cols - 1], acts[1][1][1:2]),
                    ),
                    (upper, lower),
                ]
                steps = []
                for dy in range(3):
                    group = []
                    for x, (first, final) in zip((here, inner, far), ends):
                        if dy == 0:
                            x = jnp.where(down == 0, first, pltpu.roll(x, 1, 0))
                        elif dy == 2:
                            x = jnp.where(down == n - 1, final, pltpu.roll(x, s.colrow - 1, 0))
                        group.append(x)
                    mid, inn, out_ = group
                    steps += [jnp.where(right, inn, out_), mid, jnp.where(right, out_, inn)]
                lhs.append(jnp.concatenate([x.astype(BF16) for x in steps], axis=1))
        border = jnp.dot(jnp.concatenate(lhs, axis=0), sw[...], preferred_element_type=F32) + sb[...]
        size = 2 * s.cols + s.ncol * s.colrow
        tile = 16
        cells = lax.broadcasted_iota(jnp.int32, (tile, s.chans), 0)
        for p in range(PREV):
            o = p * size
            n = (s.rows - 1) * s.cols
            grid[p, : s.cols] = border[o : o + s.cols].astype(BF16)
            grid[p, s.cols : n] = spatial[p, s.cols : n]
            grid[p, n:] = border[o + s.cols : o + 2 * s.cols].astype(BF16)
            for k in range(s.ncol):
                place = jnp.where(sides[k], tile - 1, 0)
                mask = cells == place
                for h in range(s.rows):
                    o2 = o + 2 * s.cols + k * s.colrow + h
                    at0 = h * s.cols + jnp.where(sides[k], s.cols - tile, 0)
                    part = pl.ds(pl.multiple_of(at0, tile), tile)
                    row = jnp.where(mask, border[o2 : o2 + 1], grid[p, part].astype(F32))
                    grid[p, part] = row.astype(BF16)
        half = s.rows * s.cols // 2
        for f in range(PREV):
            for k in range(2):
                part = slice(k * half, (k + 1) * half)
                lhs = jnp.concatenate([grid[q, part] for q in range(PREV - 1, f - 1, -1)], axis=1)
                y = jnp.dot(lhs, tw[(f + 1) * s.chans :], preferred_element_type=F32) + base[f, part]
                block = (s.rows // 2, s.cols, s.chans)
                out[f, k * block[0] : (k + 1) * block[0]] = y.astype(BF16).reshape(block)
                start(put(s, out, enc, sem, f, range(k * QUARTERS // 2, (k + 1) * QUARTERS // 2)))
        for f in range(PREV):
            wait(put(s, out, enc, sem, f))


def mates(n, phase):
    if phase == 0:
        return [(i, i ^ 1) for i in range(n)]
    return [(i, (i - 1) % n if i % 2 == 0 else (i + 1) % n) for i in range(n)]


def local(video, norm_gain, norm_bias, spatial_weight, spatial_bias, temporal_weight, temporal_bias):
    nta, nha, nwa = (lax.axis_size(a) for a in ("ta", "ha", "wa"))
    s = Sizes(video, nha, nwa)
    c = s.chans
    sd = jax.ShapeDtypeStruct
    ring = [(i, (i + 1) % nta) for i in range(nta)]
    if nwa == 2:
        sides = [[(0, 1), (1, 0)]]
    else:
        sides = [[(i, (i + d) % nwa) for i in range(nwa)] for d in (1, -1)]
    sw = spatial_weight.reshape(9 * c, c)
    tw = temporal_weight.reshape(3 * c, c)
    gain, nbias, sb, tb = (v.reshape(1, c) for v in (norm_gain, norm_bias, spatial_bias, temporal_bias))

    one = video.shape[1:]
    late_shape = sd((PREV * s.rows - s.early,) + one[1:], BF16)
    early, late = call(
        functools.partial(head_kernel, s),
        [sd((s.early,) + one[1:], BF16), late_shape],
        name="head",
        in_specs=[VMEM],
    )(video)
    rowpay = sd((s.frames * s.cols + s.stats, c), BF16)
    stat = sd((2 * s.frames, c), F32)
    colout = [sd((s.frames * s.colrow, c), BF16)] * s.ncol
    riding = s.stats if s.fused else 0
    pay, stats, *cols = call(
        functools.partial(local_kernel, s),
        [rowpay, stat] + colout,
        name="local",
        in_specs=[VMEM, ANY],
    )(video, early)
    early = lax.ppermute(early, "ta", ring)
    got1 = lax.ppermute(pay, "ha", mates(nha, 0))
    late, payy, part, *pays = call(
        functools.partial(pair_kernel, s),
        [late_shape, rowpay, stat]
        + [sd((s.frames * s.colrow + riding, c), BF16)] * s.ncol
        + [sd((s.corner + riding, c), BF16)] * s.ncol,
        out_specs=[ANY] + [VMEM] * (2 + 2 * s.ncol),
        name="pair",
        in_specs=[VMEM] * (3 + s.ncol) + [ANY],
        input_output_aliases={3 + s.ncol: 0},
    )(video, stats, got1, *cols, late)
    outer = mates(nha, 1)
    diagonal = [[(h * nwa + w, g * nwa + v) for h, g in outer for w, v in p] for p in sides]
    goty = lax.ppermute(payy, "ha", outer)
    gotx = [lax.ppermute(x, "wa", p) for x, p in zip(pays[: s.ncol], sides)]
    gotd = [lax.ppermute(x, ("ha", "wa"), p) for x, p in zip(pays[s.ncol :], diagonal)]
    late = lax.ppermute(late, "ta", ring[:-1])
    if not s.fused:
        every = lax.all_gather(stats, ("ha", "wa"))
        part = merge(float(s.rows * s.cols), [every[i] for i in range(nha * nwa)])
    aff, moved = call(
        functools.partial(group_kernel, s),
        [stat, sd((2 * PREV, c), F32)],
        name="group",
        in_specs=[VMEM] * (3 + 2 * s.ncol),
    )(part, gain, goty, *gotx, *gotd)
    moved = lax.ppermute(moved, "ta", ring)
    hand, halo, *cols = call(
        functools.partial(edge_kernel, s),
        [sd((PREV * s.strip, c), BF16), sd((s.frames, 2, s.cols, c), BF16)] + colout,
        name="edge",
        in_specs=[VMEM] * (3 + 2 * s.ncol),
    )(aff, got1, goty, *gotx, *gotd)
    got = lax.ppermute(hand, "ta", ring)
    frame = (s.rows * s.cols, c)
    taps = (3, s.rows + 2, s.cols, c)
    enc, base = call(
        functools.partial(own_kernel, s),
        [sd(video.shape, BF16), sd((PREV,) + frame, F32)],
        out_specs=[ANY, VMEM],
        scratch=[
            pltpu.VMEM(taps, BF16),
            pltpu.VMEM((s.frames,) + frame, BF16),
            pltpu.VMEM((s.frames,) + one, BF16),
            pltpu.SemaphoreType.DMA((s.frames, QUARTERS)),
        ],
        flops=2 * s.rows * s.cols * c * c * (9 * s.frames + 3 * (s.frames - PREV)),
        name="own",
        in_specs=[VMEM] * (8 + s.ncol) + [ANY],
    )(video, halo, aff, nbias, sw, sb, tw, tb, *cols, early)
    grid, inner = call(
        functools.partial(inner_kernel, s),
        [sd((PREV,) + taps, BF16), sd((PREV,) + frame, BF16)],
        name="inner",
        in_specs=[VMEM] * 6,
    )(early, late, moved, nbias, sw, sb)
    (enc,) = call(
        functools.partial(outer_kernel, s),
        [sd(video.shape, BF16)],
        out_specs=[ANY],
        scratch=[
            pltpu.VMEM((PREV,) + frame, BF16),
            pltpu.VMEM((PREV,) + one, BF16),
            pltpu.SemaphoreType.DMA((PREV, QUARTERS)),
        ],
        name="outer",
        in_specs=[VMEM] * 9 + [ANY],
        input_output_aliases={9: 0},
    )(got, moved, grid, inner, nbias, sw, sb, tw, base, enc)
    return enc


def solution(mesh):
    placed = (P("ta", "ha", "wa", None), P(), P(), P(), P(), P(), P())
    return jax.shard_map(
        local, mesh=mesh, in_specs=placed, out_specs=P("ta", "ha", "wa", None), check_vma=False
    )
```

```python
import functools

import jax
import jax.numpy as jnp
from jax import lax
from jax.experimental import pallas as pl
from jax.experimental.pallas import tpu as pltpu
from jax.sharding import PartitionSpec as P

G = 32
EPS = 1e-06
QUARTERS = 4
DOTS = 6
PREV = 2
F32 = jnp.float32
BF16 = jnp.bfloat16
VMEM = pl.BlockSpec(memory_space=pltpu.VMEM)
ANY = pl.BlockSpec(memory_space=pl.ANY)


def call(kernel, outs, out_specs=None, scratch=(), flops=1024, name=None, **kw):
    return pl.pallas_call(
        kernel,
        out_shape=outs,
        out_specs=out_specs or [VMEM] * len(outs),
        scratch_shapes=list(scratch),
        compiler_params=pltpu.CompilerParams(vmem_limit_bytes=24 << 20),
        cost_estimate=pl.CostEstimate(flops=flops, bytes_accessed=1024, transcendentals=0),
        name=name,
        **kw,
    )


def pad_to(n, k):
    return (n + k - 1) // k * k


def split3(x):
    hi = x.astype(BF16)
    rest = x - hi.astype(F32)
    mid = rest.astype(BF16)
    low = (rest - mid.astype(F32)).astype(BF16)
    return hi, mid, low


def as_terms(x, rows):
    parts = jnp.concatenate([t.astype(F32) for t in split3(x)], axis=0)
    fill = rows - parts.shape[0]
    if fill:
        parts = jnp.concatenate([parts, jnp.zeros((fill, x.shape[1]), F32)], axis=0)
    return parts.astype(BF16)


def from_terms(t, rows):
    t = t.astype(F32)
    return t[:rows] + t[rows : 2 * rows] + t[2 * rows : 3 * rows]


class Sizes:
    def __init__(self, video, ha, wa):
        self.frames, self.rows, self.cols, self.chans = video.shape
        self.ha, self.wa = ha, wa
        self.ncol = 1 if wa == 2 else 2
        self.fused = ha == 4 and wa == 2
        self.colrow = pad_to(self.rows + 2, 16)
        self.strip = 2 * self.cols + self.ncol * self.colrow
        self.stats = pad_to(3 * 2 * self.frames, 16)
        self.early = (PREV - 1) * self.rows + self.rows // 12
        self.tail = self.rows // 4 + 1
        self.late = PREV * self.rows - self.early - self.tail
        self.corner = pad_to(self.frames, 16)


def head_kernel(s, video, early, late):
    flat = (PREV * s.rows, s.cols, s.chans)
    sent = video[s.frames - PREV :].reshape(flat)
    early[...] = sent[: s.early]
    late[...] = sent[s.early : s.early + s.late]


def local_kernel(s, video, early, pay, stats, *cols):
    ha, wa = lax.axis_index("ha"), lax.axis_index("wa")
    even = lax.rem(ha, 2) == 0
    means, squares = [], []
    for f in range(s.frames):
        total = jnp.zeros((s.cols, s.chans), F32)
        for r in range(s.rows):
            total = total + video[f, r].astype(F32)
        mean = jnp.sum(total, axis=0, keepdims=True) * (1.0 / (s.rows * s.cols))
        spread = jnp.zeros((s.cols, s.chans), F32)
        left, right = [], []
        for r in range(s.rows):
            x = video[f, r].astype(F32)
            left.append(x[:1])
            right.append(x[s.cols - 1 :])
            x = x - mean
            spread = spread + x * x
        means.append(mean)
        squares.append(jnp.sum(spread, axis=0, keepdims=True))
        fill = [jnp.zeros((s.colrow - s.rows, s.chans), F32)]
        left = jnp.concatenate(left + fill, axis=0)
        right = jnp.concatenate(right + fill, axis=0)
        if s.ncol == 1:
            edges = [jnp.where(wa == 0, right, left)]
        else:
            edges = [right, left]
        for ref, e in zip(cols, edges):
            ref[f * s.colrow : (f + 1) * s.colrow] = e.astype(BF16)
        top = video[f, 0].astype(F32)
        bottom = video[f, s.rows - 1].astype(F32)
        pay[f * s.cols : (f + 1) * s.cols] = jnp.where(even, bottom, top).astype(BF16)
    stat = jnp.concatenate(means + squares, axis=0)
    stats[...] = stat
    o = s.frames * s.cols
    pay[o : o + s.stats] = as_terms(stat, s.stats)


def merge(n, parts):
    half = parts[0].shape[0] // 2
    mean = sum(p[:half] for p in parts) * (1.0 / len(parts))
    square = sum(p[half:] + n * (p[:half] - mean) * (p[:half] - mean) for p in parts)
    return jnp.concatenate([mean, square], axis=0)


def pair_kernel(s, video, stats, got, *refs):
    cols, refs = refs[: s.ncol], refs[s.ncol + 1 :]
    _, payy, part = refs[:3]
    payx, payd = refs[3 : 3 + s.ncol], refs[3 + s.ncol :]
    ha, wa = lax.axis_index("ha"), lax.axis_index("wa")
    even = lax.rem(ha, 2) == 0
    o = s.frames * s.cols
    stat = merge(float(s.rows * s.cols), [stats[...], from_terms(got[o : o + s.stats], 2 * s.frames)])
    part[...] = stat
    terms = as_terms(stat, s.stats)
    at = lax.broadcasted_iota(jnp.int32, (s.colrow, s.chans), 0)
    cells = [[] for _ in range(s.ncol)]
    for f in range(s.frames):
        top = video[f, 0].astype(F32)
        bottom = video[f, s.rows - 1].astype(F32)
        outer = jnp.where(even, top, bottom)
        payy[f * s.cols : (f + 1) * s.cols] = outer.astype(BF16)
        inner = got[f * s.cols : (f + 1) * s.cols].astype(F32)
        for k in range(s.ncol):
            right = wa == 0 if s.ncol == 1 else k == 0
            cell = jnp.where(right, inner[s.cols - 1 :], inner[:1])
            cells[k].append(jnp.where(right, outer[s.cols - 1 :], outer[:1]))
            edge = cols[k][f * s.colrow : (f + 1) * s.colrow].astype(F32)
            edge = jnp.where(at >= s.rows, cell, edge)
            payx[k][f * s.colrow : (f + 1) * s.colrow] = edge.astype(BF16)
    for k in range(s.ncol):
        fill = s.corner - s.frames
        rows = cells[k] + ([jnp.zeros((fill, s.chans), F32)] if fill else [])
        payd[k][: s.corner] = jnp.concatenate(rows, axis=0).astype(BF16)
    payy[o : o + s.stats] = terms
    if s.fused:
        o = s.frames * s.colrow
        payx[0][o : o + s.stats] = terms
        payd[0][s.corner : s.corner + s.stats] = terms


def group_kernel(s, part, gain, goty, *refs):
    gotx, gotd = refs[: s.ncol], refs[s.ncol : 2 * s.ncol]
    aff, moved = refs[2 * s.ncol :]
    rows = 2 * s.frames
    count = float(s.rows * s.cols * s.ha * s.wa)
    stat = part[...]
    if s.fused:
        offsets = ((goty, s.frames * s.cols), (gotx[0], s.frames * s.colrow), (gotd[0], s.corner))
        stat = merge(count / 4, [stat] + [from_terms(ref[o : o + s.stats], rows) for ref, o in offsets])
    width = s.chans // G
    a = lax.broadcasted_iota(jnp.int32, (s.chans, s.chans), 0) // width
    b = lax.broadcasted_iota(jnp.int32, (s.chans, s.chans), 1) // width
    group = jnp.where(a == b, 1.0, 0.0).astype(BF16)

    def tot(x):
        terms = jnp.concatenate(split3(x), axis=0)
        y = jnp.dot(terms, group, preferred_element_type=F32)
        n = s.frames
        return y[:n] + y[n : 2 * n] + y[2 * n :]

    m, q = stat[: s.frames], stat[s.frames :]
    mean = tot(m) * (1.0 / width)
    var = tot(q + count * (m - mean) * (m - mean)) * (1.0 / (count * width))
    scale = lax.rsqrt(var + EPS) * gain[...] * 0.5
    aff[: s.frames] = mean
    aff[s.frames :] = scale
    first = s.frames - PREV
    moved[:PREV] = mean[first:]
    moved[PREV:] = scale[first:]


def edge_kernel(s, aff, video, got, goty, *refs):
    gotx, gotd = refs[: s.ncol], refs[s.ncol : 2 * s.ncol]
    hand, halo, *cols = refs[2 * s.ncol :]
    even = lax.rem(lax.axis_index("ha"), 2) == 0
    first = s.frames - PREV
    o = PREV * s.strip
    rest = video[s.frames - 1, s.rows - s.tail :]
    hand[o : o + s.tail * s.cols] = rest.reshape(s.tail * s.cols, s.chans)
    at = lax.broadcasted_iota(jnp.int32, (s.colrow, s.chans), 0)
    for f in range(s.frames):
        p = (f - first) * s.strip
        one = got[f * s.cols : (f + 1) * s.cols].astype(F32)
        two = goty[f * s.cols : (f + 1) * s.cols].astype(F32)
        top = jnp.where(even, two, one).astype(BF16)
        bottom = jnp.where(even, one, two).astype(BF16)
        halo[f, 0] = top
        halo[f, 1] = bottom
        if f >= first:
            hand[p : p + s.cols] = top
            hand[p + s.cols : p + 2 * s.cols] = bottom
        for k in range(s.ncol):
            cell = gotd[k][: s.corner].astype(F32)[f : f + 1]
            edge = gotx[k][f * s.colrow : (f + 1) * s.colrow].astype(F32)
            outer = jnp.where(even, s.rows, s.rows + 1)
            edge = jnp.where(at == outer, cell, edge).astype(BF16)
            cols[k][f * s.colrow : (f + 1) * s.colrow] = edge
            if f >= first:
                o = p + 2 * s.cols + k * s.colrow
                hand[o : o + s.colrow] = edge


def activation(x, mean, scale, shift):
    h = (x - mean) * scale + shift
    return h + h * jnp.tanh(h)


def fill_taps(s, taps, raw_row, edges, mean, scale, shift):
    ha, wa = lax.axis_index("ha"), lax.axis_index("wa")
    top_in = jnp.where(ha > 0, 1.0, 0.0).astype(F32)
    bottom_in = jnp.where(ha < s.ha - 1, 1.0, 0.0).astype(F32)
    left_in = jnp.where(wa > 0, 1.0, 0.0).astype(F32)
    right_in = jnp.where(wa < s.wa - 1, 1.0, 0.0).astype(F32)
    if edges is not None:
        acts = [activation(e.astype(F32), mean, scale, shift) for e in edges]
        left, right = acts[0] * left_in, acts[-1] * right_in
    at = lax.broadcasted_iota(jnp.int32, (s.cols, s.chans), 0)
    for i in range(s.rows + 2):
        raw = raw_row(i)
        if raw is None:
            for dx in range(3):
                taps[dx, i] = jnp.zeros((s.cols, s.chans), BF16)
            continue
        act = activation(raw.astype(F32), mean, scale, shift)
        j = s.rows if i == 0 else s.rows + 1 if i == s.rows + 1 else i - 1
        lcell, rcell = (0.0, 0.0) if edges is None else (left[j : j + 1], right[j : j + 1])
        west = jnp.where(at == 0, lcell, pltpu.roll(act, 1, 0))
        east = jnp.where(at == s.cols - 1, rcell, pltpu.roll(act, s.cols - 1, 0))
        if i in (0, s.rows + 1):
            inside = top_in if i == 0 else bottom_in
            west, act, east = west * inside, act * inside, east * inside
        taps[0, i] = west.astype(BF16)
        taps[1, i] = act.astype(BF16)
        taps[2, i] = east.astype(BF16)


def spatial_dot(s, taps, weight, bias, rows):
    size = s.rows // DOTS
    done = []
    for r in range(0, rows, size):
        step = min(size, rows - r)
        lhs = jnp.concatenate(
            [
                taps[dx, r + dy : r + dy + step].reshape(step * s.cols, s.chans)
                for dy in range(3)
                for dx in range(3)
            ],
            axis=1,
        )
        done.append((jnp.dot(lhs, weight[...], preferred_element_type=F32) + bias[...]).astype(BF16))
    return jnp.concatenate(done, axis=0)


def temporal_dot(s, frames, weight, bias):
    lhs = jnp.concatenate(frames, axis=1)
    out = jnp.dot(lhs, weight[...], preferred_element_type=F32) + bias[...]
    return out.astype(BF16).reshape(s.rows, s.cols, s.chans)


def put(s, ref, enc, sem, f, quarters=range(QUARTERS)):
    step = s.rows // QUARTERS
    return [
        pltpu.make_async_copy(
            ref.at[f, pl.ds(k * step, step)], enc.at[f, pl.ds(k * step, step)], sem.at[f, k]
        )
        for k in quarters
    ]


def start(copies):
    for c in copies:
        c.start()


def wait(copies):
    for c in copies:
        c.wait()


def own_kernel(s, video, halo, aff, nbias, sw, sb, tw, tb, *refs):
    cols = refs[: s.ncol]
    enc, base, taps, spatial, out, sem = refs[s.ncol + 1 :]
    shift = nbias[...] * 0.5
    first = lax.axis_index("ta") == 0

    def frame(f, _):
        def raw_row(i):
            if i == 0:
                return halo[f, 0]
            if i == s.rows + 1:
                return halo[f, 1]
            return video[f, i - 1]

        edges = [c[pl.ds(f * s.colrow, s.colrow)] for c in cols]
        fill_taps(s, taps, raw_row, edges, aff[pl.ds(f, 1)], aff[pl.ds(s.frames + f, 1)], shift)
        spatial[f] = spatial_dot(s, taps, sw, sb, s.rows)
        return _

    lax.fori_loop(0, s.frames, frame, 0)

    def encode(f):
        out[f] = temporal_dot(s, [spatial[max(f - k, 0)] for k in range(3)], tw, tb)
        start(put(s, out, enc, sem, f))

    for f in range(PREV, s.frames):
        encode(f)

    @pl.when(first)
    def _():
        for f in range(PREV):
            encode(f)
        for f in range(PREV):
            wait(put(s, out, enc, sem, f))

    @pl.when(jnp.logical_not(first))
    def _():
        for f in range(PREV):
            lhs = jnp.concatenate([spatial[f - k] for k in range(f + 1)], axis=1)
            weight = tw[: (f + 1) * s.chans]
            base[f] = jnp.dot(lhs, weight, preferred_element_type=F32) + tb[...]

    for f in range(PREV, s.frames):
        wait(put(s, out, enc, sem, f))


def inner_kernel(s, early, late, moved, nbias, sw, sb, base, taps, spatial):
    shift = nbias[...] * 0.5

    @pl.when(lax.axis_index("ta") > 0)
    def _():
        for p in range(PREV):

            def raw_row(i):
                if i == 0 or i == s.rows + 1:
                    return None
                r = p * s.rows + i - 1
                if r >= s.early + s.late:
                    return None
                return early[r] if r < s.early else late[r - s.early]

            fill_taps(s, taps.at[p], raw_row, None, moved[p : p + 1], moved[PREV + p : PREV + p + 1], shift)
            rows = s.rows if p < PREV - 1 else s.rows - s.tail - 1
            spatial[p, : rows * s.cols] = spatial_dot(s, taps.at[p], sw, sb, rows)


def outer_kernel(s, got, moved, taps, spatial, nbias, sw, sb, tw, base, _, enc, more, grid, out, sem):
    ha, wa = lax.axis_index("ha"), lax.axis_index("wa")
    shift = nbias[...] * 0.5
    inside = [jnp.where(ha > 0, 1.0, 0.0).astype(F32), jnp.where(ha < s.ha - 1, 1.0, 0.0).astype(F32)]
    at = lax.broadcasted_iota(jnp.int32, (s.cols, s.chans), 0)
    down = lax.broadcasted_iota(jnp.int32, (s.colrow, s.chans), 0)
    if s.ncol == 1:
        sides = [wa == 0]
        present = [jnp.ones((), F32)]
    else:
        sides = [False, True]
        present = [jnp.where(wa > 0, 1.0, 0.0).astype(F32), jnp.where(wa < s.wa - 1, 1.0, 0.0).astype(F32)]

    @pl.when(lax.axis_index("ta") > 0)
    def _():
        lhs = []
        start_row = s.rows - s.tail - 1
        end = PREV - 1

        def tap(p, dx, i):
            return more[dx, i - start_row] if p == end and i >= start_row else taps[p, dx, i]

        def shifted(act):
            west = jnp.where(at == 0, 0.0, pltpu.roll(act, 1, 0))
            east = jnp.where(at == s.cols - 1, 0.0, pltpu.roll(act, s.cols - 1, 0))
            return [x.astype(BF16) for x in (west, act, east)]

        for dx in range(3):
            more[dx, :2] = taps[end, dx, start_row : start_row + 2]
        for i in range(s.tail):
            o = PREV * s.strip + i * s.cols
            raw = got[o : o + s.cols].astype(F32)
            act = activation(raw, moved[end : end + 1], moved[PREV + end : PREV + end + 1], shift)
            for dx, x in enumerate(shifted(act)):
                more[dx, 2 + i] = x
        for p in range(PREV):
            mean, scale = moved[p : p + 1], moved[PREV + p : PREV + p + 1]
            o = p * s.strip
            acts = []
            for k in range(2):
                raw = got[o + k * s.cols : o + (k + 1) * s.cols].astype(F32)
                act = activation(raw, mean, scale, shift) * inside[k]
                acts.append(act)
            top, bottom = shifted(acts[0]), shifted(acts[1])
            lhs.append(
                jnp.concatenate(top + [tap(p, dx, i) for i in (1, 2) for dx in range(3)], axis=1)
            )
            n = s.rows
            lhs.append(
                jnp.concatenate([tap(p, dx, i) for i in (n - 1, n) for dx in range(3)] + bottom, axis=1)
            )
            for k in range(s.ncol):
                o2 = o + 2 * s.cols + k * s.colrow
                cell = activation(got[o2 : o2 + s.colrow].astype(F32), mean, scale, shift) * present[k]
                upper = cell[n : n + 1] * inside[0]
                lower = cell[n + 1 : n + 2] * inside[1]
                right = sides[k]

                def column(d):
                    rows = []
                    for i in range(1, n + 1):
                        tile = tap(p, 1, i).astype(F32)
                        if d == 0:
                            rows.append(jnp.where(right, tile[s.cols - 1 :], tile[:1]))
                        else:
                            rows.append(jnp.where(right, tile[s.cols - 2 : s.cols - 1], tile[1:2]))
                    fill = jnp.zeros((s.colrow - n, s.chans), F32)
                    return jnp.concatenate(rows + [fill], axis=0)

                here, inner = column(0), column(1)
                far = jnp.where(down < n, cell, 0.0)
                ends = [
                    tuple(jnp.where(right, a[s.cols - 1 :], a[:1]) for a in acts),
                    tuple(jnp.where(right, a[s.cols - 2 : s.cols - 1], a[1:2]) for a in acts),
                    (upper, lower),
                ]
                steps = []
                for dy in range(3):
                    group = []
                    for x, (first, final) in zip((here, inner, far), ends):
                        if dy == 0:
                            x = jnp.where(down == 0, first, pltpu.roll(x, 1, 0))
                        elif dy == 2:
                            x = jnp.where(down == n - 1, final, pltpu.roll(x, s.colrow - 1, 0))
                        group.append(x)
                    mid, inn, out_ = group
                    steps += [jnp.where(right, inn, out_), mid, jnp.where(right, out_, inn)]
                lhs.append(jnp.concatenate([x.astype(BF16) for x in steps], axis=1))
        fresh = s.tail * s.cols
        lhs.append(
            jnp.concatenate(
                [
                    more[dx, dy : dy + s.tail].reshape(fresh, s.chans)
                    for dy in range(3)
                    for dx in range(3)
                ],
                axis=1,
            )
        )
        border = jnp.dot(jnp.concatenate(lhs, axis=0), sw[...], preferred_element_type=F32) + sb[...]
        size = 2 * s.cols + s.ncol * s.colrow
        tile = 16
        cells = lax.broadcasted_iota(jnp.int32, (tile, s.chans), 0)
        for p in range(PREV):
            o = p * size
            n = (s.rows - 1) * s.cols
            grid[p, : s.cols] = border[o : o + s.cols].astype(BF16)
            m = n if p < end else start_row * s.cols
            grid[p, s.cols : m] = spatial[p, s.cols : m]
            if p == end:
                grid[p, m : m + fresh] = border[PREV * size : PREV * size + fresh].astype(BF16)
            grid[p, n:] = border[o + s.cols : o + 2 * s.cols].astype(BF16)
            for k in range(s.ncol):
                place = jnp.where(sides[k], tile - 1, 0)
                mask = cells == place
                for h in range(s.rows):
                    o2 = o + 2 * s.cols + k * s.colrow + h
                    at0 = h * s.cols + jnp.where(sides[k], s.cols - tile, 0)
                    part = pl.ds(pl.multiple_of(at0, tile), tile)
                    row = jnp.where(mask, border[o2 : o2 + 1], grid[p, part].astype(F32))
                    grid[p, part] = row.astype(BF16)
        half = s.rows * s.cols // 2
        for f in range(PREV):
            for k in range(2):
                part = slice(k * half, (k + 1) * half)
                lhs = jnp.concatenate([grid[q, part] for q in range(PREV - 1, f - 1, -1)], axis=1)
                y = jnp.dot(lhs, tw[(f + 1) * s.chans :], preferred_element_type=F32) + base[f, part]
                block = (s.rows // 2, s.cols, s.chans)
                out[f, k * block[0] : (k + 1) * block[0]] = y.astype(BF16).reshape(block)
                start(put(s, out, enc, sem, f, range(k * QUARTERS // 2, (k + 1) * QUARTERS // 2)))
        for f in range(PREV):
            wait(put(s, out, enc, sem, f))


def mates(n, phase):
    if phase == 0:
        return [(i, i ^ 1) for i in range(n)]
    return [(i, (i - 1) % n if i % 2 == 0 else (i + 1) % n) for i in range(n)]


def local(video, norm_gain, norm_bias, spatial_weight, spatial_bias, temporal_weight, temporal_bias):
    nta, nha, nwa = (lax.axis_size(a) for a in ("ta", "ha", "wa"))
    s = Sizes(video, nha, nwa)
    c = s.chans
    sd = jax.ShapeDtypeStruct
    ring = [(i, (i + 1) % nta) for i in range(nta)]
    if nwa == 2:
        sides = [[(0, 1), (1, 0)]]
    else:
        sides = [[(i, (i + d) % nwa) for i in range(nwa)] for d in (1, -1)]
    sw = spatial_weight.reshape(9 * c, c)
    tw = temporal_weight.reshape(3 * c, c)
    gain, nbias, sb, tb = (v.reshape(1, c) for v in (norm_gain, norm_bias, spatial_bias, temporal_bias))

    one = video.shape[1:]
    late_shape = sd((s.late,) + one[1:], BF16)
    early, late = call(
        functools.partial(head_kernel, s),
        [sd((s.early,) + one[1:], BF16), late_shape],
        name="head",
        in_specs=[VMEM],
    )(video)
    rowpay = sd((s.frames * s.cols + s.stats, c), BF16)
    stat = sd((2 * s.frames, c), F32)
    colout = [sd((s.frames * s.colrow, c), BF16)] * s.ncol
    riding = s.stats if s.fused else 0
    pay, stats, *cols = call(
        functools.partial(local_kernel, s),
        [rowpay, stat] + colout,
        name="local",
        in_specs=[VMEM, ANY],
    )(video, early)
    early = lax.ppermute(early, "ta", ring)
    got1 = lax.ppermute(pay, "ha", mates(nha, 0))
    late, payy, part, *pays = call(
        functools.partial(pair_kernel, s),
        [late_shape, rowpay, stat]
        + [sd((s.frames * s.colrow + riding, c), BF16)] * s.ncol
        + [sd((s.corner + riding, c), BF16)] * s.ncol,
        out_specs=[ANY] + [VMEM] * (2 + 2 * s.ncol),
        name="pair",
        in_specs=[VMEM] * (3 + s.ncol) + [ANY],
        input_output_aliases={3 + s.ncol: 0},
    )(video, stats, got1, *cols, late)
    outer = mates(nha, 1)
    diagonal = [[(h * nwa + w, g * nwa + v) for h, g in outer for w, v in p] for p in sides]
    goty = lax.ppermute(payy, "ha", outer)
    gotx = [lax.ppermute(x, "wa", p) for x, p in zip(pays[: s.ncol], sides)]
    gotd = [lax.ppermute(x, ("ha", "wa"), p) for x, p in zip(pays[s.ncol :], diagonal)]
    late = lax.ppermute(late, "ta", ring[:-1])
    if not s.fused:
        every = lax.all_gather(stats, ("ha", "wa"))
        part = merge(float(s.rows * s.cols), [every[i] for i in range(nha * nwa)])
    aff, moved = call(
        functools.partial(group_kernel, s),
        [stat, sd((2 * PREV, c), F32)],
        name="group",
        in_specs=[VMEM] * (3 + 2 * s.ncol),
    )(part, gain, goty, *gotx, *gotd)
    moved = lax.ppermute(moved, "ta", ring)
    hand, halo, *cols = call(
        functools.partial(edge_kernel, s),
        [sd((PREV * s.strip + s.tail * s.cols, c), BF16), sd((s.frames, 2, s.cols, c), BF16)] + colout,
        name="edge",
        in_specs=[VMEM] * (4 + 2 * s.ncol),
    )(aff, video, got1, goty, *gotx, *gotd)
    got = lax.ppermute(hand, "ta", ring)
    frame = (s.rows * s.cols, c)
    taps = (3, s.rows + 2, s.cols, c)
    enc, base = call(
        functools.partial(own_kernel, s),
        [sd(video.shape, BF16), sd((PREV,) + frame, F32)],
        out_specs=[ANY, VMEM],
        scratch=[
            pltpu.VMEM(taps, BF16),
            pltpu.VMEM((s.frames,) + frame, BF16),
            pltpu.VMEM((s.frames,) + one, BF16),
            pltpu.SemaphoreType.DMA((s.frames, QUARTERS)),
        ],
        flops=2 * s.rows * s.cols * c * c * (9 * s.frames + 3 * (s.frames - PREV)),
        name="own",
        in_specs=[VMEM] * (8 + s.ncol) + [ANY],
    )(video, halo, aff, nbias, sw, sb, tw, tb, *cols, early)
    grid, inner = call(
        functools.partial(inner_kernel, s),
        [sd((PREV,) + taps, BF16), sd((PREV,) + frame, BF16)],
        name="inner",
        in_specs=[VMEM] * 6 + [ANY],
    )(early, late, moved, nbias, sw, sb, base)
    (enc,) = call(
        functools.partial(outer_kernel, s),
        [sd(video.shape, BF16)],
        out_specs=[ANY],
        scratch=[
            pltpu.VMEM((3, s.tail + 2) + one[1:], BF16),
            pltpu.VMEM((PREV,) + frame, BF16),
            pltpu.VMEM((PREV,) + one, BF16),
            pltpu.SemaphoreType.DMA((PREV, QUARTERS)),
        ],
        name="outer",
        in_specs=[VMEM] * 9 + [ANY],
        input_output_aliases={9: 0},
    )(got, moved, grid, inner, nbias, sw, sb, tw, base, enc)
    return enc


def solution(mesh):
    placed = (P("ta", "ha", "wa", None), P(), P(), P(), P(), P(), P())
    return jax.shard_map(
        local, mesh=mesh, in_specs=placed, out_specs=P("ta", "ha", "wa", None), check_vma=False
    )
```

```python
import functools

import jax
import jax.numpy as jnp
from jax import lax
from jax.experimental import pallas as pl
from jax.experimental.pallas import tpu as pltpu
from jax.sharding import PartitionSpec as P

G = 32
EPS = 1e-06
QUARTERS = 4
DOTS = 6
PREV = 2
F32 = jnp.float32
BF16 = jnp.bfloat16
VMEM = pl.BlockSpec(memory_space=pltpu.VMEM)
ANY = pl.BlockSpec(memory_space=pl.ANY)


def call(kernel, outs, out_specs=None, scratch=(), flops=1024, name=None, **kw):
    return pl.pallas_call(
        kernel,
        out_shape=outs,
        out_specs=out_specs or [VMEM] * len(outs),
        scratch_shapes=list(scratch),
        compiler_params=pltpu.CompilerParams(vmem_limit_bytes=24 << 20),
        cost_estimate=pl.CostEstimate(flops=flops, bytes_accessed=1024, transcendentals=0),
        name=name,
        **kw,
    )


def pad_to(n, k):
    return (n + k - 1) // k * k


def split3(x):
    hi = x.astype(BF16)
    rest = x - hi.astype(F32)
    mid = rest.astype(BF16)
    low = (rest - mid.astype(F32)).astype(BF16)
    return hi, mid, low


def as_terms(x, rows):
    parts = jnp.concatenate([t.astype(F32) for t in split3(x)], axis=0)
    fill = rows - parts.shape[0]
    if fill:
        parts = jnp.concatenate([parts, jnp.zeros((fill, x.shape[1]), F32)], axis=0)
    return parts.astype(BF16)


def from_terms(t, rows):
    t = t.astype(F32)
    return t[:rows] + t[rows : 2 * rows] + t[2 * rows : 3 * rows]


class Sizes:
    def __init__(self, video, ha, wa):
        self.frames, self.rows, self.cols, self.chans = video.shape
        self.ha, self.wa = ha, wa
        self.ncol = 1 if wa == 2 else 2
        self.fused = ha == 4 and wa == 2
        self.colrow = pad_to(self.rows + 2, 16)
        self.strip = 2 * self.cols + self.ncol * self.colrow
        self.stats = pad_to(3 * 2 * self.frames, 16)
        self.early = (PREV - 1) * self.rows + self.rows // 12
        self.tail = self.rows // 4 + 1
        self.late = PREV * self.rows - self.early - self.tail
        self.corner = pad_to(self.frames, 16)


def head_kernel(s, video, early, late):
    flat = (PREV * s.rows, s.cols, s.chans)
    sent = video[s.frames - PREV :].reshape(flat)
    early[...] = sent[: s.early]
    late[...] = sent[s.early : s.early + s.late]


def local_kernel(s, video, early, pay, stats, *cols):
    ha, wa = lax.axis_index("ha"), lax.axis_index("wa")
    even = lax.rem(ha, 2) == 0
    means, squares = [], []
    for f in range(s.frames):
        total = jnp.zeros((s.cols, s.chans), F32)
        for r in range(s.rows):
            total = total + video[f, r].astype(F32)
        mean = jnp.sum(total, axis=0, keepdims=True) * (1.0 / (s.rows * s.cols))
        spread = jnp.zeros((s.cols, s.chans), F32)
        left, right = [], []
        for r in range(s.rows):
            x = video[f, r].astype(F32)
            left.append(x[:1])
            right.append(x[s.cols - 1 :])
            x = x - mean
            spread = spread + x * x
        means.append(mean)
        squares.append(jnp.sum(spread, axis=0, keepdims=True))
        fill = [jnp.zeros((s.colrow - s.rows, s.chans), F32)]
        left = jnp.concatenate(left + fill, axis=0)
        right = jnp.concatenate(right + fill, axis=0)
        if s.ncol == 1:
            edges = [jnp.where(wa == 0, right, left)]
        else:
            edges = [right, left]
        for ref, e in zip(cols, edges):
            ref[f * s.colrow : (f + 1) * s.colrow] = e.astype(BF16)
        top = video[f, 0].astype(F32)
        bottom = video[f, s.rows - 1].astype(F32)
        pay[f * s.cols : (f + 1) * s.cols] = jnp.where(even, bottom, top).astype(BF16)
    stat = jnp.concatenate(means + squares, axis=0)
    stats[...] = stat
    o = s.frames * s.cols
    pay[o : o + s.stats] = as_terms(stat, s.stats)


def merge(n, parts):
    half = parts[0].shape[0] // 2
    mean = sum(p[:half] for p in parts) * (1.0 / len(parts))
    square = sum(p[half:] + n * (p[:half] - mean) * (p[:half] - mean) for p in parts)
    return jnp.concatenate([mean, square], axis=0)


def pair_kernel(s, video, stats, got, *refs):
    cols, refs = refs[: s.ncol], refs[s.ncol + 1 :]
    _, payy, part = refs[:3]
    payx, payd = refs[3 : 3 + s.ncol], refs[3 + s.ncol :]
    ha, wa = lax.axis_index("ha"), lax.axis_index("wa")
    even = lax.rem(ha, 2) == 0
    o = s.frames * s.cols
    stat = merge(float(s.rows * s.cols), [stats[...], from_terms(got[o : o + s.stats], 2 * s.frames)])
    part[...] = stat
    terms = as_terms(stat, s.stats)
    at = lax.broadcasted_iota(jnp.int32, (s.colrow, s.chans), 0)
    cells = [[] for _ in range(s.ncol)]
    for f in range(s.frames):
        top = video[f, 0].astype(F32)
        bottom = video[f, s.rows - 1].astype(F32)
        outer = jnp.where(even, top, bottom)
        payy[f * s.cols : (f + 1) * s.cols] = outer.astype(BF16)
        inner = got[f * s.cols : (f + 1) * s.cols].astype(F32)
        for k in range(s.ncol):
            right = wa == 0 if s.ncol == 1 else k == 0
            cell = jnp.where(right, inner[s.cols - 1 :], inner[:1])
            cells[k].append(jnp.where(right, outer[s.cols - 1 :], outer[:1]))
            edge = cols[k][f * s.colrow : (f + 1) * s.colrow].astype(F32)
            edge = jnp.where(at >= s.rows, cell, edge)
            payx[k][f * s.colrow : (f + 1) * s.colrow] = edge.astype(BF16)
    for k in range(s.ncol):
        fill = s.corner - s.frames
        rows = cells[k] + ([jnp.zeros((fill, s.chans), F32)] if fill else [])
        payd[k][: s.corner] = jnp.concatenate(rows, axis=0).astype(BF16)
    payy[o : o + s.stats] = terms
    if s.fused:
        o = s.frames * s.colrow
        payx[0][o : o + s.stats] = terms
        payd[0][s.corner : s.corner + s.stats] = terms


def group_kernel(s, part, gain, goty, *refs):
    gotx, gotd = refs[: s.ncol], refs[s.ncol : 2 * s.ncol]
    aff, moved = refs[2 * s.ncol :]
    rows = 2 * s.frames
    count = float(s.rows * s.cols * s.ha * s.wa)
    stat = part[...]
    if s.fused:
        offsets = ((goty, s.frames * s.cols), (gotx[0], s.frames * s.colrow), (gotd[0], s.corner))
        stat = merge(count / 4, [stat] + [from_terms(ref[o : o + s.stats], rows) for ref, o in offsets])
    width = s.chans // G
    a = lax.broadcasted_iota(jnp.int32, (s.chans, s.chans), 0) // width
    b = lax.broadcasted_iota(jnp.int32, (s.chans, s.chans), 1) // width
    group = jnp.where(a == b, 1.0, 0.0).astype(BF16)

    def tot(x):
        terms = jnp.concatenate(split3(x), axis=0)
        y = jnp.dot(terms, group, preferred_element_type=F32)
        n = s.frames
        return y[:n] + y[n : 2 * n] + y[2 * n :]

    m, q = stat[: s.frames], stat[s.frames :]
    mean = tot(m) * (1.0 / width)
    var = tot(q + count * (m - mean) * (m - mean)) * (1.0 / (count * width))
    scale = lax.rsqrt(var + EPS) * gain[...] * 0.5
    aff[: s.frames] = mean
    aff[s.frames :] = scale
    first = s.frames - PREV
    moved[:PREV] = mean[first:]
    moved[PREV:] = scale[first:]


def edge_kernel(s, aff, video, got, goty, *refs):
    gotx, gotd = refs[: s.ncol], refs[s.ncol : 2 * s.ncol]
    hand, halo, *cols = refs[2 * s.ncol :]
    even = lax.rem(lax.axis_index("ha"), 2) == 0
    first = s.frames - PREV
    o = PREV * s.strip
    rest = video[s.frames - 1, s.rows - s.tail :]
    hand[o : o + s.tail * s.cols] = rest.reshape(s.tail * s.cols, s.chans)
    at = lax.broadcasted_iota(jnp.int32, (s.colrow, s.chans), 0)
    for f in range(s.frames):
        p = (f - first) * s.strip
        one = got[f * s.cols : (f + 1) * s.cols].astype(F32)
        two = goty[f * s.cols : (f + 1) * s.cols].astype(F32)
        top = jnp.where(even, two, one).astype(BF16)
        bottom = jnp.where(even, one, two).astype(BF16)
        halo[f, 0] = top
        halo[f, 1] = bottom
        if f >= first:
            hand[p : p + s.cols] = top
            hand[p + s.cols : p + 2 * s.cols] = bottom
        for k in range(s.ncol):
            cell = gotd[k][: s.corner].astype(F32)[f : f + 1]
            edge = gotx[k][f * s.colrow : (f + 1) * s.colrow].astype(F32)
            outer = jnp.where(even, s.rows, s.rows + 1)
            edge = jnp.where(at == outer, cell, edge).astype(BF16)
            cols[k][f * s.colrow : (f + 1) * s.colrow] = edge
            if f >= first:
                o = p + 2 * s.cols + k * s.colrow
                hand[o : o + s.colrow] = edge


def activation(x, mean, scale, shift):
    h = (x - mean) * scale + shift
    return h + h * jnp.tanh(h)


def fill_taps(s, taps, raw_row, edges, mean, scale, shift):
    ha, wa = lax.axis_index("ha"), lax.axis_index("wa")
    top_in = jnp.where(ha > 0, 1.0, 0.0).astype(F32)
    bottom_in = jnp.where(ha < s.ha - 1, 1.0, 0.0).astype(F32)
    left_in = jnp.where(wa > 0, 1.0, 0.0).astype(F32)
    right_in = jnp.where(wa < s.wa - 1, 1.0, 0.0).astype(F32)
    if edges is not None:
        acts = [activation(e.astype(F32), mean, scale, shift) for e in edges]
        left, right = acts[0] * left_in, acts[-1] * right_in
    at = lax.broadcasted_iota(jnp.int32, (s.cols, s.chans), 0)
    for i in range(s.rows + 2):
        raw = raw_row(i)
        if raw is None:
            for dx in range(3):
                taps[dx, i] = jnp.zeros((s.cols, s.chans), BF16)
            continue
        act = activation(raw.astype(F32), mean, scale, shift)
        j = s.rows if i == 0 else s.rows + 1 if i == s.rows + 1 else i - 1
        lcell, rcell = (0.0, 0.0) if edges is None else (left[j : j + 1], right[j : j + 1])
        west = jnp.where(at == 0, lcell, pltpu.roll(act, 1, 0))
        east = jnp.where(at == s.cols - 1, rcell, pltpu.roll(act, s.cols - 1, 0))
        if i in (0, s.rows + 1):
            inside = top_in if i == 0 else bottom_in
            west, act, east = west * inside, act * inside, east * inside
        taps[0, i] = west.astype(BF16)
        taps[1, i] = act.astype(BF16)
        taps[2, i] = east.astype(BF16)


def spatial_dot(s, taps, weight, bias, rows):
    size = s.rows // DOTS
    done = []
    for r in range(0, rows, size):
        step = min(size, rows - r)
        lhs = jnp.concatenate(
            [
                taps[dx, r + dy : r + dy + step].reshape(step * s.cols, s.chans)
                for dy in range(3)
                for dx in range(3)
            ],
            axis=1,
        )
        done.append((jnp.dot(lhs, weight[...], preferred_element_type=F32) + bias[...]).astype(BF16))
    return jnp.concatenate(done, axis=0)


def temporal_dot(s, frames, weight, bias):
    lhs = jnp.concatenate(frames, axis=1)
    out = jnp.dot(lhs, weight[...], preferred_element_type=F32) + bias[...]
    return out.astype(BF16).reshape(s.rows, s.cols, s.chans)


def put(s, ref, enc, sem, f, quarters=range(QUARTERS)):
    step = s.rows // QUARTERS
    return [
        pltpu.make_async_copy(
            ref.at[f, pl.ds(k * step, step)], enc.at[f, pl.ds(k * step, step)], sem.at[f, k]
        )
        for k in quarters
    ]


def start(copies):
    for c in copies:
        c.start()


def wait(copies):
    for c in copies:
        c.wait()


def own_kernel(s, video, halo, aff, nbias, sw, sb, tw, tb, *refs):
    cols = refs[: s.ncol]
    enc, base, taps, spatial, out, sem = refs[s.ncol + 1 :]
    shift = nbias[...] * 0.5
    first = lax.axis_index("ta") == 0

    def frame(f, _):
        def raw_row(i):
            if i == 0:
                return halo[f, 0]
            if i == s.rows + 1:
                return halo[f, 1]
            return video[f, i - 1]

        edges = [c[pl.ds(f * s.colrow, s.colrow)] for c in cols]
        fill_taps(s, taps, raw_row, edges, aff[pl.ds(f, 1)], aff[pl.ds(s.frames + f, 1)], shift)
        spatial[f] = spatial_dot(s, taps, sw, sb, s.rows)
        return _

    lax.fori_loop(0, s.frames, frame, 0)

    def encode(f):
        out[f] = temporal_dot(s, [spatial[max(f - k, 0)] for k in range(3)], tw, tb)
        start(put(s, out, enc, sem, f))

    for f in range(PREV, s.frames):
        encode(f)

    @pl.when(first)
    def _():
        for f in range(PREV):
            encode(f)
        for f in range(PREV):
            wait(put(s, out, enc, sem, f))

    @pl.when(jnp.logical_not(first))
    def _():
        for f in range(PREV):
            lhs = jnp.concatenate([spatial[f - k] for k in range(f + 1)], axis=1)
            weight = tw[: (f + 1) * s.chans]
            base[f] = jnp.dot(lhs, weight, preferred_element_type=F32) + tb[...]

    for f in range(PREV, s.frames):
        wait(put(s, out, enc, sem, f))


def taps_back(s, grids, f, tw):
    lhs = jnp.concatenate([grids[q] for q in range(PREV - 1, f - 1, -1)], axis=1)
    return jnp.dot(lhs, tw[(f + 1) * s.chans :], preferred_element_type=F32)


def inner_kernel(s, early, late, moved, nbias, sw, sb, tw, base, taps, spatial, pre, rim):
    shift = nbias[...] * 0.5

    @pl.when(lax.axis_index("ta") > 0)
    def _():
        for p in range(PREV):

            def raw_row(i):
                if i == 0 or i == s.rows + 1:
                    return None
                r = p * s.rows + i - 1
                if r >= s.early + s.late:
                    return None
                return early[r] if r < s.early else late[r - s.early]

            fill_taps(s, taps.at[p], raw_row, None, moved[p : p + 1], moved[PREV + p : PREV + p + 1], shift)
            rows = s.rows if p < PREV - 1 else s.rows - s.tail - 1
            spatial[p, : rows * s.cols] = spatial_dot(s, taps.at[p], sw, sb, rows)
        part = slice(s.cols, (s.rows - s.tail - 1) * s.cols)
        for f in range(PREV):
            y = taps_back(s, [spatial[q, part] for q in range(PREV)], f, tw) + base[f, part]
            pre[f, 1 : s.rows - s.tail - 1] = y.astype(BF16).reshape(-1, s.cols, s.chans)
            for k in range(s.ncol):
                right = lax.axis_index("wa") == 0 if s.ncol == 1 else k == 1
                cells = []
                for h in range(s.rows):
                    o = h * s.cols
                    last = base[f, o + s.cols - 8 : o + s.cols]
                    cells.append(jnp.where(right, last[7:], base[f, o : o + 8][:1]))
                cells.append(jnp.zeros((s.colrow - s.rows, s.chans), F32))
                rim[f, k] = jnp.concatenate(cells, axis=0)


def outer_kernel(s, got, moved, taps, spatial, nbias, sw, sb, tw, base, pre, rim, _, enc, more, grid, out, sem):
    ha, wa = lax.axis_index("ha"), lax.axis_index("wa")
    shift = nbias[...] * 0.5
    inside = [jnp.where(ha > 0, 1.0, 0.0).astype(F32), jnp.where(ha < s.ha - 1, 1.0, 0.0).astype(F32)]
    at = lax.broadcasted_iota(jnp.int32, (s.cols, s.chans), 0)
    down = lax.broadcasted_iota(jnp.int32, (s.colrow, s.chans), 0)
    if s.ncol == 1:
        sides = [wa == 0]
        present = [jnp.ones((), F32)]
    else:
        sides = [False, True]
        present = [jnp.where(wa > 0, 1.0, 0.0).astype(F32), jnp.where(wa < s.wa - 1, 1.0, 0.0).astype(F32)]

    @pl.when(lax.axis_index("ta") > 0)
    def _():
        lhs = []
        start_row = s.rows - s.tail - 1
        end = PREV - 1

        def tap(p, dx, i):
            return more[dx, i - start_row] if p == end and i >= start_row else taps[p, dx, i]

        def shifted(act):
            west = jnp.where(at == 0, 0.0, pltpu.roll(act, 1, 0))
            east = jnp.where(at == s.cols - 1, 0.0, pltpu.roll(act, s.cols - 1, 0))
            return [x.astype(BF16) for x in (west, act, east)]

        for dx in range(3):
            more[dx, :2] = taps[end, dx, start_row : start_row + 2]
        for i in range(s.tail):
            o = PREV * s.strip + i * s.cols
            raw = got[o : o + s.cols].astype(F32)
            act = activation(raw, moved[end : end + 1], moved[PREV + end : PREV + end + 1], shift)
            for dx, x in enumerate(shifted(act)):
                more[dx, 2 + i] = x
        for p in range(PREV):
            mean, scale = moved[p : p + 1], moved[PREV + p : PREV + p + 1]
            o = p * s.strip
            acts = []
            for k in range(2):
                raw = got[o + k * s.cols : o + (k + 1) * s.cols].astype(F32)
                act = activation(raw, mean, scale, shift) * inside[k]
                acts.append(act)
            top, bottom = shifted(acts[0]), shifted(acts[1])
            lhs.append(
                jnp.concatenate(top + [tap(p, dx, i) for i in (1, 2) for dx in range(3)], axis=1)
            )
            n = s.rows
            lhs.append(
                jnp.concatenate([tap(p, dx, i) for i in (n - 1, n) for dx in range(3)] + bottom, axis=1)
            )
            for k in range(s.ncol):
                o2 = o + 2 * s.cols + k * s.colrow
                cell = activation(got[o2 : o2 + s.colrow].astype(F32), mean, scale, shift) * present[k]
                upper = cell[n : n + 1] * inside[0]
                lower = cell[n + 1 : n + 2] * inside[1]
                right = sides[k]

                def column(d):
                    rows = []
                    for i in range(1, n + 1):
                        tile = tap(p, 1, i).astype(F32)
                        if d == 0:
                            rows.append(jnp.where(right, tile[s.cols - 1 :], tile[:1]))
                        else:
                            rows.append(jnp.where(right, tile[s.cols - 2 : s.cols - 1], tile[1:2]))
                    fill = jnp.zeros((s.colrow - n, s.chans), F32)
                    return jnp.concatenate(rows + [fill], axis=0)

                here, inner = column(0), column(1)
                far = jnp.where(down < n, cell, 0.0)
                ends = [
                    tuple(jnp.where(right, a[s.cols - 1 :], a[:1]) for a in acts),
                    tuple(jnp.where(right, a[s.cols - 2 : s.cols - 1], a[1:2]) for a in acts),
                    (upper, lower),
                ]
                steps = []
                for dy in range(3):
                    group = []
                    for x, (first, final) in zip((here, inner, far), ends):
                        if dy == 0:
                            x = jnp.where(down == 0, first, pltpu.roll(x, 1, 0))
                        elif dy == 2:
                            x = jnp.where(down == n - 1, final, pltpu.roll(x, s.colrow - 1, 0))
                        group.append(x)
                    mid, inn, out_ = group
                    steps += [jnp.where(right, inn, out_), mid, jnp.where(right, out_, inn)]
                lhs.append(jnp.concatenate([x.astype(BF16) for x in steps], axis=1))
        fresh = s.tail * s.cols
        lhs.append(
            jnp.concatenate(
                [
                    more[dx, dy : dy + s.tail].reshape(fresh, s.chans)
                    for dy in range(3)
                    for dx in range(3)
                ],
                axis=1,
            )
        )
        border = jnp.dot(jnp.concatenate(lhs, axis=0), sw[...], preferred_element_type=F32) + sb[...]
        size = 2 * s.cols + s.ncol * s.colrow
        tile = 16
        cells = lax.broadcasted_iota(jnp.int32, (tile, s.chans), 0)
        masks = [cells == jnp.where(right, tile - 1, 0) for right in sides]
        starts = [jnp.where(right, s.cols - tile, 0) for right in sides]
        first, body = s.cols, (s.tail + 1) * s.cols
        for p in range(PREV):
            o = p * size
            grid[p, :first] = border[o : o + first].astype(BF16)
            if p < end:
                rest = spatial[p, start_row * s.cols : (s.rows - 1) * s.cols]
            else:
                rest = border[PREV * size : PREV * size + fresh].astype(BF16)
            grid[p, first : body] = rest
            grid[p, body : body + s.cols] = border[o + s.cols : o + 2 * s.cols].astype(BF16)
            for k in range(s.ncol):
                o2 = o + 2 * s.cols + k * s.colrow
                for g in range(s.tail + 2):
                    h = 0 if g == 0 else start_row + g - 1
                    at0 = pl.ds(pl.multiple_of(g * s.cols + starts[k], tile), tile)
                    row = jnp.where(masks[k], border[o2 + h : o2 + h + 1], grid[p, at0].astype(F32))
                    grid[p, at0] = row.astype(BF16)
                o3 = body + s.cols + k * s.colrow
                grid[p, o3 : o3 + s.colrow] = border[o2 : o2 + s.colrow].astype(BF16)
        for f in range(PREV):
            own = [base[f, :first], base[f, start_row * s.cols :]] + [rim[f, k] for k in range(s.ncol)]
            y = taps_back(s, [grid[q] for q in range(PREV)], f, tw) + jnp.concatenate(own, axis=0)
            out[f, 0] = y[:first].astype(BF16)
            out[f, start_row:] = y[first : body + s.cols].astype(BF16).reshape(-1, s.cols, s.chans)
            out[f, 1:start_row] = pre[f, 1:start_row]
            for k in range(s.ncol):
                o3 = body + s.cols + k * s.colrow
                at0 = pl.ds(pl.multiple_of(starts[k], tile), tile)
                for h in range(1, start_row):
                    row = jnp.where(masks[k], y[o3 + h : o3 + h + 1], out[f, h, at0].astype(F32))
                    out[f, h, at0] = row.astype(BF16)
            start(put(s, out, enc, sem, f))
        for f in range(PREV):
            wait(put(s, out, enc, sem, f))


def mates(n, phase):
    if phase == 0:
        return [(i, i ^ 1) for i in range(n)]
    return [(i, (i - 1) % n if i % 2 == 0 else (i + 1) % n) for i in range(n)]


def local(video, norm_gain, norm_bias, spatial_weight, spatial_bias, temporal_weight, temporal_bias):
    nta, nha, nwa = (lax.axis_size(a) for a in ("ta", "ha", "wa"))
    s = Sizes(video, nha, nwa)
    c = s.chans
    sd = jax.ShapeDtypeStruct
    ring = [(i, (i + 1) % nta) for i in range(nta)]
    if nwa == 2:
        sides = [[(0, 1), (1, 0)]]
    else:
        sides = [[(i, (i + d) % nwa) for i in range(nwa)] for d in (1, -1)]
    sw = spatial_weight.reshape(9 * c, c)
    tw = temporal_weight.reshape(3 * c, c)
    gain, nbias, sb, tb = (v.reshape(1, c) for v in (norm_gain, norm_bias, spatial_bias, temporal_bias))

    one = video.shape[1:]
    late_shape = sd((s.late,) + one[1:], BF16)
    early, late = call(
        functools.partial(head_kernel, s),
        [sd((s.early,) + one[1:], BF16), late_shape],
        name="head",
        in_specs=[VMEM],
    )(video)
    rowpay = sd((s.frames * s.cols + s.stats, c), BF16)
    stat = sd((2 * s.frames, c), F32)
    colout = [sd((s.frames * s.colrow, c), BF16)] * s.ncol
    riding = s.stats if s.fused else 0
    pay, stats, *cols = call(
        functools.partial(local_kernel, s),
        [rowpay, stat] + colout,
        name="local",
        in_specs=[VMEM, ANY],
    )(video, early)
    early = lax.ppermute(early, "ta", ring)
    got1 = lax.ppermute(pay, "ha", mates(nha, 0))
    late, payy, part, *pays = call(
        functools.partial(pair_kernel, s),
        [late_shape, rowpay, stat]
        + [sd((s.frames * s.colrow + riding, c), BF16)] * s.ncol
        + [sd((s.corner + riding, c), BF16)] * s.ncol,
        out_specs=[ANY] + [VMEM] * (2 + 2 * s.ncol),
        name="pair",
        in_specs=[VMEM] * (3 + s.ncol) + [ANY],
        input_output_aliases={3 + s.ncol: 0},
    )(video, stats, got1, *cols, late)
    outer = mates(nha, 1)
    diagonal = [[(h * nwa + w, g * nwa + v) for h, g in outer for w, v in p] for p in sides]
    goty = lax.ppermute(payy, "ha", outer)
    gotx = [lax.ppermute(x, "wa", p) for x, p in zip(pays[: s.ncol], sides)]
    gotd = [lax.ppermute(x, ("ha", "wa"), p) for x, p in zip(pays[s.ncol :], diagonal)]
    late = lax.ppermute(late, "ta", ring[:-1])
    if not s.fused:
        every = lax.all_gather(stats, ("ha", "wa"))
        part = merge(float(s.rows * s.cols), [every[i] for i in range(nha * nwa)])
    aff, moved = call(
        functools.partial(group_kernel, s),
        [stat, sd((2 * PREV, c), F32)],
        name="group",
        in_specs=[VMEM] * (3 + 2 * s.ncol),
    )(part, gain, goty, *gotx, *gotd)
    moved = lax.ppermute(moved, "ta", ring)
    hand, halo, *cols = call(
        functools.partial(edge_kernel, s),
        [sd((PREV * s.strip + s.tail * s.cols, c), BF16), sd((s.frames, 2, s.cols, c), BF16)] + colout,
        name="edge",
        in_specs=[VMEM] * (4 + 2 * s.ncol),
    )(aff, video, got1, goty, *gotx, *gotd)
    got = lax.ppermute(hand, "ta", ring)
    frame = (s.rows * s.cols, c)
    taps = (3, s.rows + 2, s.cols, c)
    enc, base = call(
        functools.partial(own_kernel, s),
        [sd(video.shape, BF16), sd((PREV,) + frame, F32)],
        out_specs=[ANY, VMEM],
        scratch=[
            pltpu.VMEM(taps, BF16),
            pltpu.VMEM((s.frames,) + frame, BF16),
            pltpu.VMEM((s.frames,) + one, BF16),
            pltpu.SemaphoreType.DMA((s.frames, QUARTERS)),
        ],
        flops=2 * s.rows * s.cols * c * c * (9 * s.frames + 3 * (s.frames - PREV)),
        name="own",
        in_specs=[VMEM] * (8 + s.ncol) + [ANY],
    )(video, halo, aff, nbias, sw, sb, tw, tb, *cols, early)
    grid, inner, pre, rim = call(
        functools.partial(inner_kernel, s),
        [
            sd((PREV,) + taps, BF16),
            sd((PREV,) + frame, BF16),
            sd((PREV,) + one, BF16),
            sd((PREV, s.ncol, s.colrow, c), F32),
        ],
        name="inner",
        in_specs=[VMEM] * 8,
    )(early, late, moved, nbias, sw, sb, tw, base)
    (enc,) = call(
        functools.partial(outer_kernel, s),
        [sd(video.shape, BF16)],
        out_specs=[ANY],
        scratch=[
            pltpu.VMEM((3, s.tail + 2) + one[1:], BF16),
            pltpu.VMEM((PREV, (s.tail + 2) * s.cols + s.ncol * s.colrow, c), BF16),
            pltpu.VMEM((PREV,) + one, BF16),
            pltpu.SemaphoreType.DMA((PREV, QUARTERS)),
        ],
        name="outer",
        in_specs=[VMEM] * 11 + [ANY],
        input_output_aliases={11: 0},
    )(got, moved, grid, inner, nbias, sw, sb, tw, base, pre, rim, enc)
    return enc


def solution(mesh):
    placed = (P("ta", "ha", "wa", None), P(), P(), P(), P(), P(), P())
    return jax.shard_map(
        local, mesh=mesh, in_specs=placed, out_specs=P("ta", "ha", "wa", None), check_vma=False
    )
```

```python
import functools

import jax
import jax.numpy as jnp
from jax import lax
from jax.experimental import pallas as pl
from jax.experimental.pallas import tpu as pltpu
from jax.sharding import PartitionSpec as P

G = 32
EPS = 1e-06
QUARTERS = 4
EDGE = 8
DOTS = 6
PREV = 2
F32 = jnp.float32
BF16 = jnp.bfloat16
VMEM = pl.BlockSpec(memory_space=pltpu.VMEM)
ANY = pl.BlockSpec(memory_space=pl.ANY)


def call(kernel, outs, out_specs=None, scratch=(), flops=1024, name=None, **kw):
    return pl.pallas_call(
        kernel,
        out_shape=outs,
        out_specs=out_specs or [VMEM] * len(outs),
        scratch_shapes=list(scratch),
        compiler_params=pltpu.CompilerParams(vmem_limit_bytes=24 << 20),
        cost_estimate=pl.CostEstimate(flops=flops, bytes_accessed=1024, transcendentals=0),
        name=name,
        **kw,
    )


def pad_to(n, k):
    return (n + k - 1) // k * k


def split3(x):
    hi = x.astype(BF16)
    rest = x - hi.astype(F32)
    mid = rest.astype(BF16)
    low = (rest - mid.astype(F32)).astype(BF16)
    return hi, mid, low


def as_terms(x, rows):
    parts = jnp.concatenate([t.astype(F32) for t in split3(x)], axis=0)
    fill = rows - parts.shape[0]
    if fill:
        parts = jnp.concatenate([parts, jnp.zeros((fill, x.shape[1]), F32)], axis=0)
    return parts.astype(BF16)


def from_terms(t, rows):
    t = t.astype(F32)
    return t[:rows] + t[rows : 2 * rows] + t[2 * rows : 3 * rows]


class Sizes:
    def __init__(self, video, ha, wa):
        self.frames, self.rows, self.cols, self.chans = video.shape
        self.ha, self.wa = ha, wa
        self.ncol = 1 if wa == 2 else 2
        self.fused = ha == 4 and wa == 2
        self.colrow = pad_to(self.rows + 2, 16)
        self.strip = 2 * self.cols + self.ncol * self.colrow
        self.stats = pad_to(3 * 2 * self.frames, 16)
        self.early = (PREV - 1) * self.rows + self.rows // 12
        self.tail = self.rows // 4 + 1
        self.late = PREV * self.rows - self.early - self.tail
        self.corner = pad_to(self.frames, 16)


def head_kernel(s, video, early, late):
    flat = (PREV * s.rows, s.cols, s.chans)
    sent = video[s.frames - PREV :].reshape(flat)
    early[...] = sent[: s.early]
    late[...] = sent[s.early : s.early + s.late]


def local_kernel(s, video, early, pay, stats, *cols):
    ha, wa = lax.axis_index("ha"), lax.axis_index("wa")
    even = lax.rem(ha, 2) == 0
    means, squares = [], []
    for f in range(s.frames):
        total = jnp.zeros((s.cols, s.chans), F32)
        for r in range(s.rows):
            total = total + video[f, r].astype(F32)
        mean = jnp.sum(total, axis=0, keepdims=True) * (1.0 / (s.rows * s.cols))
        spread = jnp.zeros((s.cols, s.chans), F32)
        left, right = [], []
        for r in range(s.rows):
            x = video[f, r].astype(F32)
            left.append(x[:1])
            right.append(x[s.cols - 1 :])
            x = x - mean
            spread = spread + x * x
        means.append(mean)
        squares.append(jnp.sum(spread, axis=0, keepdims=True))
        fill = [jnp.zeros((s.colrow - s.rows, s.chans), F32)]
        left = jnp.concatenate(left + fill, axis=0)
        right = jnp.concatenate(right + fill, axis=0)
        if s.ncol == 1:
            edges = [jnp.where(wa == 0, right, left)]
        else:
            edges = [right, left]
        for ref, e in zip(cols, edges):
            ref[f * s.colrow : (f + 1) * s.colrow] = e.astype(BF16)
        top = video[f, 0].astype(F32)
        bottom = video[f, s.rows - 1].astype(F32)
        pay[f * s.cols : (f + 1) * s.cols] = jnp.where(even, bottom, top).astype(BF16)
    stat = jnp.concatenate(means + squares, axis=0)
    stats[...] = stat
    o = s.frames * s.cols
    pay[o : o + s.stats] = as_terms(stat, s.stats)


def merge(n, parts):
    half = parts[0].shape[0] // 2
    mean = sum(p[:half] for p in parts) * (1.0 / len(parts))
    square = sum(p[half:] + n * (p[:half] - mean) * (p[:half] - mean) for p in parts)
    return jnp.concatenate([mean, square], axis=0)


def pair_kernel(s, video, stats, got, *refs):
    cols, refs = refs[: s.ncol], refs[s.ncol + 1 :]
    _, payy, part = refs[:3]
    payx, payd = refs[3 : 3 + s.ncol], refs[3 + s.ncol :]
    ha, wa = lax.axis_index("ha"), lax.axis_index("wa")
    even = lax.rem(ha, 2) == 0
    o = s.frames * s.cols
    stat = merge(float(s.rows * s.cols), [stats[...], from_terms(got[o : o + s.stats], 2 * s.frames)])
    part[...] = stat
    terms = as_terms(stat, s.stats)
    at = lax.broadcasted_iota(jnp.int32, (s.colrow, s.chans), 0)
    cells = [[] for _ in range(s.ncol)]
    for f in range(s.frames):
        top = video[f, 0].astype(F32)
        bottom = video[f, s.rows - 1].astype(F32)
        outer = jnp.where(even, top, bottom)
        payy[f * s.cols : (f + 1) * s.cols] = outer.astype(BF16)
        inner = got[f * s.cols : (f + 1) * s.cols].astype(F32)
        for k in range(s.ncol):
            right = wa == 0 if s.ncol == 1 else k == 0
            cell = jnp.where(right, inner[s.cols - 1 :], inner[:1])
            cells[k].append(jnp.where(right, outer[s.cols - 1 :], outer[:1]))
            edge = cols[k][f * s.colrow : (f + 1) * s.colrow].astype(F32)
            edge = jnp.where(at >= s.rows, cell, edge)
            payx[k][f * s.colrow : (f + 1) * s.colrow] = edge.astype(BF16)
    for k in range(s.ncol):
        fill = s.corner - s.frames
        rows = cells[k] + ([jnp.zeros((fill, s.chans), F32)] if fill else [])
        payd[k][: s.corner] = jnp.concatenate(rows, axis=0).astype(BF16)
    payy[o : o + s.stats] = terms
    if s.fused:
        o = s.frames * s.colrow
        payx[0][o : o + s.stats] = terms
        payd[0][s.corner : s.corner + s.stats] = terms


def group_kernel(s, part, gain, goty, *refs):
    gotx, gotd = refs[: s.ncol], refs[s.ncol : 2 * s.ncol]
    aff, moved = refs[2 * s.ncol :]
    rows = 2 * s.frames
    count = float(s.rows * s.cols * s.ha * s.wa)
    stat = part[...]
    if s.fused:
        offsets = ((goty, s.frames * s.cols), (gotx[0], s.frames * s.colrow), (gotd[0], s.corner))
        stat = merge(count / 4, [stat] + [from_terms(ref[o : o + s.stats], rows) for ref, o in offsets])
    width = s.chans // G
    a = lax.broadcasted_iota(jnp.int32, (s.chans, s.chans), 0) // width
    b = lax.broadcasted_iota(jnp.int32, (s.chans, s.chans), 1) // width
    group = jnp.where(a == b, 1.0, 0.0).astype(BF16)

    def tot(x):
        terms = jnp.concatenate(split3(x), axis=0)
        y = jnp.dot(terms, group, preferred_element_type=F32)
        n = s.frames
        return y[:n] + y[n : 2 * n] + y[2 * n :]

    m, q = stat[: s.frames], stat[s.frames :]
    mean = tot(m) * (1.0 / width)
    var = tot(q + count * (m - mean) * (m - mean)) * (1.0 / (count * width))
    scale = lax.rsqrt(var + EPS) * gain[...] * 0.5
    aff[: s.frames] = mean
    aff[s.frames :] = scale
    first = s.frames - PREV
    moved[:PREV] = mean[first:]
    moved[PREV:] = scale[first:]


def edge_kernel(s, aff, video, got, goty, *refs):
    gotx, gotd = refs[: s.ncol], refs[s.ncol : 2 * s.ncol]
    hand, halo, *cols = refs[2 * s.ncol :]
    even = lax.rem(lax.axis_index("ha"), 2) == 0
    first = s.frames - PREV
    o = PREV * s.strip
    rest = video[s.frames - 1, s.rows - s.tail :]
    hand[o : o + s.tail * s.cols] = rest.reshape(s.tail * s.cols, s.chans)
    at = lax.broadcasted_iota(jnp.int32, (s.colrow, s.chans), 0)
    for f in range(s.frames):
        p = (f - first) * s.strip
        one = got[f * s.cols : (f + 1) * s.cols].astype(F32)
        two = goty[f * s.cols : (f + 1) * s.cols].astype(F32)
        top = jnp.where(even, two, one).astype(BF16)
        bottom = jnp.where(even, one, two).astype(BF16)
        halo[f, 0] = top
        halo[f, 1] = bottom
        if f >= first:
            hand[p : p + s.cols] = top
            hand[p + s.cols : p + 2 * s.cols] = bottom
        for k in range(s.ncol):
            cell = gotd[k][: s.corner].astype(F32)[f : f + 1]
            edge = gotx[k][f * s.colrow : (f + 1) * s.colrow].astype(F32)
            outer = jnp.where(even, s.rows, s.rows + 1)
            edge = jnp.where(at == outer, cell, edge).astype(BF16)
            cols[k][f * s.colrow : (f + 1) * s.colrow] = edge
            if f >= first:
                o = p + 2 * s.cols + k * s.colrow
                hand[o : o + s.colrow] = edge


def activation(x, mean, scale, shift):
    h = (x - mean) * scale + shift
    return h + h * jnp.tanh(h)


def fill_taps(s, taps, raw_row, edges, mean, scale, shift):
    ha, wa = lax.axis_index("ha"), lax.axis_index("wa")
    top_in = jnp.where(ha > 0, 1.0, 0.0).astype(F32)
    bottom_in = jnp.where(ha < s.ha - 1, 1.0, 0.0).astype(F32)
    left_in = jnp.where(wa > 0, 1.0, 0.0).astype(F32)
    right_in = jnp.where(wa < s.wa - 1, 1.0, 0.0).astype(F32)
    if edges is not None:
        acts = [activation(e.astype(F32), mean, scale, shift) for e in edges]
        left, right = acts[0] * left_in, acts[-1] * right_in
    at = lax.broadcasted_iota(jnp.int32, (s.cols, s.chans), 0)
    for i in range(s.rows + 2):
        raw = raw_row(i)
        if raw is None:
            for dx in range(3):
                taps[dx, i] = jnp.zeros((s.cols, s.chans), BF16)
            continue
        act = activation(raw.astype(F32), mean, scale, shift)
        j = s.rows if i == 0 else s.rows + 1 if i == s.rows + 1 else i - 1
        lcell, rcell = (0.0, 0.0) if edges is None else (left[j : j + 1], right[j : j + 1])
        west = jnp.where(at == 0, lcell, pltpu.roll(act, 1, 0))
        east = jnp.where(at == s.cols - 1, rcell, pltpu.roll(act, s.cols - 1, 0))
        if i in (0, s.rows + 1):
            inside = top_in if i == 0 else bottom_in
            west, act, east = west * inside, act * inside, east * inside
        taps[0, i] = west.astype(BF16)
        taps[1, i] = act.astype(BF16)
        taps[2, i] = east.astype(BF16)


def spatial_dot(s, taps, weight, bias, rows):
    size = s.rows // DOTS
    done = []
    for r in range(0, rows, size):
        step = min(size, rows - r)
        lhs = jnp.concatenate(
            [
                taps[dx, r + dy : r + dy + step].reshape(step * s.cols, s.chans)
                for dy in range(3)
                for dx in range(3)
            ],
            axis=1,
        )
        done.append((jnp.dot(lhs, weight[...], preferred_element_type=F32) + bias[...]).astype(BF16))
    return jnp.concatenate(done, axis=0)


def temporal_dot(s, frames, weight, bias):
    lhs = jnp.concatenate(frames, axis=1)
    out = jnp.dot(lhs, weight[...], preferred_element_type=F32) + bias[...]
    return out.astype(BF16).reshape(s.rows, s.cols, s.chans)


def put(s, ref, enc, sem, f, quarters=range(QUARTERS)):
    step = s.rows // QUARTERS
    return [
        pltpu.make_async_copy(
            ref.at[f, pl.ds(k * step, step)], enc.at[f, pl.ds(k * step, step)], sem.at[f, k]
        )
        for k in quarters
    ]


def start(copies):
    for c in copies:
        c.start()


def wait(copies):
    for c in copies:
        c.wait()


def own_kernel(s, video, halo, aff, nbias, sw, sb, tw, tb, *refs):
    cols = refs[: s.ncol]
    enc, base, taps, spatial, out, sem = refs[s.ncol + 1 :]
    shift = nbias[...] * 0.5
    first = lax.axis_index("ta") == 0

    def frame(f, _):
        def raw_row(i):
            if i == 0:
                return halo[f, 0]
            if i == s.rows + 1:
                return halo[f, 1]
            return video[f, i - 1]

        edges = [c[pl.ds(f * s.colrow, s.colrow)] for c in cols]
        fill_taps(s, taps, raw_row, edges, aff[pl.ds(f, 1)], aff[pl.ds(s.frames + f, 1)], shift)
        spatial[f] = spatial_dot(s, taps, sw, sb, s.rows)
        return _

    lax.fori_loop(0, s.frames, frame, 0)

    def encode(f):
        out[f] = temporal_dot(s, [spatial[max(f - k, 0)] for k in range(3)], tw, tb)
        start(put(s, out, enc, sem, f))

    for f in range(PREV, s.frames):
        encode(f)

    @pl.when(first)
    def _():
        for f in range(PREV):
            encode(f)
        for f in range(PREV):
            wait(put(s, out, enc, sem, f))

    @pl.when(jnp.logical_not(first))
    def _():
        for f in range(PREV):
            lhs = jnp.concatenate([spatial[f - k] for k in range(f + 1)], axis=1)
            weight = tw[: (f + 1) * s.chans]
            base[f] = jnp.dot(lhs, weight, preferred_element_type=F32) + tb[...]

    for f in range(PREV, s.frames):
        wait(put(s, out, enc, sem, f))


def taps_back(s, grids, f, tw):
    lhs = jnp.concatenate([grids[q] for q in range(PREV - 1, f - 1, -1)], axis=1)
    return jnp.dot(lhs, tw[(f + 1) * s.chans :], preferred_element_type=F32)


def inner_kernel(s, early, late, moved, nbias, sw, sb, tw, base, taps, spatial, pre, rim):
    shift = nbias[...] * 0.5

    @pl.when(lax.axis_index("ta") > 0)
    def _():
        for p in range(PREV):

            def raw_row(i):
                if i == 0 or i == s.rows + 1:
                    return None
                r = p * s.rows + i - 1
                if r >= s.early + s.late:
                    return None
                return early[r] if r < s.early else late[r - s.early]

            fill_taps(s, taps.at[p], raw_row, None, moved[p : p + 1], moved[PREV + p : PREV + p + 1], shift)
            rows = s.rows if p < PREV - 1 else s.rows - s.tail - 1
            spatial[p, : rows * s.cols] = spatial_dot(s, taps.at[p], sw, sb, rows)
        part = slice(s.cols, (s.rows - s.tail - 1) * s.cols)
        for f in range(PREV):
            y = taps_back(s, [spatial[q, part] for q in range(PREV)], f, tw) + base[f, part]
            pre[f, 1 : s.rows - s.tail - 1] = y.astype(BF16).reshape(-1, s.cols, s.chans)
            for k in range(s.ncol):
                right = lax.axis_index("wa") == 0 if s.ncol == 1 else k == 1
                cells = []
                for h in range(s.rows):
                    o = h * s.cols
                    last = base[f, o + s.cols - 8 : o + s.cols]
                    cells.append(jnp.where(right, last[7:], base[f, o : o + 8][:1]))
                cells.append(jnp.zeros((s.colrow - s.rows, s.chans), F32))
                rim[f, k] = jnp.concatenate(cells, axis=0)


def outer_kernel(s, got, moved, taps, spatial, nbias, sw, sb, tw, base, pre, rim, _, enc, more, grid, out, sem):
    ha, wa = lax.axis_index("ha"), lax.axis_index("wa")
    shift = nbias[...] * 0.5
    inside = [jnp.where(ha > 0, 1.0, 0.0).astype(F32), jnp.where(ha < s.ha - 1, 1.0, 0.0).astype(F32)]
    at = lax.broadcasted_iota(jnp.int32, (s.cols, s.chans), 0)
    down = lax.broadcasted_iota(jnp.int32, (s.colrow, s.chans), 0)
    if s.ncol == 1:
        sides = [wa == 0]
        present = [jnp.ones((), F32)]
    else:
        sides = [False, True]
        present = [jnp.where(wa > 0, 1.0, 0.0).astype(F32), jnp.where(wa < s.wa - 1, 1.0, 0.0).astype(F32)]

    @pl.when(lax.axis_index("ta") > 0)
    def _():
        copies = []
        width = s.cols - EDGE * s.ncol
        safe = EDGE if s.ncol > 1 else pl.multiple_of(jnp.where(wa == 0, 0, EDGE), EDGE)
        for f in range(PREV):
            place = (f, pl.ds(1, s.rows - s.tail - 2), pl.ds(safe, width))
            copies.append(pltpu.make_async_copy(pre.at[place], enc.at[place], sem.at[f, 4]))
        start(copies)
        lhs = []
        start_row = s.rows - s.tail - 1
        end = PREV - 1

        def tap(p, dx, i):
            return more[dx, i - start_row] if p == end and i >= start_row else taps[p, dx, i]

        def shifted(act):
            west = jnp.where(at == 0, 0.0, pltpu.roll(act, 1, 0))
            east = jnp.where(at == s.cols - 1, 0.0, pltpu.roll(act, s.cols - 1, 0))
            return [x.astype(BF16) for x in (west, act, east)]

        for dx in range(3):
            more[dx, :2] = taps[end, dx, start_row : start_row + 2]
        for i in range(s.tail):
            o = PREV * s.strip + i * s.cols
            raw = got[o : o + s.cols].astype(F32)
            act = activation(raw, moved[end : end + 1], moved[PREV + end : PREV + end + 1], shift)
            for dx, x in enumerate(shifted(act)):
                more[dx, 2 + i] = x
        for p in range(PREV):
            mean, scale = moved[p : p + 1], moved[PREV + p : PREV + p + 1]
            o = p * s.strip
            acts = []
            for k in range(2):
                raw = got[o + k * s.cols : o + (k + 1) * s.cols].astype(F32)
                act = activation(raw, mean, scale, shift) * inside[k]
                acts.append(act)
            top, bottom = shifted(acts[0]), shifted(acts[1])
            lhs.append(
                jnp.concatenate(top + [tap(p, dx, i) for i in (1, 2) for dx in range(3)], axis=1)
            )
            n = s.rows
            lhs.append(
                jnp.concatenate([tap(p, dx, i) for i in (n - 1, n) for dx in range(3)] + bottom, axis=1)
            )
            for k in range(s.ncol):
                o2 = o + 2 * s.cols + k * s.colrow
                cell = activation(got[o2 : o2 + s.colrow].astype(F32), mean, scale, shift) * present[k]
                upper = cell[n : n + 1] * inside[0]
                lower = cell[n + 1 : n + 2] * inside[1]
                right = sides[k]

                def column(d):
                    rows = []
                    for i in range(1, n + 1):
                        tile = tap(p, 1, i).astype(F32)
                        if d == 0:
                            rows.append(jnp.where(right, tile[s.cols - 1 :], tile[:1]))
                        else:
                            rows.append(jnp.where(right, tile[s.cols - 2 : s.cols - 1], tile[1:2]))
                    fill = jnp.zeros((s.colrow - n, s.chans), F32)
                    return jnp.concatenate(rows + [fill], axis=0)

                here, inner = column(0), column(1)
                far = jnp.where(down < n, cell, 0.0)
                ends = [
                    tuple(jnp.where(right, a[s.cols - 1 :], a[:1]) for a in acts),
                    tuple(jnp.where(right, a[s.cols - 2 : s.cols - 1], a[1:2]) for a in acts),
                    (upper, lower),
                ]
                steps = []
                for dy in range(3):
                    group = []
                    for x, (first, final) in zip((here, inner, far), ends):
                        if dy == 0:
                            x = jnp.where(down == 0, first, pltpu.roll(x, 1, 0))
                        elif dy == 2:
                            x = jnp.where(down == n - 1, final, pltpu.roll(x, s.colrow - 1, 0))
                        group.append(x)
                    mid, inn, out_ = group
                    steps += [jnp.where(right, inn, out_), mid, jnp.where(right, out_, inn)]
                lhs.append(jnp.concatenate([x.astype(BF16) for x in steps], axis=1))
        fresh = s.tail * s.cols
        lhs.append(
            jnp.concatenate(
                [
                    more[dx, dy : dy + s.tail].reshape(fresh, s.chans)
                    for dy in range(3)
                    for dx in range(3)
                ],
                axis=1,
            )
        )
        border = jnp.dot(jnp.concatenate(lhs, axis=0), sw[...], preferred_element_type=F32) + sb[...]
        size = 2 * s.cols + s.ncol * s.colrow
        tile = 16
        cells = lax.broadcasted_iota(jnp.int32, (tile, s.chans), 0)
        masks = [cells == jnp.where(right, tile - 1, 0) for right in sides]
        starts = [jnp.where(right, s.cols - tile, 0) for right in sides]
        first, body = s.cols, (s.tail + 1) * s.cols
        for p in range(PREV):
            o = p * size
            grid[p, :first] = border[o : o + first].astype(BF16)
            if p < end:
                rest = spatial[p, start_row * s.cols : (s.rows - 1) * s.cols]
            else:
                rest = border[PREV * size : PREV * size + fresh].astype(BF16)
            grid[p, first : body] = rest
            grid[p, body : body + s.cols] = border[o + s.cols : o + 2 * s.cols].astype(BF16)
            for k in range(s.ncol):
                o2 = o + 2 * s.cols + k * s.colrow
                for g in range(s.tail + 2):
                    h = 0 if g == 0 else start_row + g - 1
                    at0 = pl.ds(pl.multiple_of(g * s.cols + starts[k], tile), tile)
                    row = jnp.where(masks[k], border[o2 + h : o2 + h + 1], grid[p, at0].astype(F32))
                    grid[p, at0] = row.astype(BF16)
                o3 = body + s.cols + k * s.colrow
                grid[p, o3 : o3 + s.colrow] = border[o2 : o2 + s.colrow].astype(BF16)
        for f in range(PREV):
            own = [base[f, :first], base[f, start_row * s.cols :]] + [rim[f, k] for k in range(s.ncol)]
            y = taps_back(s, [grid[q] for q in range(PREV)], f, tw) + jnp.concatenate(own, axis=0)
            out[f, 0] = y[:first].astype(BF16)
            out[f, start_row:] = y[first : body + s.cols].astype(BF16).reshape(-1, s.cols, s.chans)
            rows = pl.ds(start_row, s.tail + 1)
            copies += [
                pltpu.make_async_copy(out.at[f, 0], enc.at[f, 0], sem.at[f, 0]),
                pltpu.make_async_copy(out.at[f, rows], enc.at[f, rows], sem.at[f, 1]),
            ]
            start(copies[-2:])
            for k in range(s.ncol):
                o3 = body + s.cols + k * s.colrow
                at0 = pl.ds(pl.multiple_of(starts[k], tile), tile)
                for h in range(1, start_row):
                    row = jnp.where(masks[k], y[o3 + h : o3 + h + 1], pre[f, h, at0].astype(F32))
                    out[f, h, at0] = row.astype(BF16)
                edge = pl.multiple_of(jnp.where(sides[k], s.cols - EDGE, 0), EDGE)
                place = (f, pl.ds(1, start_row - 1), pl.ds(edge, EDGE))
                copies.append(pltpu.make_async_copy(out.at[place], enc.at[place], sem.at[f, 2 + k]))
                copies[-1].start()
        wait(copies)


def mates(n, phase):
    if phase == 0:
        return [(i, i ^ 1) for i in range(n)]
    return [(i, (i - 1) % n if i % 2 == 0 else (i + 1) % n) for i in range(n)]


def local(video, norm_gain, norm_bias, spatial_weight, spatial_bias, temporal_weight, temporal_bias):
    nta, nha, nwa = (lax.axis_size(a) for a in ("ta", "ha", "wa"))
    s = Sizes(video, nha, nwa)
    c = s.chans
    sd = jax.ShapeDtypeStruct
    ring = [(i, (i + 1) % nta) for i in range(nta)]
    if nwa == 2:
        sides = [[(0, 1), (1, 0)]]
    else:
        sides = [[(i, (i + d) % nwa) for i in range(nwa)] for d in (1, -1)]
    sw = spatial_weight.reshape(9 * c, c)
    tw = temporal_weight.reshape(3 * c, c)
    gain, nbias, sb, tb = (v.reshape(1, c) for v in (norm_gain, norm_bias, spatial_bias, temporal_bias))

    one = video.shape[1:]
    late_shape = sd((s.late,) + one[1:], BF16)
    early, late = call(
        functools.partial(head_kernel, s),
        [sd((s.early,) + one[1:], BF16), late_shape],
        name="head",
        in_specs=[VMEM],
    )(video)
    rowpay = sd((s.frames * s.cols + s.stats, c), BF16)
    stat = sd((2 * s.frames, c), F32)
    colout = [sd((s.frames * s.colrow, c), BF16)] * s.ncol
    riding = s.stats if s.fused else 0
    pay, stats, *cols = call(
        functools.partial(local_kernel, s),
        [rowpay, stat] + colout,
        name="local",
        in_specs=[VMEM, ANY],
    )(video, early)
    early = lax.ppermute(early, "ta", ring)
    got1 = lax.ppermute(pay, "ha", mates(nha, 0))
    late, payy, part, *pays = call(
        functools.partial(pair_kernel, s),
        [late_shape, rowpay, stat]
        + [sd((s.frames * s.colrow + riding, c), BF16)] * s.ncol
        + [sd((s.corner + riding, c), BF16)] * s.ncol,
        out_specs=[ANY] + [VMEM] * (2 + 2 * s.ncol),
        name="pair",
        in_specs=[VMEM] * (3 + s.ncol) + [ANY],
        input_output_aliases={3 + s.ncol: 0},
    )(video, stats, got1, *cols, late)
    outer = mates(nha, 1)
    diagonal = [[(h * nwa + w, g * nwa + v) for h, g in outer for w, v in p] for p in sides]
    goty = lax.ppermute(payy, "ha", outer)
    gotx = [lax.ppermute(x, "wa", p) for x, p in zip(pays[: s.ncol], sides)]
    gotd = [lax.ppermute(x, ("ha", "wa"), p) for x, p in zip(pays[s.ncol :], diagonal)]
    late = lax.ppermute(late, "ta", ring[:-1])
    if not s.fused:
        every = lax.all_gather(stats, ("ha", "wa"))
        part = merge(float(s.rows * s.cols), [every[i] for i in range(nha * nwa)])
    aff, moved = call(
        functools.partial(group_kernel, s),
        [stat, sd((2 * PREV, c), F32)],
        name="group",
        in_specs=[VMEM] * (3 + 2 * s.ncol),
    )(part, gain, goty, *gotx, *gotd)
    moved = lax.ppermute(moved, "ta", ring)
    hand, halo, *cols = call(
        functools.partial(edge_kernel, s),
        [sd((PREV * s.strip + s.tail * s.cols, c), BF16), sd((s.frames, 2, s.cols, c), BF16)] + colout,
        name="edge",
        in_specs=[VMEM] * (4 + 2 * s.ncol),
    )(aff, video, got1, goty, *gotx, *gotd)
    got = lax.ppermute(hand, "ta", ring)
    frame = (s.rows * s.cols, c)
    taps = (3, s.rows + 2, s.cols, c)
    enc, base = call(
        functools.partial(own_kernel, s),
        [sd(video.shape, BF16), sd((PREV,) + frame, F32)],
        out_specs=[ANY, VMEM],
        scratch=[
            pltpu.VMEM(taps, BF16),
            pltpu.VMEM((s.frames,) + frame, BF16),
            pltpu.VMEM((s.frames,) + one, BF16),
            pltpu.SemaphoreType.DMA((s.frames, QUARTERS)),
        ],
        flops=2 * s.rows * s.cols * c * c * (9 * s.frames + 3 * (s.frames - PREV)),
        name="own",
        in_specs=[VMEM] * (8 + s.ncol) + [ANY],
    )(video, halo, aff, nbias, sw, sb, tw, tb, *cols, early)
    grid, inner, pre, rim = call(
        functools.partial(inner_kernel, s),
        [
            sd((PREV,) + taps, BF16),
            sd((PREV,) + frame, BF16),
            sd((PREV,) + one, BF16),
            sd((PREV, s.ncol, s.colrow, c), F32),
        ],
        name="inner",
        in_specs=[VMEM] * 8,
    )(early, late, moved, nbias, sw, sb, tw, base)
    (enc,) = call(
        functools.partial(outer_kernel, s),
        [sd(video.shape, BF16)],
        out_specs=[ANY],
        scratch=[
            pltpu.VMEM((3, s.tail + 2) + one[1:], BF16),
            pltpu.VMEM((PREV, (s.tail + 2) * s.cols + s.ncol * s.colrow, c), BF16),
            pltpu.VMEM((PREV,) + one, BF16),
            pltpu.SemaphoreType.DMA((PREV, 5)),
        ],
        name="outer",
        in_specs=[VMEM] * 11 + [ANY],
        input_output_aliases={11: 0},
    )(got, moved, grid, inner, nbias, sw, sb, tw, base, pre, rim, enc)
    return enc


def solution(mesh):
    placed = (P("ta", "ha", "wa", None), P(), P(), P(), P(), P(), P())
    return jax.shard_map(
        local, mesh=mesh, in_specs=placed, out_specs=P("ta", "ha", "wa", None), check_vma=False
    )
```

```python
import functools

import jax
import jax.numpy as jnp
from jax import lax
from jax.experimental import pallas as pl
from jax.experimental.pallas import tpu as pltpu
from jax.sharding import PartitionSpec as P

G = 32
EPS = 1e-06
QUARTERS = 4
EDGE = 8
DOTS = 6
PREV = 2
F32 = jnp.float32
BF16 = jnp.bfloat16
VMEM = pl.BlockSpec(memory_space=pltpu.VMEM)
ANY = pl.BlockSpec(memory_space=pl.ANY)


def call(kernel, outs, out_specs=None, scratch=(), flops=1024, name=None, **kw):
    return pl.pallas_call(
        kernel,
        out_shape=outs,
        out_specs=out_specs or [VMEM] * len(outs),
        scratch_shapes=list(scratch),
        compiler_params=pltpu.CompilerParams(vmem_limit_bytes=24 << 20),
        cost_estimate=pl.CostEstimate(flops=flops, bytes_accessed=1024, transcendentals=0),
        name=name,
        **kw,
    )


def pad_to(n, k):
    return (n + k - 1) // k * k


def split3(x):
    hi = x.astype(BF16)
    rest = x - hi.astype(F32)
    mid = rest.astype(BF16)
    low = (rest - mid.astype(F32)).astype(BF16)
    return hi, mid, low


def as_terms(x, rows):
    parts = jnp.concatenate([t.astype(F32) for t in split3(x)], axis=0)
    fill = rows - parts.shape[0]
    if fill:
        parts = jnp.concatenate([parts, jnp.zeros((fill, x.shape[1]), F32)], axis=0)
    return parts.astype(BF16)


def from_terms(t, rows):
    t = t.astype(F32)
    return t[:rows] + t[rows : 2 * rows] + t[2 * rows : 3 * rows]


class Sizes:
    def __init__(self, video, ha, wa):
        self.frames, self.rows, self.cols, self.chans = video.shape
        self.ha, self.wa = ha, wa
        self.ncol = 1 if wa == 2 else 2
        self.fused = ha == 4 and wa == 2
        self.colrow = pad_to(self.rows + 2, 16)
        self.strip = 2 * self.cols + self.ncol * self.colrow
        self.stats = pad_to(3 * 2 * self.frames, 16)
        self.early = (PREV - 1) * self.rows + self.rows // 12
        self.tail = self.rows // 4 + 1
        self.late = PREV * self.rows - self.early - self.tail
        self.corner = pad_to(self.frames, 16)


def head_kernel(s, video, early, late):
    flat = (PREV * s.rows, s.cols, s.chans)
    sent = video[s.frames - PREV :].reshape(flat)
    early[...] = sent[: s.early]
    late[...] = sent[s.early : s.early + s.late]


def local_kernel(s, video, early, pay, stats, *cols):
    ha, wa = lax.axis_index("ha"), lax.axis_index("wa")
    even = lax.rem(ha, 2) == 0
    means, squares = [], []
    for f in range(s.frames):
        total = jnp.zeros((s.cols, s.chans), F32)
        for r in range(s.rows):
            total = total + video[f, r].astype(F32)
        mean = jnp.sum(total, axis=0, keepdims=True) * (1.0 / (s.rows * s.cols))
        spread = jnp.zeros((s.cols, s.chans), F32)
        left, right = [], []
        for r in range(s.rows):
            x = video[f, r].astype(F32)
            left.append(x[:1])
            right.append(x[s.cols - 1 :])
            x = x - mean
            spread = spread + x * x
        means.append(mean)
        squares.append(jnp.sum(spread, axis=0, keepdims=True))
        fill = [jnp.zeros((s.colrow - s.rows, s.chans), F32)]
        left = jnp.concatenate(left + fill, axis=0)
        right = jnp.concatenate(right + fill, axis=0)
        if s.ncol == 1:
            edges = [jnp.where(wa == 0, right, left)]
        else:
            edges = [right, left]
        for ref, e in zip(cols, edges):
            ref[f * s.colrow : (f + 1) * s.colrow] = e.astype(BF16)
        top = video[f, 0].astype(F32)
        bottom = video[f, s.rows - 1].astype(F32)
        pay[f * s.cols : (f + 1) * s.cols] = jnp.where(even, bottom, top).astype(BF16)
    stat = jnp.concatenate(means + squares, axis=0)
    stats[...] = stat
    o = s.frames * s.cols
    pay[o : o + s.stats] = as_terms(stat, s.stats)


def merge(n, parts):
    half = parts[0].shape[0] // 2
    mean = sum(p[:half] for p in parts) * (1.0 / len(parts))
    square = sum(p[half:] + n * (p[:half] - mean) * (p[:half] - mean) for p in parts)
    return jnp.concatenate([mean, square], axis=0)


def pair_kernel(s, video, stats, got, *refs):
    cols, refs = refs[: s.ncol], refs[s.ncol + 1 :]
    _, payy, part = refs[:3]
    payx, payd = refs[3 : 3 + s.ncol], refs[3 + s.ncol :]
    ha, wa = lax.axis_index("ha"), lax.axis_index("wa")
    even = lax.rem(ha, 2) == 0
    o = s.frames * s.cols
    stat = merge(float(s.rows * s.cols), [stats[...], from_terms(got[o : o + s.stats], 2 * s.frames)])
    part[...] = stat
    terms = as_terms(stat, s.stats)
    at = lax.broadcasted_iota(jnp.int32, (s.colrow, s.chans), 0)
    cells = [[] for _ in range(s.ncol)]
    for f in range(s.frames):
        top = video[f, 0].astype(F32)
        bottom = video[f, s.rows - 1].astype(F32)
        outer = jnp.where(even, top, bottom)
        payy[f * s.cols : (f + 1) * s.cols] = outer.astype(BF16)
        inner = got[f * s.cols : (f + 1) * s.cols].astype(F32)
        for k in range(s.ncol):
            right = wa == 0 if s.ncol == 1 else k == 0
            cell = jnp.where(right, inner[s.cols - 1 :], inner[:1])
            cells[k].append(jnp.where(right, outer[s.cols - 1 :], outer[:1]))
            edge = cols[k][f * s.colrow : (f + 1) * s.colrow].astype(F32)
            edge = jnp.where(at >= s.rows, cell, edge)
            payx[k][f * s.colrow : (f + 1) * s.colrow] = edge.astype(BF16)
    for k in range(s.ncol):
        fill = s.corner - s.frames
        rows = cells[k] + ([jnp.zeros((fill, s.chans), F32)] if fill else [])
        payd[k][: s.corner] = jnp.concatenate(rows, axis=0).astype(BF16)
    payy[o : o + s.stats] = terms
    if s.fused:
        o = s.frames * s.colrow
        payx[0][o : o + s.stats] = terms
        payd[0][s.corner : s.corner + s.stats] = terms


def group_kernel(s, part, gain, goty, *refs):
    gotx, gotd = refs[: s.ncol], refs[s.ncol : 2 * s.ncol]
    aff, moved = refs[2 * s.ncol :]
    rows = 2 * s.frames
    count = float(s.rows * s.cols * s.ha * s.wa)
    stat = part[...]
    if s.fused:
        offsets = ((goty, s.frames * s.cols), (gotx[0], s.frames * s.colrow), (gotd[0], s.corner))
        stat = merge(count / 4, [stat] + [from_terms(ref[o : o + s.stats], rows) for ref, o in offsets])
    width = s.chans // G
    a = lax.broadcasted_iota(jnp.int32, (s.chans, s.chans), 0) // width
    b = lax.broadcasted_iota(jnp.int32, (s.chans, s.chans), 1) // width
    group = jnp.where(a == b, 1.0, 0.0).astype(BF16)

    def tot(x):
        terms = jnp.concatenate(split3(x), axis=0)
        y = jnp.dot(terms, group, preferred_element_type=F32)
        n = s.frames
        return y[:n] + y[n : 2 * n] + y[2 * n :]

    m, q = stat[: s.frames], stat[s.frames :]
    mean = tot(m) * (1.0 / width)
    var = tot(q + count * (m - mean) * (m - mean)) * (1.0 / (count * width))
    scale = lax.rsqrt(var + EPS) * gain[...] * 0.5
    aff[: s.frames] = mean
    aff[s.frames :] = scale
    first = s.frames - PREV
    moved[:PREV] = mean[first:]
    moved[PREV:] = scale[first:]


def edge_kernel(s, aff, video, got, goty, *refs):
    gotx, gotd = refs[: s.ncol], refs[s.ncol : 2 * s.ncol]
    hand, halo, *cols = refs[2 * s.ncol :]
    even = lax.rem(lax.axis_index("ha"), 2) == 0
    first = s.frames - PREV
    o = PREV * s.strip
    rest = video[s.frames - 1, s.rows - s.tail :]
    hand[o : o + s.tail * s.cols] = rest.reshape(s.tail * s.cols, s.chans)
    at = lax.broadcasted_iota(jnp.int32, (s.colrow, s.chans), 0)
    for f in range(s.frames):
        p = (f - first) * s.strip
        one = got[f * s.cols : (f + 1) * s.cols].astype(F32)
        two = goty[f * s.cols : (f + 1) * s.cols].astype(F32)
        top = jnp.where(even, two, one).astype(BF16)
        bottom = jnp.where(even, one, two).astype(BF16)
        halo[f, 0] = top
        halo[f, 1] = bottom
        if f >= first:
            hand[p : p + s.cols] = top
            hand[p + s.cols : p + 2 * s.cols] = bottom
        for k in range(s.ncol):
            cell = gotd[k][: s.corner].astype(F32)[f : f + 1]
            edge = gotx[k][f * s.colrow : (f + 1) * s.colrow].astype(F32)
            outer = jnp.where(even, s.rows, s.rows + 1)
            edge = jnp.where(at == outer, cell, edge).astype(BF16)
            cols[k][f * s.colrow : (f + 1) * s.colrow] = edge
            if f >= first:
                o = p + 2 * s.cols + k * s.colrow
                hand[o : o + s.colrow] = edge


def activation(x, mean, scale, shift):
    h = (x - mean) * scale + shift
    return h + h * jnp.tanh(h)


def fill_taps(s, taps, raw_row, edges, mean, scale, shift):
    ha, wa = lax.axis_index("ha"), lax.axis_index("wa")
    top_in = jnp.where(ha > 0, 1.0, 0.0).astype(F32)
    bottom_in = jnp.where(ha < s.ha - 1, 1.0, 0.0).astype(F32)
    left_in = jnp.where(wa > 0, 1.0, 0.0).astype(F32)
    right_in = jnp.where(wa < s.wa - 1, 1.0, 0.0).astype(F32)
    if edges is not None:
        acts = [activation(e.astype(F32), mean, scale, shift) for e in edges]
        left, right = acts[0] * left_in, acts[-1] * right_in
    at = lax.broadcasted_iota(jnp.int32, (s.cols, s.chans), 0)
    for i in range(s.rows + 2):
        raw = raw_row(i)
        if raw is None:
            for dx in range(3):
                taps[dx, i] = jnp.zeros((s.cols, s.chans), BF16)
            continue
        act = activation(raw.astype(F32), mean, scale, shift)
        j = s.rows if i == 0 else s.rows + 1 if i == s.rows + 1 else i - 1
        lcell, rcell = (0.0, 0.0) if edges is None else (left[j : j + 1], right[j : j + 1])
        west = jnp.where(at == 0, lcell, pltpu.roll(act, 1, 0))
        east = jnp.where(at == s.cols - 1, rcell, pltpu.roll(act, s.cols - 1, 0))
        if i in (0, s.rows + 1):
            inside = top_in if i == 0 else bottom_in
            west, act, east = west * inside, act * inside, east * inside
        taps[0, i] = west.astype(BF16)
        taps[1, i] = act.astype(BF16)
        taps[2, i] = east.astype(BF16)


def spatial_dot(s, taps, weight, bias, rows):
    size = s.rows // DOTS
    done = []
    for r in range(0, rows, size):
        step = min(size, rows - r)
        lhs = jnp.concatenate(
            [
                taps[dx, r + dy : r + dy + step].reshape(step * s.cols, s.chans)
                for dy in range(3)
                for dx in range(3)
            ],
            axis=1,
        )
        done.append((jnp.dot(lhs, weight[...], preferred_element_type=F32) + bias[...]).astype(BF16))
    return jnp.concatenate(done, axis=0)


def temporal_dot(s, frames, weight, bias):
    lhs = jnp.concatenate(frames, axis=1)
    out = jnp.dot(lhs, weight[...], preferred_element_type=F32) + bias[...]
    return out.astype(BF16).reshape(s.rows, s.cols, s.chans)


def put(s, ref, enc, sem, f, quarters=range(QUARTERS)):
    step = s.rows // QUARTERS
    return [
        pltpu.make_async_copy(
            ref.at[f, pl.ds(k * step, step)], enc.at[f, pl.ds(k * step, step)], sem.at[f, k]
        )
        for k in quarters
    ]


def start(copies):
    for c in copies:
        c.start()


def wait(copies):
    for c in copies:
        c.wait()


def own_kernel(s, video, halo, aff, nbias, sw, sb, tw, tb, *refs):
    cols = refs[: s.ncol]
    enc, base, taps, spatial, out, sem = refs[s.ncol + 1 :]
    shift = nbias[...] * 0.5
    first = lax.axis_index("ta") == 0

    def frame(f, _):
        def raw_row(i):
            if i == 0:
                return halo[f, 0]
            if i == s.rows + 1:
                return halo[f, 1]
            return video[f, i - 1]

        edges = [c[pl.ds(f * s.colrow, s.colrow)] for c in cols]
        fill_taps(s, taps, raw_row, edges, aff[pl.ds(f, 1)], aff[pl.ds(s.frames + f, 1)], shift)
        spatial[f] = spatial_dot(s, taps, sw, sb, s.rows)
        return _

    lax.fori_loop(0, s.frames, frame, 0)

    def encode(f):
        out[f] = temporal_dot(s, [spatial[max(f - k, 0)] for k in range(3)], tw, tb)
        start(put(s, out, enc, sem, f))

    for f in range(PREV, s.frames):
        encode(f)

    @pl.when(first)
    def _():
        for f in range(PREV):
            encode(f)
        for f in range(PREV):
            wait(put(s, out, enc, sem, f))

    @pl.when(jnp.logical_not(first))
    def _():
        for f in range(PREV):
            lhs = jnp.concatenate([spatial[f - k] for k in range(f + 1)], axis=1)
            weight = tw[: (f + 1) * s.chans]
            base[f] = jnp.dot(lhs, weight, preferred_element_type=F32) + tb[...]

    for f in range(PREV, s.frames):
        wait(put(s, out, enc, sem, f))


def taps_back(s, grids, f, tw):
    lhs = jnp.concatenate([grids[q] for q in range(PREV - 1, f - 1, -1)], axis=1)
    return jnp.dot(lhs, tw[(f + 1) * s.chans :], preferred_element_type=F32)


def inner_kernel(s, early, late, moved, nbias, sw, sb, tw, base, taps, spatial, pre, rim, cut):
    shift = nbias[...] * 0.5

    @pl.when(lax.axis_index("ta") > 0)
    def _():
        for p in range(PREV):

            def raw_row(i):
                if i == 0 or i == s.rows + 1:
                    return None
                r = p * s.rows + i - 1
                if r >= s.early + s.late:
                    return None
                return early[r] if r < s.early else late[r - s.early]

            fill_taps(s, taps.at[p], raw_row, None, moved[p : p + 1], moved[PREV + p : PREV + p + 1], shift)
            rows = s.rows if p < PREV - 1 else s.rows - s.tail - 1
            for k in range(s.ncol):
                right = lax.axis_index("wa") == 0 if s.ncol == 1 else k == 1
                for d in range(2):
                    cells = []
                    for i in range(1, rows + 1):
                        tile = taps[p, 1, i].astype(F32)
                        far = tile[s.cols - 1 - d : s.cols - d]
                        cells.append(jnp.where(right, far, tile[d : d + 1]))
                    cells.append(jnp.zeros((s.colrow - rows, s.chans), F32))
                    cut[p, 2 * k + d] = jnp.concatenate(cells, axis=0)
            spatial[p, : rows * s.cols] = spatial_dot(s, taps.at[p], sw, sb, rows)
        part = slice(s.cols, (s.rows - s.tail - 1) * s.cols)
        for f in range(PREV):
            y = taps_back(s, [spatial[q, part] for q in range(PREV)], f, tw) + base[f, part]
            pre[f, 1 : s.rows - s.tail - 1] = y.astype(BF16).reshape(-1, s.cols, s.chans)
            for k in range(s.ncol):
                right = lax.axis_index("wa") == 0 if s.ncol == 1 else k == 1
                cells = []
                for h in range(s.rows):
                    o = h * s.cols
                    last = base[f, o + s.cols - 8 : o + s.cols]
                    cells.append(jnp.where(right, last[7:], base[f, o : o + 8][:1]))
                cells.append(jnp.zeros((s.colrow - s.rows, s.chans), F32))
                rim[f, k] = jnp.concatenate(cells, axis=0)


def outer_kernel(s, got, moved, taps, spatial, nbias, sw, sb, tw, base, pre, rim, cut, _, enc, more, grid, out, sem):
    ha, wa = lax.axis_index("ha"), lax.axis_index("wa")
    shift = nbias[...] * 0.5
    inside = [jnp.where(ha > 0, 1.0, 0.0).astype(F32), jnp.where(ha < s.ha - 1, 1.0, 0.0).astype(F32)]
    at = lax.broadcasted_iota(jnp.int32, (s.cols, s.chans), 0)
    down = lax.broadcasted_iota(jnp.int32, (s.colrow, s.chans), 0)
    if s.ncol == 1:
        sides = [wa == 0]
        present = [jnp.ones((), F32)]
    else:
        sides = [False, True]
        present = [jnp.where(wa > 0, 1.0, 0.0).astype(F32), jnp.where(wa < s.wa - 1, 1.0, 0.0).astype(F32)]

    @pl.when(lax.axis_index("ta") > 0)
    def _():
        copies = []
        width = s.cols - EDGE * s.ncol
        safe = EDGE if s.ncol > 1 else pl.multiple_of(jnp.where(wa == 0, 0, EDGE), EDGE)
        for f in range(PREV):
            place = (f, pl.ds(1, s.rows - s.tail - 2), pl.ds(safe, width))
            copies.append(pltpu.make_async_copy(pre.at[place], enc.at[place], sem.at[f, 4]))
        start(copies)
        lhs = []
        start_row = s.rows - s.tail - 1
        end = PREV - 1

        def tap(p, dx, i):
            return more[dx, i - start_row] if p == end and i >= start_row else taps[p, dx, i]

        def shifted(act):
            west = jnp.where(at == 0, 0.0, pltpu.roll(act, 1, 0))
            east = jnp.where(at == s.cols - 1, 0.0, pltpu.roll(act, s.cols - 1, 0))
            return [x.astype(BF16) for x in (west, act, east)]

        for dx in range(3):
            more[dx, :2] = taps[end, dx, start_row : start_row + 2]
        for i in range(s.tail):
            o = PREV * s.strip + i * s.cols
            raw = got[o : o + s.cols].astype(F32)
            act = activation(raw, moved[end : end + 1], moved[PREV + end : PREV + end + 1], shift)
            for dx, x in enumerate(shifted(act)):
                more[dx, 2 + i] = x
        for p in range(PREV):
            mean, scale = moved[p : p + 1], moved[PREV + p : PREV + p + 1]
            o = p * s.strip
            acts = []
            for k in range(2):
                raw = got[o + k * s.cols : o + (k + 1) * s.cols].astype(F32)
                act = activation(raw, mean, scale, shift) * inside[k]
                acts.append(act)
            top, bottom = shifted(acts[0]), shifted(acts[1])
            lhs.append(
                jnp.concatenate(top + [tap(p, dx, i) for i in (1, 2) for dx in range(3)], axis=1)
            )
            n = s.rows
            lhs.append(
                jnp.concatenate([tap(p, dx, i) for i in (n - 1, n) for dx in range(3)] + bottom, axis=1)
            )
            for k in range(s.ncol):
                o2 = o + 2 * s.cols + k * s.colrow
                cell = activation(got[o2 : o2 + s.colrow].astype(F32), mean, scale, shift) * present[k]
                upper = cell[n : n + 1] * inside[0]
                lower = cell[n + 1 : n + 2] * inside[1]
                right = sides[k]

                def column(d):
                    known = n if p < end else start_row
                    x = cut[p, 2 * k + d]
                    if known == n:
                        return x
                    rows = [jnp.zeros((known, s.chans), F32)]
                    for i in range(known + 1, n + 1):
                        tile = tap(p, 1, i).astype(F32)
                        far = tile[s.cols - 1 - d : s.cols - d]
                        rows.append(jnp.where(right, far, tile[d : d + 1]))
                    rows.append(jnp.zeros((s.colrow - n, s.chans), F32))
                    return x + jnp.concatenate(rows, axis=0)

                here, inner = column(0), column(1)
                far = jnp.where(down < n, cell, 0.0)
                ends = [
                    tuple(jnp.where(right, a[s.cols - 1 :], a[:1]) for a in acts),
                    tuple(jnp.where(right, a[s.cols - 2 : s.cols - 1], a[1:2]) for a in acts),
                    (upper, lower),
                ]
                steps = []
                for dy in range(3):
                    group = []
                    for x, (first, final) in zip((here, inner, far), ends):
                        if dy == 0:
                            x = jnp.where(down == 0, first, pltpu.roll(x, 1, 0))
                        elif dy == 2:
                            x = jnp.where(down == n - 1, final, pltpu.roll(x, s.colrow - 1, 0))
                        group.append(x)
                    mid, inn, out_ = group
                    steps += [jnp.where(right, inn, out_), mid, jnp.where(right, out_, inn)]
                lhs.append(jnp.concatenate([x.astype(BF16) for x in steps], axis=1))
        fresh = s.tail * s.cols
        lhs.append(
            jnp.concatenate(
                [
                    more[dx, dy : dy + s.tail].reshape(fresh, s.chans)
                    for dy in range(3)
                    for dx in range(3)
                ],
                axis=1,
            )
        )
        border = jnp.dot(jnp.concatenate(lhs, axis=0), sw[...], preferred_element_type=F32) + sb[...]
        size = 2 * s.cols + s.ncol * s.colrow
        tile = 16
        cells = lax.broadcasted_iota(jnp.int32, (tile, s.chans), 0)
        masks = [cells == jnp.where(right, tile - 1, 0) for right in sides]
        starts = [jnp.where(right, s.cols - tile, 0) for right in sides]
        first, body = s.cols, (s.tail + 1) * s.cols
        for p in range(PREV):
            o = p * size
            grid[p, :first] = border[o : o + first].astype(BF16)
            if p < end:
                rest = spatial[p, start_row * s.cols : (s.rows - 1) * s.cols]
            else:
                rest = border[PREV * size : PREV * size + fresh].astype(BF16)
            grid[p, first : body] = rest
            grid[p, body : body + s.cols] = border[o + s.cols : o + 2 * s.cols].astype(BF16)
            for k in range(s.ncol):
                o2 = o + 2 * s.cols + k * s.colrow
                for g in range(s.tail + 2):
                    h = 0 if g == 0 else start_row + g - 1
                    at0 = pl.ds(pl.multiple_of(g * s.cols + starts[k], tile), tile)
                    row = jnp.where(masks[k], border[o2 + h : o2 + h + 1], grid[p, at0].astype(F32))
                    grid[p, at0] = row.astype(BF16)
                o3 = body + s.cols + k * s.colrow
                grid[p, o3 : o3 + s.colrow] = border[o2 : o2 + s.colrow].astype(BF16)
        for f in range(PREV):
            own = [base[f, :first], base[f, start_row * s.cols :]] + [rim[f, k] for k in range(s.ncol)]
            y = taps_back(s, [grid[q] for q in range(PREV)], f, tw) + jnp.concatenate(own, axis=0)
            out[f, 0] = y[:first].astype(BF16)
            out[f, start_row:] = y[first : body + s.cols].astype(BF16).reshape(-1, s.cols, s.chans)
            rows = pl.ds(start_row, s.tail + 1)
            copies += [
                pltpu.make_async_copy(out.at[f, 0], enc.at[f, 0], sem.at[f, 0]),
                pltpu.make_async_copy(out.at[f, rows], enc.at[f, rows], sem.at[f, 1]),
            ]
            start(copies[-2:])
            for k in range(s.ncol):
                o3 = body + s.cols + k * s.colrow
                at0 = pl.ds(pl.multiple_of(starts[k], tile), tile)
                for h in range(1, start_row):
                    row = jnp.where(masks[k], y[o3 + h : o3 + h + 1], pre[f, h, at0].astype(F32))
                    out[f, h, at0] = row.astype(BF16)
                edge = pl.multiple_of(jnp.where(sides[k], s.cols - EDGE, 0), EDGE)
                place = (f, pl.ds(1, start_row - 1), pl.ds(edge, EDGE))
                copies.append(pltpu.make_async_copy(out.at[place], enc.at[place], sem.at[f, 2 + k]))
                copies[-1].start()
        wait(copies)


def mates(n, phase):
    if phase == 0:
        return [(i, i ^ 1) for i in range(n)]
    return [(i, (i - 1) % n if i % 2 == 0 else (i + 1) % n) for i in range(n)]


def local(video, norm_gain, norm_bias, spatial_weight, spatial_bias, temporal_weight, temporal_bias):
    nta, nha, nwa = (lax.axis_size(a) for a in ("ta", "ha", "wa"))
    s = Sizes(video, nha, nwa)
    c = s.chans
    sd = jax.ShapeDtypeStruct
    ring = [(i, (i + 1) % nta) for i in range(nta)]
    if nwa == 2:
        sides = [[(0, 1), (1, 0)]]
    else:
        sides = [[(i, (i + d) % nwa) for i in range(nwa)] for d in (1, -1)]
    sw = spatial_weight.reshape(9 * c, c)
    tw = temporal_weight.reshape(3 * c, c)
    gain, nbias, sb, tb = (v.reshape(1, c) for v in (norm_gain, norm_bias, spatial_bias, temporal_bias))

    one = video.shape[1:]
    late_shape = sd((s.late,) + one[1:], BF16)
    early, late = call(
        functools.partial(head_kernel, s),
        [sd((s.early,) + one[1:], BF16), late_shape],
        name="head",
        in_specs=[VMEM],
    )(video)
    rowpay = sd((s.frames * s.cols + s.stats, c), BF16)
    stat = sd((2 * s.frames, c), F32)
    colout = [sd((s.frames * s.colrow, c), BF16)] * s.ncol
    riding = s.stats if s.fused else 0
    pay, stats, *cols = call(
        functools.partial(local_kernel, s),
        [rowpay, stat] + colout,
        name="local",
        in_specs=[VMEM, ANY],
    )(video, early)
    early = lax.ppermute(early, "ta", ring)
    got1 = lax.ppermute(pay, "ha", mates(nha, 0))
    late, payy, part, *pays = call(
        functools.partial(pair_kernel, s),
        [late_shape, rowpay, stat]
        + [sd((s.frames * s.colrow + riding, c), BF16)] * s.ncol
        + [sd((s.corner + riding, c), BF16)] * s.ncol,
        out_specs=[ANY] + [VMEM] * (2 + 2 * s.ncol),
        name="pair",
        in_specs=[VMEM] * (3 + s.ncol) + [ANY],
        input_output_aliases={3 + s.ncol: 0},
    )(video, stats, got1, *cols, late)
    outer = mates(nha, 1)
    diagonal = [[(h * nwa + w, g * nwa + v) for h, g in outer for w, v in p] for p in sides]
    goty = lax.ppermute(payy, "ha", outer)
    gotx = [lax.ppermute(x, "wa", p) for x, p in zip(pays[: s.ncol], sides)]
    gotd = [lax.ppermute(x, ("ha", "wa"), p) for x, p in zip(pays[s.ncol :], diagonal)]
    late = lax.ppermute(late, "ta", ring[:-1])
    if not s.fused:
        every = lax.all_gather(stats, ("ha", "wa"))
        part = merge(float(s.rows * s.cols), [every[i] for i in range(nha * nwa)])
    aff, moved = call(
        functools.partial(group_kernel, s),
        [stat, sd((2 * PREV, c), F32)],
        name="group",
        in_specs=[VMEM] * (3 + 2 * s.ncol),
    )(part, gain, goty, *gotx, *gotd)
    moved = lax.ppermute(moved, "ta", ring)
    hand, halo, *cols = call(
        functools.partial(edge_kernel, s),
        [sd((PREV * s.strip + s.tail * s.cols, c), BF16), sd((s.frames, 2, s.cols, c), BF16)] + colout,
        name="edge",
        in_specs=[VMEM] * (4 + 2 * s.ncol),
    )(aff, video, got1, goty, *gotx, *gotd)
    got = lax.ppermute(hand, "ta", ring)
    frame = (s.rows * s.cols, c)
    taps = (3, s.rows + 2, s.cols, c)
    enc, base = call(
        functools.partial(own_kernel, s),
        [sd(video.shape, BF16), sd((PREV,) + frame, F32)],
        out_specs=[ANY, VMEM],
        scratch=[
            pltpu.VMEM(taps, BF16),
            pltpu.VMEM((s.frames,) + frame, BF16),
            pltpu.VMEM((s.frames,) + one, BF16),
            pltpu.SemaphoreType.DMA((s.frames, QUARTERS)),
        ],
        flops=2 * s.rows * s.cols * c * c * (9 * s.frames + 3 * (s.frames - PREV)),
        name="own",
        in_specs=[VMEM] * (8 + s.ncol) + [ANY],
    )(video, halo, aff, nbias, sw, sb, tw, tb, *cols, early)
    grid, inner, pre, rim, cut = call(
        functools.partial(inner_kernel, s),
        [
            sd((PREV,) + taps, BF16),
            sd((PREV,) + frame, BF16),
            sd((PREV,) + one, BF16),
            sd((PREV, s.ncol, s.colrow, c), F32),
            sd((PREV, 2 * s.ncol, s.colrow, c), F32),
        ],
        name="inner",
        in_specs=[VMEM] * 8,
    )(early, late, moved, nbias, sw, sb, tw, base)
    (enc,) = call(
        functools.partial(outer_kernel, s),
        [sd(video.shape, BF16)],
        out_specs=[ANY],
        scratch=[
            pltpu.VMEM((3, s.tail + 2) + one[1:], BF16),
            pltpu.VMEM((PREV, (s.tail + 2) * s.cols + s.ncol * s.colrow, c), BF16),
            pltpu.VMEM((PREV,) + one, BF16),
            pltpu.SemaphoreType.DMA((PREV, 5)),
        ],
        name="outer",
        in_specs=[VMEM] * 12 + [ANY],
        input_output_aliases={12: 0},
    )(got, moved, grid, inner, nbias, sw, sb, tw, base, pre, rim, cut, enc)
    return enc


def solution(mesh):
    placed = (P("ta", "ha", "wa", None), P(), P(), P(), P(), P(), P())
    return jax.shard_map(
        local, mesh=mesh, in_specs=placed, out_specs=P("ta", "ha", "wa", None), check_vma=False
    )
```

```python
import functools

import jax
import jax.numpy as jnp
from jax import lax
from jax.experimental import pallas as pl
from jax.experimental.pallas import tpu as pltpu
from jax.sharding import PartitionSpec as P

G = 32
EPS = 1e-06
QUARTERS = 4
EDGE = 8
DOTS = 6
PREV = 2
F32 = jnp.float32
BF16 = jnp.bfloat16
VMEM = pl.BlockSpec(memory_space=pltpu.VMEM)
ANY = pl.BlockSpec(memory_space=pl.ANY)


def call(kernel, outs, out_specs=None, scratch=(), flops=1024, name=None, **kw):
    return pl.pallas_call(
        kernel,
        out_shape=outs,
        out_specs=out_specs or [VMEM] * len(outs),
        scratch_shapes=list(scratch),
        compiler_params=pltpu.CompilerParams(vmem_limit_bytes=24 << 20),
        cost_estimate=pl.CostEstimate(flops=flops, bytes_accessed=1024, transcendentals=0),
        name=name,
        **kw,
    )


def pad_to(n, k):
    return (n + k - 1) // k * k


def split3(x):
    hi = x.astype(BF16)
    rest = x - hi.astype(F32)
    mid = rest.astype(BF16)
    low = (rest - mid.astype(F32)).astype(BF16)
    return hi, mid, low


def as_terms(x, rows):
    parts = jnp.concatenate([t.astype(F32) for t in split3(x)], axis=0)
    fill = rows - parts.shape[0]
    if fill:
        parts = jnp.concatenate([parts, jnp.zeros((fill, x.shape[1]), F32)], axis=0)
    return parts.astype(BF16)


def from_terms(t, rows):
    t = t.astype(F32)
    return t[:rows] + t[rows : 2 * rows] + t[2 * rows : 3 * rows]


class Sizes:
    def __init__(self, video, ha, wa):
        self.frames, self.rows, self.cols, self.chans = video.shape
        self.ha, self.wa = ha, wa
        self.ncol = 1 if wa == 2 else 2
        self.fused = ha == 4 and wa == 2
        self.colrow = pad_to(self.rows + 2, 16)
        self.strip = 2 * self.cols + self.ncol * self.colrow
        self.stats = pad_to(3 * 2 * self.frames, 16)
        self.early = (PREV - 1) * self.rows + self.rows // 12
        self.tail = self.rows // 4 + 1
        self.late = PREV * self.rows - self.early - self.tail
        self.corner = pad_to(self.frames, 16)


def head_kernel(s, video, early, late):
    flat = (PREV * s.rows, s.cols, s.chans)
    sent = video[s.frames - PREV :].reshape(flat)
    early[...] = sent[: s.early]
    late[...] = sent[s.early : s.early + s.late]


def local_kernel(s, video, early, pay, stats, *cols):
    ha, wa = lax.axis_index("ha"), lax.axis_index("wa")
    even = lax.rem(ha, 2) == 0
    means, squares = [], []
    for f in range(s.frames):
        total = jnp.zeros((s.cols, s.chans), F32)
        for r in range(s.rows):
            total = total + video[f, r].astype(F32)
        mean = jnp.sum(total, axis=0, keepdims=True) * (1.0 / (s.rows * s.cols))
        spread = jnp.zeros((s.cols, s.chans), F32)
        left, right = [], []
        for r in range(s.rows):
            x = video[f, r].astype(F32)
            left.append(x[:1])
            right.append(x[s.cols - 1 :])
            x = x - mean
            spread = spread + x * x
        means.append(mean)
        squares.append(jnp.sum(spread, axis=0, keepdims=True))
        fill = [jnp.zeros((s.colrow - s.rows, s.chans), F32)]
        left = jnp.concatenate(left + fill, axis=0)
        right = jnp.concatenate(right + fill, axis=0)
        if s.ncol == 1:
            edges = [jnp.where(wa == 0, right, left)]
        else:
            edges = [right, left]
        for ref, e in zip(cols, edges):
            ref[f * s.colrow : (f + 1) * s.colrow] = e.astype(BF16)
        top = video[f, 0].astype(F32)
        bottom = video[f, s.rows - 1].astype(F32)
        pay[f * s.cols : (f + 1) * s.cols] = jnp.where(even, bottom, top).astype(BF16)
    stat = jnp.concatenate(means + squares, axis=0)
    stats[...] = stat
    o = s.frames * s.cols
    pay[o : o + s.stats] = as_terms(stat, s.stats)


def merge(n, parts):
    half = parts[0].shape[0] // 2
    mean = sum(p[:half] for p in parts) * (1.0 / len(parts))
    square = sum(p[half:] + n * (p[:half] - mean) * (p[:half] - mean) for p in parts)
    return jnp.concatenate([mean, square], axis=0)


def pair_kernel(s, video, stats, got, *refs):
    cols, refs = refs[: s.ncol], refs[s.ncol + 1 :]
    _, payy, part = refs[:3]
    payx, payd = refs[3 : 3 + s.ncol], refs[3 + s.ncol :]
    ha, wa = lax.axis_index("ha"), lax.axis_index("wa")
    even = lax.rem(ha, 2) == 0
    o = s.frames * s.cols
    stat = merge(float(s.rows * s.cols), [stats[...], from_terms(got[o : o + s.stats], 2 * s.frames)])
    part[...] = stat
    terms = as_terms(stat, s.stats)
    at = lax.broadcasted_iota(jnp.int32, (s.colrow, s.chans), 0)
    cells = [[] for _ in range(s.ncol)]
    for f in range(s.frames):
        top = video[f, 0].astype(F32)
        bottom = video[f, s.rows - 1].astype(F32)
        outer = jnp.where(even, top, bottom)
        payy[f * s.cols : (f + 1) * s.cols] = outer.astype(BF16)
        inner = got[f * s.cols : (f + 1) * s.cols].astype(F32)
        for k in range(s.ncol):
            right = wa == 0 if s.ncol == 1 else k == 0
            cell = jnp.where(right, inner[s.cols - 1 :], inner[:1])
            cells[k].append(jnp.where(right, outer[s.cols - 1 :], outer[:1]))
            edge = cols[k][f * s.colrow : (f + 1) * s.colrow].astype(F32)
            edge = jnp.where(at >= s.rows, cell, edge)
            payx[k][f * s.colrow : (f + 1) * s.colrow] = edge.astype(BF16)
    for k in range(s.ncol):
        fill = s.corner - s.frames
        rows = cells[k] + ([jnp.zeros((fill, s.chans), F32)] if fill else [])
        payd[k][: s.corner] = jnp.concatenate(rows, axis=0).astype(BF16)
    payy[o : o + s.stats] = terms
    if s.fused:
        o = s.frames * s.colrow
        payx[0][o : o + s.stats] = terms
        payd[0][s.corner : s.corner + s.stats] = terms


def group_kernel(s, part, gain, goty, *refs):
    gotx, gotd = refs[: s.ncol], refs[s.ncol : 2 * s.ncol]
    aff, moved = refs[2 * s.ncol :]
    rows = 2 * s.frames
    count = float(s.rows * s.cols * s.ha * s.wa)
    stat = part[...]
    if s.fused:
        offsets = ((goty, s.frames * s.cols), (gotx[0], s.frames * s.colrow), (gotd[0], s.corner))
        stat = merge(count / 4, [stat] + [from_terms(ref[o : o + s.stats], rows) for ref, o in offsets])
    width = s.chans // G
    a = lax.broadcasted_iota(jnp.int32, (s.chans, s.chans), 0) // width
    b = lax.broadcasted_iota(jnp.int32, (s.chans, s.chans), 1) // width
    group = jnp.where(a == b, 1.0, 0.0).astype(BF16)

    def tot(x):
        terms = jnp.concatenate(split3(x), axis=0)
        y = jnp.dot(terms, group, preferred_element_type=F32)
        n = s.frames
        return y[:n] + y[n : 2 * n] + y[2 * n :]

    m, q = stat[: s.frames], stat[s.frames :]
    mean = tot(m) * (1.0 / width)
    var = tot(q + count * (m - mean) * (m - mean)) * (1.0 / (count * width))
    scale = lax.rsqrt(var + EPS) * gain[...] * 0.5
    aff[: s.frames] = mean
    aff[s.frames :] = scale
    first = s.frames - PREV
    moved[:PREV] = mean[first:]
    moved[PREV:] = scale[first:]


def edge_kernel(s, aff, video, got, goty, *refs):
    gotx, gotd = refs[: s.ncol], refs[s.ncol : 2 * s.ncol]
    hand, halo, *cols = refs[2 * s.ncol :]
    even = lax.rem(lax.axis_index("ha"), 2) == 0
    first = s.frames - PREV
    o = PREV * s.strip
    rest = video[s.frames - 1, s.rows - s.tail :]
    hand[o : o + s.tail * s.cols] = rest.reshape(s.tail * s.cols, s.chans)
    at = lax.broadcasted_iota(jnp.int32, (s.colrow, s.chans), 0)
    for f in range(s.frames):
        p = (f - first) * s.strip
        one = got[f * s.cols : (f + 1) * s.cols].astype(F32)
        two = goty[f * s.cols : (f + 1) * s.cols].astype(F32)
        top = jnp.where(even, two, one).astype(BF16)
        bottom = jnp.where(even, one, two).astype(BF16)
        halo[f, 0] = top
        halo[f, 1] = bottom
        if f >= first:
            hand[p : p + s.cols] = top
            hand[p + s.cols : p + 2 * s.cols] = bottom
        for k in range(s.ncol):
            cell = gotd[k][: s.corner].astype(F32)[f : f + 1]
            edge = gotx[k][f * s.colrow : (f + 1) * s.colrow].astype(F32)
            outer = jnp.where(even, s.rows, s.rows + 1)
            edge = jnp.where(at == outer, cell, edge).astype(BF16)
            cols[k][f * s.colrow : (f + 1) * s.colrow] = edge
            if f >= first:
                o = p + 2 * s.cols + k * s.colrow
                hand[o : o + s.colrow] = edge


def activation(x, mean, scale, shift):
    h = (x - mean) * scale + shift
    return h + h * jnp.tanh(h)


def fill_taps(s, taps, raw_row, edges, mean, scale, shift):
    ha, wa = lax.axis_index("ha"), lax.axis_index("wa")
    top_in = jnp.where(ha > 0, 1.0, 0.0).astype(F32)
    bottom_in = jnp.where(ha < s.ha - 1, 1.0, 0.0).astype(F32)
    left_in = jnp.where(wa > 0, 1.0, 0.0).astype(F32)
    right_in = jnp.where(wa < s.wa - 1, 1.0, 0.0).astype(F32)
    if edges is not None:
        acts = [activation(e.astype(F32), mean, scale, shift) for e in edges]
        left, right = acts[0] * left_in, acts[-1] * right_in
    at = lax.broadcasted_iota(jnp.int32, (s.cols, s.chans), 0)
    for i in range(s.rows + 2):
        raw = raw_row(i)
        if raw is None:
            for dx in range(3):
                taps[dx, i] = jnp.zeros((s.cols, s.chans), BF16)
            continue
        act = activation(raw.astype(F32), mean, scale, shift)
        j = s.rows if i == 0 else s.rows + 1 if i == s.rows + 1 else i - 1
        lcell, rcell = (0.0, 0.0) if edges is None else (left[j : j + 1], right[j : j + 1])
        west = jnp.where(at == 0, lcell, pltpu.roll(act, 1, 0))
        east = jnp.where(at == s.cols - 1, rcell, pltpu.roll(act, s.cols - 1, 0))
        if i in (0, s.rows + 1):
            inside = top_in if i == 0 else bottom_in
            west, act, east = west * inside, act * inside, east * inside
        taps[0, i] = west.astype(BF16)
        taps[1, i] = act.astype(BF16)
        taps[2, i] = east.astype(BF16)


def spatial_dot(s, taps, weight, bias, rows):
    size = s.rows // DOTS
    done = []
    for r in range(0, rows, size):
        step = min(size, rows - r)
        lhs = jnp.concatenate(
            [
                taps[dx, r + dy : r + dy + step].reshape(step * s.cols, s.chans)
                for dy in range(3)
                for dx in range(3)
            ],
            axis=1,
        )
        done.append((jnp.dot(lhs, weight[...], preferred_element_type=F32) + bias[...]).astype(BF16))
    return jnp.concatenate(done, axis=0)


def temporal_dot(s, frames, weight, bias):
    lhs = jnp.concatenate(frames, axis=1)
    out = jnp.dot(lhs, weight[...], preferred_element_type=F32) + bias[...]
    return out.astype(BF16).reshape(s.rows, s.cols, s.chans)


def put(s, ref, enc, sem, f, quarters=range(QUARTERS)):
    step = s.rows // QUARTERS
    return [
        pltpu.make_async_copy(
            ref.at[f, pl.ds(k * step, step)], enc.at[f, pl.ds(k * step, step)], sem.at[f, k]
        )
        for k in quarters
    ]


def start(copies):
    for c in copies:
        c.start()


def wait(copies):
    for c in copies:
        c.wait()


def own_kernel(s, video, halo, aff, nbias, sw, sb, tw, tb, *refs):
    cols = refs[: s.ncol]
    enc, base, taps, spatial, out, sem = refs[s.ncol + 1 :]
    shift = nbias[...] * 0.5
    first = lax.axis_index("ta") == 0

    def frame(f):
        def raw_row(i):
            if i == 0:
                return halo[f, 0]
            if i == s.rows + 1:
                return halo[f, 1]
            return video[f, i - 1]

        edges = [c[pl.ds(f * s.colrow, s.colrow)] for c in cols]
        fill_taps(s, taps.at[f % 2], raw_row, edges, aff[pl.ds(f, 1)], aff[pl.ds(s.frames + f, 1)], shift)
        spatial[f] = spatial_dot(s, taps.at[f % 2], sw, sb, s.rows)

    for f in range(s.frames):
        frame(f)

    def encode(f):
        out[f] = temporal_dot(s, [spatial[max(f - k, 0)] for k in range(3)], tw, tb)
        start(put(s, out, enc, sem, f))

    for f in range(PREV, s.frames):
        encode(f)

    @pl.when(first)
    def _():
        for f in range(PREV):
            encode(f)
        for f in range(PREV):
            wait(put(s, out, enc, sem, f))

    @pl.when(jnp.logical_not(first))
    def _():
        for f in range(PREV):
            lhs = jnp.concatenate([spatial[f - k] for k in range(f + 1)], axis=1)
            weight = tw[: (f + 1) * s.chans]
            base[f] = jnp.dot(lhs, weight, preferred_element_type=F32) + tb[...]

    for f in range(PREV, s.frames):
        wait(put(s, out, enc, sem, f))


def taps_back(s, grids, f, tw):
    lhs = jnp.concatenate([grids[q] for q in range(PREV - 1, f - 1, -1)], axis=1)
    return jnp.dot(lhs, tw[(f + 1) * s.chans :], preferred_element_type=F32)


def inner_kernel(s, early, late, moved, nbias, sw, sb, tw, base, taps, spatial, pre, rim, cut):
    shift = nbias[...] * 0.5

    @pl.when(lax.axis_index("ta") > 0)
    def _():
        for p in range(PREV):

            def raw_row(i):
                if i == 0 or i == s.rows + 1:
                    return None
                r = p * s.rows + i - 1
                if r >= s.early + s.late:
                    return None
                return early[r] if r < s.early else late[r - s.early]

            fill_taps(s, taps.at[p], raw_row, None, moved[p : p + 1], moved[PREV + p : PREV + p + 1], shift)
            rows = s.rows if p < PREV - 1 else s.rows - s.tail - 1
            for k in range(s.ncol):
                right = lax.axis_index("wa") == 0 if s.ncol == 1 else k == 1
                for d in range(2):
                    cells = []
                    for i in range(1, rows + 1):
                        tile = taps[p, 1, i].astype(F32)
                        far = tile[s.cols - 1 - d : s.cols - d]
                        cells.append(jnp.where(right, far, tile[d : d + 1]))
                    cells.append(jnp.zeros((s.colrow - rows, s.chans), F32))
                    cut[p, 2 * k + d] = jnp.concatenate(cells, axis=0)
            spatial[p, : rows * s.cols] = spatial_dot(s, taps.at[p], sw, sb, rows)
        part = slice(s.cols, (s.rows - s.tail - 1) * s.cols)
        for f in range(PREV):
            y = taps_back(s, [spatial[q, part] for q in range(PREV)], f, tw) + base[f, part]
            pre[f, 1 : s.rows - s.tail - 1] = y.astype(BF16).reshape(-1, s.cols, s.chans)
            for k in range(s.ncol):
                right = lax.axis_index("wa") == 0 if s.ncol == 1 else k == 1
                cells = []
                for h in range(s.rows):
                    o = h * s.cols
                    last = base[f, o + s.cols - 8 : o + s.cols]
                    cells.append(jnp.where(right, last[7:], base[f, o : o + 8][:1]))
                cells.append(jnp.zeros((s.colrow - s.rows, s.chans), F32))
                rim[f, k] = jnp.concatenate(cells, axis=0)


def outer_kernel(s, got, moved, taps, spatial, nbias, sw, sb, tw, base, pre, rim, cut, _, enc, more, grid, out, sem):
    ha, wa = lax.axis_index("ha"), lax.axis_index("wa")
    shift = nbias[...] * 0.5
    inside = [jnp.where(ha > 0, 1.0, 0.0).astype(F32), jnp.where(ha < s.ha - 1, 1.0, 0.0).astype(F32)]
    at = lax.broadcasted_iota(jnp.int32, (s.cols, s.chans), 0)
    down = lax.broadcasted_iota(jnp.int32, (s.colrow, s.chans), 0)
    if s.ncol == 1:
        sides = [wa == 0]
        present = [jnp.ones((), F32)]
    else:
        sides = [False, True]
        present = [jnp.where(wa > 0, 1.0, 0.0).astype(F32), jnp.where(wa < s.wa - 1, 1.0, 0.0).astype(F32)]

    @pl.when(lax.axis_index("ta") > 0)
    def _():
        copies = []
        width = s.cols - EDGE * s.ncol
        safe = EDGE if s.ncol > 1 else pl.multiple_of(jnp.where(wa == 0, 0, EDGE), EDGE)
        for f in range(PREV):
            place = (f, pl.ds(1, s.rows - s.tail - 2), pl.ds(safe, width))
            copies.append(pltpu.make_async_copy(pre.at[place], enc.at[place], sem.at[f, 4]))
        start(copies)
        lhs = []
        start_row = s.rows - s.tail - 1
        end = PREV - 1

        def tap(p, dx, i):
            return more[dx, i - start_row] if p == end and i >= start_row else taps[p, dx, i]

        def shifted(act):
            west = jnp.where(at == 0, 0.0, pltpu.roll(act, 1, 0))
            east = jnp.where(at == s.cols - 1, 0.0, pltpu.roll(act, s.cols - 1, 0))
            return [x.astype(BF16) for x in (west, act, east)]

        for dx in range(3):
            more[dx, :2] = taps[end, dx, start_row : start_row + 2]
        for i in range(s.tail):
            o = PREV * s.strip + i * s.cols
            raw = got[o : o + s.cols].astype(F32)
            act = activation(raw, moved[end : end + 1], moved[PREV + end : PREV + end + 1], shift)
            for dx, x in enumerate(shifted(act)):
                more[dx, 2 + i] = x
        for p in range(PREV):
            mean, scale = moved[p : p + 1], moved[PREV + p : PREV + p + 1]
            o = p * s.strip
            acts = []
            for k in range(2):
                raw = got[o + k * s.cols : o + (k + 1) * s.cols].astype(F32)
                act = activation(raw, mean, scale, shift) * inside[k]
                acts.append(act)
            top, bottom = shifted(acts[0]), shifted(acts[1])
            lhs.append(
                jnp.concatenate(top + [tap(p, dx, i) for i in (1, 2) for dx in range(3)], axis=1)
            )
            n = s.rows
            lhs.append(
                jnp.concatenate([tap(p, dx, i) for i in (n - 1, n) for dx in range(3)] + bottom, axis=1)
            )
            for k in range(s.ncol):
                o2 = o + 2 * s.cols + k * s.colrow
                cell = activation(got[o2 : o2 + s.colrow].astype(F32), mean, scale, shift) * present[k]
                upper = cell[n : n + 1] * inside[0]
                lower = cell[n + 1 : n + 2] * inside[1]
                right = sides[k]

                def column(d):
                    known = n if p < end else start_row
                    x = cut[p, 2 * k + d]
                    if known == n:
                        return x
                    rows = [jnp.zeros((known, s.chans), F32)]
                    for i in range(known + 1, n + 1):
                        tile = tap(p, 1, i).astype(F32)
                        far = tile[s.cols - 1 - d : s.cols - d]
                        rows.append(jnp.where(right, far, tile[d : d + 1]))
                    rows.append(jnp.zeros((s.colrow - n, s.chans), F32))
                    return x + jnp.concatenate(rows, axis=0)

                here, inner = column(0), column(1)
                far = jnp.where(down < n, cell, 0.0)
                ends = [
                    tuple(jnp.where(right, a[s.cols - 1 :], a[:1]) for a in acts),
                    tuple(jnp.where(right, a[s.cols - 2 : s.cols - 1], a[1:2]) for a in acts),
                    (upper, lower),
                ]
                steps = []
                for dy in range(3):
                    group = []
                    for x, (first, final) in zip((here, inner, far), ends):
                        if dy == 0:
                            x = jnp.where(down == 0, first, pltpu.roll(x, 1, 0))
                        elif dy == 2:
                            x = jnp.where(down == n - 1, final, pltpu.roll(x, s.colrow - 1, 0))
                        group.append(x)
                    mid, inn, out_ = group
                    steps += [jnp.where(right, inn, out_), mid, jnp.where(right, out_, inn)]
                lhs.append(jnp.concatenate([x.astype(BF16) for x in steps], axis=1))
        fresh = s.tail * s.cols
        lhs.append(
            jnp.concatenate(
                [
                    more[dx, dy : dy + s.tail].reshape(fresh, s.chans)
                    for dy in range(3)
                    for dx in range(3)
                ],
                axis=1,
            )
        )
        border = jnp.dot(jnp.concatenate(lhs, axis=0), sw[...], preferred_element_type=F32) + sb[...]
        size = 2 * s.cols + s.ncol * s.colrow
        tile = 16
        cells = lax.broadcasted_iota(jnp.int32, (tile, s.chans), 0)
        masks = [cells == jnp.where(right, tile - 1, 0) for right in sides]
        starts = [jnp.where(right, s.cols - tile, 0) for right in sides]
        first, body = s.cols, (s.tail + 1) * s.cols
        for p in range(PREV):
            o = p * size
            grid[p, :first] = border[o : o + first].astype(BF16)
            if p < end:
                rest = spatial[p, start_row * s.cols : (s.rows - 1) * s.cols]
            else:
                rest = border[PREV * size : PREV * size + fresh].astype(BF16)
            grid[p, first : body] = rest
            grid[p, body : body + s.cols] = border[o + s.cols : o + 2 * s.cols].astype(BF16)
            for k in range(s.ncol):
                o2 = o + 2 * s.cols + k * s.colrow
                for g in range(s.tail + 2):
                    h = 0 if g == 0 else start_row + g - 1
                    at0 = pl.ds(pl.multiple_of(g * s.cols + starts[k], tile), tile)
                    row = jnp.where(masks[k], border[o2 + h : o2 + h + 1], grid[p, at0].astype(F32))
                    grid[p, at0] = row.astype(BF16)
                o3 = body + s.cols + k * s.colrow
                grid[p, o3 : o3 + s.colrow] = border[o2 : o2 + s.colrow].astype(BF16)
        for f in range(PREV):
            own = [base[f, :first], base[f, start_row * s.cols :]] + [rim[f, k] for k in range(s.ncol)]
            y = taps_back(s, [grid[q] for q in range(PREV)], f, tw) + jnp.concatenate(own, axis=0)
            out[f, 0] = y[:first].astype(BF16)
            out[f, start_row:] = y[first : body + s.cols].astype(BF16).reshape(-1, s.cols, s.chans)
            rows = pl.ds(start_row, s.tail + 1)
            copies += [
                pltpu.make_async_copy(out.at[f, 0], enc.at[f, 0], sem.at[f, 0]),
                pltpu.make_async_copy(out.at[f, rows], enc.at[f, rows], sem.at[f, 1]),
            ]
            start(copies[-2:])
            for k in range(s.ncol):
                o3 = body + s.cols + k * s.colrow
                at0 = pl.ds(pl.multiple_of(starts[k], tile), tile)
                for h in range(1, start_row):
                    row = jnp.where(masks[k], y[o3 + h : o3 + h + 1], pre[f, h, at0].astype(F32))
                    out[f, h, at0] = row.astype(BF16)
                edge = pl.multiple_of(jnp.where(sides[k], s.cols - EDGE, 0), EDGE)
                place = (f, pl.ds(1, start_row - 1), pl.ds(edge, EDGE))
                copies.append(pltpu.make_async_copy(out.at[place], enc.at[place], sem.at[f, 2 + k]))
                copies[-1].start()
        wait(copies)


def mates(n, phase):
    if phase == 0:
        return [(i, i ^ 1) for i in range(n)]
    return [(i, (i - 1) % n if i % 2 == 0 else (i + 1) % n) for i in range(n)]


def local(video, norm_gain, norm_bias, spatial_weight, spatial_bias, temporal_weight, temporal_bias):
    nta, nha, nwa = (lax.axis_size(a) for a in ("ta", "ha", "wa"))
    s = Sizes(video, nha, nwa)
    c = s.chans
    sd = jax.ShapeDtypeStruct
    ring = [(i, (i + 1) % nta) for i in range(nta)]
    if nwa == 2:
        sides = [[(0, 1), (1, 0)]]
    else:
        sides = [[(i, (i + d) % nwa) for i in range(nwa)] for d in (1, -1)]
    sw = spatial_weight.reshape(9 * c, c)
    tw = temporal_weight.reshape(3 * c, c)
    gain, nbias, sb, tb = (v.reshape(1, c) for v in (norm_gain, norm_bias, spatial_bias, temporal_bias))

    one = video.shape[1:]
    late_shape = sd((s.late,) + one[1:], BF16)
    early, late = call(
        functools.partial(head_kernel, s),
        [sd((s.early,) + one[1:], BF16), late_shape],
        name="head",
        in_specs=[VMEM],
    )(video)
    rowpay = sd((s.frames * s.cols + s.stats, c), BF16)
    stat = sd((2 * s.frames, c), F32)
    colout = [sd((s.frames * s.colrow, c), BF16)] * s.ncol
    riding = s.stats if s.fused else 0
    pay, stats, *cols = call(
        functools.partial(local_kernel, s),
        [rowpay, stat] + colout,
        name="local",
        in_specs=[VMEM, ANY],
    )(video, early)
    early = lax.ppermute(early, "ta", ring)
    got1 = lax.ppermute(pay, "ha", mates(nha, 0))
    late, payy, part, *pays = call(
        functools.partial(pair_kernel, s),
        [late_shape, rowpay, stat]
        + [sd((s.frames * s.colrow + riding, c), BF16)] * s.ncol
        + [sd((s.corner + riding, c), BF16)] * s.ncol,
        out_specs=[ANY] + [VMEM] * (2 + 2 * s.ncol),
        name="pair",
        in_specs=[VMEM] * (3 + s.ncol) + [ANY],
        input_output_aliases={3 + s.ncol: 0},
    )(video, stats, got1, *cols, late)
    outer = mates(nha, 1)
    diagonal = [[(h * nwa + w, g * nwa + v) for h, g in outer for w, v in p] for p in sides]
    goty = lax.ppermute(payy, "ha", outer)
    gotx = [lax.ppermute(x, "wa", p) for x, p in zip(pays[: s.ncol], sides)]
    gotd = [lax.ppermute(x, ("ha", "wa"), p) for x, p in zip(pays[s.ncol :], diagonal)]
    late = lax.ppermute(late, "ta", ring[:-1])
    if not s.fused:
        every = lax.all_gather(stats, ("ha", "wa"))
        part = merge(float(s.rows * s.cols), [every[i] for i in range(nha * nwa)])
    aff, moved = call(
        functools.partial(group_kernel, s),
        [stat, sd((2 * PREV, c), F32)],
        name="group",
        in_specs=[VMEM] * (3 + 2 * s.ncol),
    )(part, gain, goty, *gotx, *gotd)
    moved = lax.ppermute(moved, "ta", ring)
    hand, halo, *cols = call(
        functools.partial(edge_kernel, s),
        [sd((PREV * s.strip + s.tail * s.cols, c), BF16), sd((s.frames, 2, s.cols, c), BF16)] + colout,
        name="edge",
        in_specs=[VMEM] * (4 + 2 * s.ncol),
    )(aff, video, got1, goty, *gotx, *gotd)
    got = lax.ppermute(hand, "ta", ring)
    frame = (s.rows * s.cols, c)
    taps = (3, s.rows + 2, s.cols, c)
    enc, base = call(
        functools.partial(own_kernel, s),
        [sd(video.shape, BF16), sd((PREV,) + frame, F32)],
        out_specs=[ANY, VMEM],
        scratch=[
            pltpu.VMEM((2,) + taps, BF16),
            pltpu.VMEM((s.frames,) + frame, BF16),
            pltpu.VMEM((s.frames,) + one, BF16),
            pltpu.SemaphoreType.DMA((s.frames, QUARTERS)),
        ],
        flops=2 * s.rows * s.cols * c * c * (9 * s.frames + 3 * (s.frames - PREV)),
        name="own",
        in_specs=[VMEM] * (8 + s.ncol) + [ANY],
    )(video, halo, aff, nbias, sw, sb, tw, tb, *cols, early)
    grid, inner, pre, rim, cut = call(
        functools.partial(inner_kernel, s),
        [
            sd((PREV,) + taps, BF16),
            sd((PREV,) + frame, BF16),
            sd((PREV,) + one, BF16),
            sd((PREV, s.ncol, s.colrow, c), F32),
            sd((PREV, 2 * s.ncol, s.colrow, c), F32),
        ],
        name="inner",
        in_specs=[VMEM] * 8,
    )(early, late, moved, nbias, sw, sb, tw, base)
    (enc,) = call(
        functools.partial(outer_kernel, s),
        [sd(video.shape, BF16)],
        out_specs=[ANY],
        scratch=[
            pltpu.VMEM((3, s.tail + 2) + one[1:], BF16),
            pltpu.VMEM((PREV, (s.tail + 2) * s.cols + s.ncol * s.colrow, c), BF16),
            pltpu.VMEM((PREV,) + one, BF16),
            pltpu.SemaphoreType.DMA((PREV, 5)),
        ],
        name="outer",
        in_specs=[VMEM] * 12 + [ANY],
        input_output_aliases={12: 0},
    )(got, moved, grid, inner, nbias, sw, sb, tw, base, pre, rim, cut, enc)
    return enc


def solution(mesh):
    placed = (P("ta", "ha", "wa", None), P(), P(), P(), P(), P(), P())
    return jax.shard_map(
        local, mesh=mesh, in_specs=placed, out_specs=P("ta", "ha", "wa", None), check_vma=False
    )
```
